128 devices in a mesh: seq: 16 (over y, x), ctx: 8 (over z, core).
Axes of the slice: x: 4, y: 4, z: 4, core: 2. Of those that a mesh axis runs over, the one named last changes fastest.
Arguments:
- hidden_in: bfloat16 [16, 1024, 1024], P('seq', 'ctx'), may hold values from -6 to 6
- positions: int32 [16, 1024], P('seq', 'ctx'), may hold values from 0 to 1534, as said below
- starts: int32 [16, 2], P('seq'), may hold values from 0 to 768, as said below
- routes: int32 [16, 1024, 4], P('seq', 'ctx'), may hold values from 0 to 7, all different within a row; in each aligned block of 128 rows (0 to 127, 128 to 255, ..., all dimensions but the last counted through in order) at most 80 rows name the same one
- qkv_weight: bfloat16 [2048, 1024], P(('seq', 'ctx')), may hold values from -0.1875 to 0.1875
- out_weight: bfloat16 [1024, 1024], P(('seq', 'ctx')), may hold values from -1.5 to 1.5
- expert_in: bfloat16 [1024, 8, 1024], P(('seq', 'ctx')), may hold values from -0.1875 to 0.1875
- expert_out: bfloat16 [1024, 8, 512], P(('seq', 'ctx')), may hold values from -1.5 to 1.5
- router: bfloat16 [1024, 8], replicated, may hold values from -0.09375 to 0.09375
- attn_gain: bfloat16 [1024], replicated, may hold values from 0.25 to 1.75
- query_gain: bfloat16 [1024], replicated, may hold values from 0.25 to 1.75
- key_gain: bfloat16 [512], replicated, may hold values from 0.25 to 1.75
- mlp_gain: bfloat16 [1024], replicated, may hold values from 0.25 to 1.75
- out_grad: bfloat16 [16, 1024, 1024], P('seq', 'ctx'), may hold values from -6 to 6
Outputs:
- result: bfloat16 [16, 1024, 1024], P('seq', 'ctx')
- grad_input: float32 [16, 1024, 1024], P('seq', 'ctx')
- grad_qkv: float32 [2048, 1024], P(('seq', 'ctx'))
- grad_out: float32 [1024, 1024], P(('seq', 'ctx'))
- grad_expert_in: float32 [1024, 8, 1024], P(('seq', 'ctx'))
- grad_expert_out: float32 [1024, 8, 512], P(('seq', 'ctx'))
- grad_router: float32 [1024, 8], replicated
- grad_attn_gain: float32 [1024], replicated
- grad_query_gain: float32 [1024], replicated
- grad_key_gain: float32 [512], replicated
- grad_mlp_gain: float32 [1024], replicated
The draws below stay inside these ranges and needn't reach their ends.
Inputs may be any that keep to these rules, and one draw needn't show every extreme that they name: `routes`: each row names 4 different experts; among the 128 tokens of one sequence on one device (aligned blocks), no expert is named by more than 80 of them. Piece k of a sequence starts at a token index from k * 512 to (k + 1) * 512 - 256; pieces never intersect. Within a sequence positions start at 0 and rise by 1 or 2 from token to token; the last token of every sequence has position 1534.
All inputs are finite; a program needn't handle non-finite values.
Results may differ from the reference program's by a relative error of at most 0.018.
Values may be sent and summed in bfloat16 or wider, within the bound.
A program may use at most 256 MiB of HBM per device.

```python
import math
import jax
import jax.numpy as jnp
import numpy as np
from jax import lax

D = 1024
QUERY_HEADS = 16
KEY_VALUE_HEADS = 8
FF = 512
E = 8
TOP = 4
SEQUENCE_LENGTH = 1024
PIECE = 256
NPIC = 2
KVW = 512
QKVW = 2048
TS = 128
MOST = 80
SEQUENCE_COUNT = 16


def draw_positions(key, part):
    count = SEQUENCE_LENGTH - 1
    base_steps = jnp.where(jnp.arange(count, dtype=jnp.int32) < count // 2, 2, 1).astype(jnp.int32)
    seq_keys = jax.random.split(key, SEQUENCE_COUNT)
    shuffled = jax.vmap(lambda one_key: jax.random.permutation(one_key, base_steps))(seq_keys)
    rising = jnp.cumsum(shuffled, axis=1).astype(jnp.int32)
    return jnp.concatenate([jnp.zeros((SEQUENCE_COUNT, 1), jnp.int32), rising], axis=1)


def draw_starts(key, part):
    region = SEQUENCE_LENGTH // NPIC
    offsets = jax.random.randint(key, (SEQUENCE_COUNT, NPIC), 0, region - PIECE + 1, dtype=jnp.int32)
    offsets = offsets.at[0, 0].set(0)
    offsets = offsets.at[0, NPIC - 1].set(region - PIECE)
    return offsets + region * jnp.arange(NPIC, dtype=jnp.int32)[None, :]


def block_levels(rng, shape, pieces, least, largest):
    gain = 1.0
    for axis_at, shards_of in pieces:
        draws = jax.random.uniform(jax.random.fold_in(jax.random.fold_in(rng, 6), axis_at), (shards_of,), jnp.float32, least / len(pieces), largest / len(pieces))
        gain = gain * jnp.repeat(jnp.exp(draws), shape[axis_at] // shards_of).reshape((-1,) + (1,) * (len(shape) - 1 - axis_at))
    return gain


def deal_out(own_key, own, number, rows, count, top, reach, lean):
    order = jax.random.permutation(own_key, count)
    heavy_load, usual = load_shares(count, rows * top, reach, lean, True), load_shares(count, rows * top, reach, lean, False)
    places = jnp.arange(count)

    def named(tallies, rotation):
        used = int((tallies > 0).sum())
        fixed = max(1, used // 4)
        moved = fixed + (places - fixed + rotation * (used - fixed)) % max(1, count - fixed)
        return jnp.zeros((count,), jnp.int32).at[order[jnp.where(places < fixed, places, moved)]].set(jnp.asarray(tallies, jnp.int32))

    tallies = jnp.where(number % 4 == 0, named(heavy_load, number // 4), named(usual, number - number // 4 - 1))
    mixed = jax.random.permutation(jax.random.fold_in(own, 3), count)
    giver, taker = mixed[0:count // 2 * 2:2], mixed[1:count // 2 * 2:2]
    room = jnp.minimum(tallies[giver] - 1, reach - tallies[taker]) // 2
    room = jnp.where((giver == order[0]) | (taker == order[0]) | (tallies[taker] == 0), 0, jnp.maximum(room, 0))
    moved = jax.random.randint(jax.random.fold_in(own, 4), (count // 2,), 0, 1 << 20) % (room + 1)
    tallies = tallies.at[giver].add(-moved).at[taker].add(moved)
    members = jnp.searchsorted(jnp.cumsum(tallies), jnp.arange(rows * top), side="right").astype(jnp.int32)
    grid = members.reshape(top, rows).T
    grid = grid[jax.random.permutation(jax.random.fold_in(own, 1), rows)]
    rotation = jax.random.randint(jax.random.fold_in(own, 2), (rows, 1), 0, top)
    return jnp.take_along_axis(grid, (jnp.arange(top)[None, :] + rotation) % top, axis=1)


def load_shares(count, total, most, skew, full):
    loads = [(1 << 20) // math.isqrt(standing ** skew) + 1 for standing in range(1, count + 1)]
    largest = most if full else min(most, max(-(-total // count), total * loads[0] // sum(loads)))
    least = 1 if total - largest >= count - 1 else 0
    given, rest = [largest] + [least] * (count - 1), total - largest - least * (count - 1)
    while rest > 0:
        candidates = [i for i in range(1, count) if given[i] < largest] or [i for i in range(1, count) if given[i] < most]
        mass, left = sum([loads[i] for i in candidates]), rest
        for i in candidates:
            more = min(most - given[i], max(1, left * loads[i] // mass), rest)
            given[i] = given[i] + more
            rest = rest - more
    return np.array(given)


def centred(own_key, dims, width, limit, cuts=(), held_as=jnp.bfloat16):
    entries = width * jax.random.normal(own_key, dims, jnp.float32)
    if cuts:
        entries = entries * block_levels(own_key, dims, cuts, -0.22, 0.18)
    return jnp.clip(entries, -limit, limit).astype(held_as)


def setup_inputs(seed: int = 0) -> dict:
    keys = jax.random.split(jax.random.key(seed), 15)
    hidden_in = centred(keys[0], (SEQUENCE_COUNT, SEQUENCE_LENGTH, D), 1.0, 6.0, ((0, 16), (1, 8)))
    positions = draw_positions(jax.random.fold_in(keys[14], 71), 0)
    starts = draw_starts(jax.random.fold_in(keys[14], 71), 0)
    routes_keys = jax.random.split(jax.random.fold_in(keys[3], 1), SEQUENCE_COUNT * SEQUENCE_LENGTH // TS)
    routes_turns = jax.random.permutation(jax.random.fold_in(keys[3], 3), SEQUENCE_COUNT * SEQUENCE_LENGTH // TS)
    routes = jax.vmap(lambda own, number: deal_out(jax.random.fold_in(keys[3], 2), own, number, TS, E, TOP, MOST, 1))(routes_keys, routes_turns).reshape((SEQUENCE_COUNT, SEQUENCE_LENGTH, TOP))
    qkv_weight = centred(keys[4], (QKVW, D), D ** -0.5, 0.1875, ((0, 128),))
    out_weight = centred(keys[5], (D, D), (D // 64) ** -0.5, 1.5, ((0, 128),))
    expert_in = centred(keys[6], (D, E, 2 * FF), D ** -0.5, 0.1875, ((0, 128),))
    expert_out = centred(keys[7], (D, E, FF), (FF // 32) ** -0.5, 1.5, ((0, 128),))
    router = centred(keys[8], (D, E), (4 * D) ** -0.5, 0.09375)
    attn_gain = jnp.clip(1.0 + 0.15 * jax.random.normal(keys[9], (D,), jnp.float32), 0.25, 1.75).astype(jnp.bfloat16)
    query_gain = jnp.clip(1.0 + 0.15 * jax.random.normal(keys[10], (D,), jnp.float32), 0.25, 1.75).astype(jnp.bfloat16)
    key_gain = jnp.clip(1.0 + 0.15 * jax.random.normal(keys[11], (KVW,), jnp.float32), 0.25, 1.75).astype(jnp.bfloat16)
    mlp_gain = jnp.clip(1.0 + 0.15 * jax.random.normal(keys[12], (D,), jnp.float32), 0.25, 1.75).astype(jnp.bfloat16)
    out_grad = centred(keys[13], (SEQUENCE_COUNT, SEQUENCE_LENGTH, D), 1.0, 6.0, ((0, 16), (1, 8)))
    return {"hidden_in": hidden_in, "positions": positions, "starts": starts, "routes": routes, "qkv_weight": qkv_weight, "out_weight": out_weight, "expert_in": expert_in, "expert_out": expert_out, "router": router, "attn_gain": attn_gain, "query_gain": query_gain, "key_gain": key_gain, "mlp_gain": mlp_gain, "out_grad": out_grad}


EPSILON = 1e-06
ROPE_BASE = 10000.0
PRECISE = lax.Precision.HIGHEST

@jax.custom_vjp
def low(v):
    return lax.optimization_barrier(v.astype(jnp.bfloat16)).astype(jnp.float32)

@jax.custom_vjp
def low_back(v):
    return v

def low_keep(v):
    return (low(v), None)

def low_pass(kept, grad):
    return (grad,)

def back_keep(v):
    return (v, None)

def back_low(kept, grad):
    return (low(grad),)
low.defvjp(low_keep, low_pass)
low_back.defvjp(back_keep, back_low)

def root_mean_norm(field, gain_row):
    return field * lax.rsqrt(lax.optimization_barrier(jnp.mean(field * field, axis=-1, keepdims=True)) + EPSILON) * gain_row

def apply_rotary(field, cosine_values, sine_values):
    half_size = field.shape[-1] // 2
    lower_half = field[..., :half_size]
    upper_half = field[..., half_size:]
    return jnp.concatenate([lower_half * cosine_values - upper_half * sine_values, upper_half * cosine_values + lower_half * sine_values], axis=-1)

def sequence_mask(piece_starts):
    places = jnp.arange(SEQUENCE_LENGTH, dtype=jnp.int32)
    inside = (places[:, None] >= piece_starts[None, :]) & (places[:, None] < piece_starts[None, :] + PIECE)
    labels = lax.optimization_barrier(jnp.sum(inside.astype(jnp.int32) * (jnp.arange(NPIC, dtype=jnp.int32) + 1), axis=1))
    return (places[None, :] <= places[:, None]) | (labels[:, None] == labels[None, :]) & (labels[:, None] > 0)

def single_sequence(packed):
    query_rotated, key_rotated, value_reduced, piece_starts = packed
    allowed = sequence_mask(piece_starts)
    score_scale = query_rotated.shape[-1] ** (-0.5)
    scores = low_back(jnp.einsum('tkgd,skd->kgts', query_rotated, key_rotated, precision=PRECISE) * score_scale)
    scores = jnp.where(allowed, scores, -1e+30)
    attn_probs = low(jax.nn.softmax(scores, axis=-1))
    return jnp.einsum('kgts,skd->tkgd', attn_probs, value_reduced, precision=PRECISE)

def reference(hidden_in, positions, starts, routes, qkv_weight, out_weight, expert_in, expert_out, router, attn_gain, query_gain, key_gain, mlp_gain, out_grad):
    token_rows = SEQUENCE_COUNT * SEQUENCE_LENGTH
    head_width = D // QUERY_HEADS
    key_value_width = KEY_VALUE_HEADS * head_width
    query_group_width = QUERY_HEADS // KEY_VALUE_HEADS
    half_size = head_width // 2
    frequency = ROPE_BASE ** (-jnp.arange(half_size, dtype=jnp.float32) * 2.0 / head_width)
    angles = positions.reshape(token_rows).astype(jnp.float32)[:, None] * frequency
    cosine_values = jnp.cos(angles)[:, None, :]
    sine_values = jnp.sin(angles)[:, None, :]
    member = (routes.reshape(token_rows, TOP)[:, :, None] == jnp.arange(E, dtype=jnp.int32)).astype(jnp.float32)
    chosen = lax.optimization_barrier(jnp.sum(member, axis=1))

    def forward(inputs, w_qkv, w_attn_out, w_in_all, w_down_all, w_route, gain_attn, gain_query, key_norm_gain, gain_mlp):
        x_flat = inputs.reshape(token_rows, D)
        x_low = low(root_mean_norm(x_flat, gain_attn))
        qkv = low_back(jnp.dot(x_low, w_qkv.T, precision=PRECISE))
        q_raw = qkv[:, :D]
        key_unnormed = qkv[:, D:D + key_value_width]
        v_raw = qkv[:, D + key_value_width:]
        query_rotated = low(apply_rotary(root_mean_norm(q_raw, gain_query).reshape(token_rows, QUERY_HEADS, head_width), cosine_values, sine_values))
        key_rotated = low(apply_rotary(root_mean_norm(key_unnormed, key_norm_gain).reshape(token_rows, KEY_VALUE_HEADS, head_width), cosine_values, sine_values))
        value_reduced = low(v_raw)
        attention_mixed = lax.map(jax.checkpoint(single_sequence), (query_rotated.reshape(SEQUENCE_COUNT, SEQUENCE_LENGTH, KEY_VALUE_HEADS, query_group_width, head_width), key_rotated.reshape(SEQUENCE_COUNT, SEQUENCE_LENGTH, KEY_VALUE_HEADS, head_width), value_reduced.reshape(SEQUENCE_COUNT, SEQUENCE_LENGTH, KEY_VALUE_HEADS, head_width), starts))
        attn_low = low(low_back(attention_mixed.reshape(token_rows, D)))
        midway = x_flat + low_back(jnp.dot(attn_low, w_attn_out.T, precision=PRECISE))
        h_low = low(root_mean_norm(midway, gain_mlp))
        gates = jax.nn.softmax(low_back(jnp.dot(h_low, w_route, precision=PRECISE)), axis=-1)
        combine = gates * chosen

        def expert_step(running, slab_part):
            w_in_one, w_out_one, weight_col = slab_part
            gate_up = low_back(jnp.dot(h_low, w_in_one, precision=PRECISE))
            act_low = low(jax.nn.silu(gate_up[:, :FF]) * gate_up[:, FF:])
            exp_result = low_back(jnp.dot(act_low, w_out_one.T, precision=PRECISE))
            return (running + weight_col[:, None] * exp_result, None)
        mixture, unused = lax.scan(jax.checkpoint(expert_step), jnp.zeros((token_rows, D), jnp.float32), (jnp.moveaxis(w_in_all, 1, 0), jnp.moveaxis(w_down_all, 1, 0), combine.T))
        return midway + mixture
    primals = (hidden_in.astype(jnp.float32), qkv_weight.astype(jnp.float32), out_weight.astype(jnp.float32), expert_in.astype(jnp.float32), expert_out.astype(jnp.float32), router.astype(jnp.float32), attn_gain.astype(jnp.float32), query_gain.astype(jnp.float32), key_gain.astype(jnp.float32), mlp_gain.astype(jnp.float32))
    outcome, pullback = jax.vjp(forward, *primals)
    gradients = pullback(out_grad.reshape(token_rows, D).astype(jnp.float32))
    return (outcome.astype(jnp.bfloat16).reshape(SEQUENCE_COUNT, SEQUENCE_LENGTH, D), gradients[0], gradients[1], gradients[2], gradients[3], gradients[4], gradients[5], gradients[6], gradients[7], gradients[8], gradients[9])
```

```python
import jax
import jax.numpy as jnp
import numpy as np
from jax import lax
from jax.sharding import PartitionSpec as P

QUERY_HEADS = 16
KEY_VALUE_HEADS = 8
PIECE = 256
EPSILON = 1e-06
ROPE_BASE = 10000.0
MASKED = -1e30
F32 = jnp.float32
BF16 = jnp.bfloat16


def rms_scale(field):
    return lax.rsqrt(jnp.mean(field * field, axis=-1, keepdims=True) + EPSILON)


def rms_back(upstream, normed, scales):
    return scales * (upstream - normed * jnp.mean(upstream * normed, axis=-1, keepdims=True))


def rotary(field, cosine, sine):
    half = field.shape[-1] // 2
    a, b = field[..., :half], field[..., half:]
    return jnp.concatenate([a * cosine - b * sine, b * cosine + a * sine], axis=-1)


def owner_of(s, c):
    if s < 8:
        return 8 * c + s
    if s < 12:
        return 64 + 4 * c + (s - 8)
    return 96 + 4 * c + (s - 12)


def dot(a, b, ca, cb):
    return lax.dot_general(a, b, (((ca,), (cb,)), ((), ())), preferred_element_type=F32)


def local(hidden_in, positions, starts, routes, qkv_weight, out_weight, expert_in, expert_out,
          router, attn_gain, query_gain, key_gain, mlp_gain, out_grad):
    rows = hidden_in.shape[1]
    width = hidden_in.shape[2]
    me = lax.axis_index("ctx")
    ns, nc = lax.axis_size("seq"), lax.axis_size("ctx")
    perm_in = [(owner_of(s, c), s * nc + c) for s in range(ns) for c in range(nc)]
    perm_out = [(b, a) for a, b in perm_in]
    ag = lambda v, ax: lax.all_gather(v, ax, axis=0, tiled=True)
    a2a = lambda v, sp, cc: lax.all_to_all(v, "ctx", sp, cc, tiled=True)
    w_qkv = ag(lax.ppermute(qkv_weight, ("seq", "ctx"), perm_in), "seq")
    w_out = ag(a2a(out_weight, 1, 0), "seq")
    w_in = ag(a2a(expert_in, 1, 0)[:, 0], "seq")
    w_down = ag(a2a(expert_out, 1, 0)[:, 0], "seq")
    x_own = hidden_in[0].astype(F32)
    x = ag(hidden_in[0], "ctx").astype(F32)
    dy = ag(out_grad[0], "ctx").astype(F32)
    pos = ag(positions[0], "ctx")
    routes_all = ag(routes[0], "ctx")
    s1 = rms_scale(x)
    attn_gain_f = attn_gain.astype(F32)
    x_low = (x * s1 * attn_gain_f).astype(BF16)
    qkv = dot(x_low, w_qkv, 1, 1)
    q, k, v = qkv[:, :128], qkv[:, 128:192], qkv[:, 192:]
    sums = lax.psum(jnp.stack([jnp.sum(q * q, 1), jnp.sum(k * k, 1)]), "ctx")
    sq = lax.rsqrt(sums[0] / 1024 + EPSILON)[:, None]
    sk = lax.rsqrt(sums[1] / 512 + EPSILON)[:, None]
    nq, nk = q * sq, k * sk
    gq = lax.dynamic_slice(query_gain, (128 * me,), (128,)).astype(F32)
    gk = lax.dynamic_slice(key_gain, (64 * me,), (64,)).astype(F32)
    freq = ROPE_BASE ** (-jnp.arange(32, dtype=F32) * 2.0 / 64)
    ang = pos.astype(F32)[:, None] * freq
    cosv, sinv = jnp.cos(ang), jnp.sin(ang)
    q_rot = rotary((nq * gq).reshape(-1, 2, 64), cosv[:, None], sinv[:, None]).astype(BF16)
    k_rot = rotary(nk * gk, cosv, sinv).astype(BF16)
    v_low = v.astype(BF16)
    places = jnp.arange(pos.shape[0], dtype=jnp.int32)
    inside = (places[:, None] >= starts) & (places[:, None] < starts + PIECE)
    label = jnp.sum(inside.astype(jnp.int32) * jnp.array([1, 2], jnp.int32), axis=1)
    allowed = (places[None, :] <= places[:, None]) | (
        (label[:, None] == label[None, :]) & (label[:, None] > 0))
    scores = jnp.einsum("tgd,sd->gts", q_rot, k_rot, preferred_element_type=F32) * 0.125
    scores = jnp.where(allowed[None], scores, MASKED)
    p = jax.nn.softmax(scores, axis=-1)
    p_low = p.astype(BF16)
    attn = jnp.einsum("gts,sd->tgd", p_low, v_low, preferred_element_type=F32)
    attn_low = attn.reshape(-1, 128).astype(BF16)
    rs = lambda t: lax.psum_scatter(t, "ctx", scatter_dimension=0, tiled=True)
    mid = x_own + rs(dot(attn_low, w_out, 1, 1))
    s2 = rms_scale(mid)
    n2 = mid * s2
    gm = mlp_gain.astype(F32)
    h_own = (n2 * gm).astype(BF16)
    gates_own = jax.nn.softmax(jnp.dot(h_own, router, preferred_element_type=F32), axis=-1)
    h = ag(h_own, "ctx")
    gates = ag(gates_own, "ctx")
    routed = jnp.any(routes_all == me, axis=1)
    gate_c = jnp.where(routed, lax.dynamic_slice(gates, (0, me), (gates.shape[0], 1))[:, 0], 0.0)[:, None]
    gu = dot(h, w_in, 1, 0)
    g, u = gu[:, :512], gu[:, 512:]
    sig = jax.nn.sigmoid(g)
    sw = g * sig
    act = (sw * u).astype(BF16)
    res = dot(act, w_down, 1, 1)
    result = (mid + rs(gate_c * res)).astype(BF16)[None]
    d_res = (gate_c * dy).astype(BF16)
    d_gate_c = jnp.where(routed, jnp.sum(dy * res, axis=1), 0.0)
    d_act = dot(d_res, w_down, 1, 0)
    d_gu = jnp.concatenate([d_act * u * sig * (1.0 + g * (1.0 - sig)), d_act * sw], axis=1).astype(BF16)
    d_h = rs(dot(d_gu, w_in, 1, 1))
    g_in = dot(h, d_gu, 0, 0)
    g_down = dot(d_res, act, 0, 0)
    d_gates = a2a(d_gate_c[:, None], 0, 1)
    d_logits = (gates_own * (d_gates - jnp.sum(gates_own * d_gates, axis=1, keepdims=True))).astype(BF16)
    d_h = d_h + dot(d_logits, router, 1, 1)
    router_loc = dot(h_own, d_logits, 0, 0)
    mlp_loc = jnp.sum(d_h * n2, axis=0)
    d_mid = out_grad[0].astype(F32) + rms_back(d_h * gm, n2, s2)
    d_branch_own = d_mid.astype(BF16)
    d_branch = ag(d_branch_own, "ctx")
    d_attn = dot(d_branch, w_out, 1, 0).astype(BF16)
    g_out = dot(d_branch, attn_low, 0, 0)
    dp = jnp.einsum("tgd,sd->gts", d_attn.reshape(-1, 2, 64), v_low, preferred_element_type=F32)
    ds = (p * (dp - jnp.sum(p * dp, axis=-1, keepdims=True))).astype(BF16)
    dq = jnp.einsum("gts,sd->tgd", ds, k_rot, preferred_element_type=F32) * 0.125
    dk = jnp.einsum("gts,tgd->sd", ds, q_rot, preferred_element_type=F32) * 0.125
    dv = jnp.einsum("gts,tgd->sd", p_low, d_attn.reshape(-1, 2, 64), preferred_element_type=F32)
    dnq = rotary(dq, cosv[:, None], -sinv[:, None]).reshape(-1, 128)
    dnk = rotary(dk, cosv, -sinv)
    gq_loc = jnp.sum(dnq * nq, axis=0)
    gk_loc = jnp.sum(dnk * nk, axis=0)
    means = lax.psum(jnp.stack([jnp.sum(dnq * gq * nq, 1), jnp.sum(dnk * gk * nk, 1)]), "ctx")
    d_q = sq * (dnq * gq - nq * means[0][:, None] / 1024)
    d_k = sk * (dnk * gk - nk * means[1][:, None] / 512)
    d_qkv = jnp.concatenate([d_q, d_k, dv], axis=1).astype(BF16)
    d_x_low = rs(dot(d_qkv, w_qkv, 1, 0))
    g_qkv = dot(d_qkv, x_low, 0, 0)
    s1_own = rms_scale(x_own)
    n1_own = x_own * s1_own
    attn_loc = jnp.sum(d_x_low * n1_own, axis=0)
    grad_input = (d_mid + rms_back(d_x_low * attn_gain_f, n1_own, s1_own))[None]
    rss = lambda t: lax.psum_scatter(t, "seq", scatter_dimension=0, tiled=True)
    grad_qkv = lax.ppermute(rss(g_qkv), ("seq", "ctx"), perm_out)
    grad_out = a2a(rss(g_out), 0, 1)
    grad_in = a2a(rss(g_in)[:, None], 0, 1)
    grad_down = a2a(rss(g_down)[:, None], 0, 1)
    gq_all = lax.dynamic_update_slice(jnp.zeros((1024,), F32), gq_loc, (128 * me,))
    gk_all = lax.dynamic_update_slice(jnp.zeros((512,), F32), gk_loc, (64 * me,))
    ga, gqo, gko, gmo, gr = lax.psum((attn_loc, gq_all, gk_all, mlp_loc, router_loc), ("seq", "ctx"))
    return result, grad_input, grad_qkv, grad_out, grad_in, grad_down, gr, ga, gqo, gko, gmo


def solution(mesh):
    t = ("seq", "ctx")
    in_specs = (P("seq", "ctx", None), P("seq", "ctx"), P("seq", None), P("seq", "ctx", None),
                P(t, None), P(t, None), P(t, None, None), P(t, None, None),
                P(), P(), P(), P(), P(), P("seq", "ctx", None))
    out_specs = (P("seq", "ctx", None), P("seq", "ctx", None), P(t, None), P(t, None),
                 P(t, None, None), P(t, None, None), P(), P(), P(), P(), P())
    return jax.shard_map(local, mesh=mesh, in_specs=in_specs, out_specs=out_specs, check_vma=False)
```

```python
import functools

import jax
import jax.numpy as jnp
from jax import lax
from jax.experimental import pallas as pl
from jax.experimental.pallas import tpu as pltpu
from jax.sharding import PartitionSpec as P

PIECE = 256
EPSILON = 1e-06
ROPE_BASE = 10000.0
MASKED = -1e30
F32 = jnp.float32
BF16 = jnp.bfloat16
MESH = pl.DeviceIdType.MESH
HI = lax.Precision.HIGHEST
SEMS = 320


def dot(a, b, ca, cb, precision=None):
    return lax.dot_general(a, b, (((ca,), (cb,)), ((), ())), precision=precision,
                           preferred_element_type=F32)


def iota(shape, axis):
    return lax.broadcasted_iota(jnp.int32, shape, axis)


class Sems:
    def __init__(self, send, recv):
        self.send, self.recv, self.used, self.log = send, recv, 0, []

    def take(self, count):
        base = self.used
        self.used += count
        assert self.used <= SEMS
        return base


def kernel(hid, og, wq, wo, wi, wd, par1, par2, tbl, starts, rt, rout,
           res_o, gi_o, gq_o, go_o, gin_o, gdn_o, sm_o,
           xl, dyb, hb, dbb, tb, wqb, wo1, wi1, wd1, wob, wib, wdb,
           qkvb, scb, qr, ka, kb, va, vb, at, pb, drawb, dgub, agb,
           part, sibb, rin, st, stb, st2, gtb, dgs, dgr, midb, dab, dqb, dkv, dnb, dqkv,
           gin_s, gin_r, gdn_s, gdn_r, go_s, go_r, gq_s, gq_r, gsum_in, gsum_dn, gsum_o,
           sm3, sm1, sm2, acc, send, recv):
    s, c = lax.axis_index("seq"), lax.axis_index("ctx")
    z, k = lax.div(c, 2), lax.rem(c, 2)
    sems = Sems(send, recv)
    sib = (s, z * 2 + 1 - k)
    drain = []

    def zdev(dz):
        return (s, lax.rem(z + dz, 4) * 2 + k)

    def cpeer(dc):
        return (s, lax.rem(c + dc, 8))

    def speer(ds):
        return (lax.rem(s + ds, 16), c)

    def copy(src, dst, index, slot, dev):
        return pltpu.make_async_remote_copy(src_ref=src, dst_ref=dst, send_sem=send.at[index],
                                            recv_sem=recv.at[slot], device_id=dev, device_id_type=MESH)

    def got(dst, slot):
        copy(dst, dst, slot, slot, sib).wait_recv()

    def sent(src, index):
        copy(src, src, index, index, sib).wait_send()

    c4, r4 = lax.div(c, 4), lax.rem(c, 4)
    tg = jnp.where(s < 8, s, jnp.where(s < 12, 2 * (s - 8) + c4, 2 * (s - 12) + c4))
    ts = jnp.where(s < 8, c, jnp.where(s < 12, 8 + r4, 12 + r4))
    mine = tg == c

    def owner(j):
        half = lax.div(c, 2)
        odd = 4 * lax.rem(c, 2)
        os = jnp.where(j < 8, c, jnp.where(j < 12, 8 + half, 12 + half))
        oc = jnp.where(j < 8, j, jnp.where(j < 12, odd + j - 8, odd + j - 12))
        return os, oc

    def not_me(dev):
        return jnp.logical_or(dev[0] != s, dev[1] != c)

    bar = pltpu.get_barrier_semaphore()
    for dc in range(1, 8):
        pl.semaphore_signal(bar, inc=1, device_id=cpeer(dc), device_id_type=MESH)

    def sig_seq(ds, _):
        pl.semaphore_signal(bar, inc=1, device_id=speer(ds), device_id_type=MESH)
        return 0
    lax.fori_loop(1, 16, sig_seq, 0)

    def sig_own(j, _):
        dev = owner(j)

        @pl.when(not_me(dev))
        def _():
            pl.semaphore_signal(bar, inc=1, device_id=dev, device_id_type=MESH)
        dev2 = (j, tg)

        @pl.when(not_me(dev2))
        def _():
            pl.semaphore_signal(bar, inc=1, device_id=dev2, device_id_type=MESH)
        return 0
    lax.fori_loop(0, 16, sig_own, 0)

    gain_a = par1[0:1, :]
    gain_m = par1[1:2, :]
    gains = par2[pl.ds(c, 1), :]
    x = hid[...].astype(F32)
    s1 = lax.rsqrt(jnp.mean(x * x, axis=-1, keepdims=True) + EPSILON)
    xl[c] = (x * s1 * gain_a).astype(BF16)
    tb[c] = tbl[...]
    dyb[c] = og[...]
    wo1[c] = wo[c]
    wi1[c] = wi[c]
    wd1[c] = wd[c]

    @pl.when(mine)
    def _():
        wqb[ts] = wq[...]
    pl.semaphore_wait(bar, 54 - 2 * mine.astype(jnp.int32))

    def ag_start(buf):
        base = sems.take(7)
        for dz in (1, 3, 2):
            copy(buf.at[c], buf.at[c], base + dz - 1, base + dz - 1, zdev(dz)).start()
        copy(buf.at[c], buf.at[c], base + 3, base + 3, sib).start()

        def done():
            for i in range(7):
                sent(buf.at[c], base + i)
        drain.append(done)
        return base

    def ag_chip(buf, base, n, dz):
        ch = lax.rem(z - dz + 4, 4)
        b = ch * 2 + k

        @pl.when(n > 0)
        def _():
            got(buf.at[b], base + dz - 1)
            copy(buf.at[b], buf.at[b], base + 3 + dz, base + 3 + dz, sib).start()
        got(buf.at[b], base + 3 + dz)
        return ch

    def gray(n):
        return jnp.where(n == 2, 3, jnp.where(n == 3, 2, n))

    xbase = ag_start(xl)
    qs = sems.take(16)

    def send_q(j, _):
        dev = (j, tg)

        @pl.when(not_me(dev))
        def _():
            copy(wq, wqb.at[ts], qs + j, qs + ts, dev).start()
        return 0
    lax.fori_loop(0, 16, send_q, 0)
    tbase = ag_start(tb)
    w1 = sems.take(21)
    for a, (src, dst) in enumerate(((wo, wo1), (wd, wd1), (wi, wi1))):
        for dc in range(1, 8):
            dev = cpeer(dc)
            copy(src.at[dev[1]], dst.at[c], w1 + 7 * a + dc - 1, w1 + 7 * a + dc - 1, dev).start()

    ws = sems.take(45)
    for a, (one, full, width) in enumerate(((wo1, wob, 128), (wd1, wdb, 512), (wi1, wib, 1024))):
        for dc in range(1, 8):
            got(one.at[0], w1 + 7 * a + dc - 1)
        full[s] = one[...].astype(F32).reshape(64, width).astype(BF16)

        def send_w(ds, _, a=a, full=full):
            copy(full.at[s], full.at[s], ws + 15 * a + ds - 1, ws + 15 * a + ds - 1, speer(ds)).start()
            return 0
        lax.fori_loop(1, 16, send_w, 0)

    def got_w(a, full):
        def body(ds, _):
            got(full.at[0], ws + 15 * a + ds - 1)
            return 0
        lax.fori_loop(1, 16, body, 0)

    def wait_q(j, _):
        @pl.when(not_me(owner(j)))
        def _():
            got(wqb.at[0], qs + j)
        return 0
    lax.fori_loop(0, 16, wait_q, 0)

    lane = iota((1, 256), 1)
    sel8 = jnp.where(iota((8, 256), 0) == 0, jnp.where(iota((8, 256), 1) < 128, 1.0, 0.0),
                     jnp.where((iota((8, 256), 0) == 1) & (iota((8, 256), 1) >= 128)
                               & (iota((8, 256), 1) < 192), 1.0, 0.0))

    def put_rows(ref, ch, rows):
        ref[pl.ds(2 * ch, 1), :] = rows[0:1, 0:128]
        ref[pl.ds(2 * ch + 1, 1), :] = rows[0:1, 128:256]
        ref[pl.ds(8 + 2 * ch, 1), :] = rows[1:2, 0:128]
        ref[pl.ds(9 + 2 * ch, 1), :] = rows[1:2, 128:256]

    def qkv_step(n, _):
        dz = gray(n)
        ch = ag_chip(xl, xbase, n, dz)
        qkv = dot(xl[pl.ds(2 * ch, 2)].reshape(256, 1024), wqb[...].reshape(256, 1024), 1, 1)
        qkvb[ch] = qkv
        put_rows(st, ch, dot(sel8, qkv * qkv, 1, 1, HI))
        return 0
    lax.fori_loop(0, 4, qkv_step, 0)

    def all_reduce(own, slots):
        base = sems.take(7)
        slots[c] = own[...]
        for dc in range(1, 8):
            copy(slots.at[c], slots.at[c], base + dc - 1, base + dc - 1, cpeer(dc)).start()

        def finish():
            for dc in range(1, 8):
                got(slots.at[0], base + dc - 1)
            return jnp.sum(slots[...], axis=0)

        def done():
            for i in range(7):
                sent(slots.at[c], base + i)
        drain.append(done)
        return finish

    row16 = iota((16, 128), 0)
    count = jnp.where(row16 < 8, 1.0 / 1024, 1.0 / 512)
    finish = all_reduce(st, stb.at[0])
    dybase = ag_start(dyb)

    def table_step(n, _):
        ag_chip(tb, tbase, n, gray(n))
        return 0
    lax.fori_loop(0, 4, table_step, 0)
    st[...] = lax.rsqrt(finish() * count + EPSILON)

    def pick(b):
        r, l = iota((16, 256), 0), iota((16, 256), 1)
        return jnp.where(((r == b) & (l < 128)) | ((r == 8 + b) & (l >= 128) & (l < 192)), 1.0, 0.0)

    even = lax.rem(lax.div(iota((128, 128), 1), 32), 2) == 0
    low64 = iota((128, 128), 1) < 64

    def tables(b):
        t = tb[b]
        t2 = pltpu.roll(t, 32, 1)
        return jnp.where(even, t, t2), jnp.where(even, -t2, t)

    def partner(w):
        return jnp.where(even, pltpu.roll(w, 96, 1), pltpu.roll(w, 32, 1))

    def rope_step(b, _):
        rows = pl.ds(lax.rem(b, 2) * 128, 128)
        ch = lax.div(b, 2)
        scale = dot(st[...], pick(b), 0, 0, HI) + jnp.where(lane >= 192, 1.0, 0.0)
        scb[ch, rows, :] = scale
        normed = qkvb[ch, rows, :] * scale
        qkvb[ch, rows, :] = normed
        w = normed * gains
        cs, sn = tables(b)
        wq_, wk_ = w[:, :128], w[:, 128:]
        qr[b] = ((wq_ * cs + partner(wq_) * sn) * 0.125).astype(BF16)
        kv = wk_ * jnp.where(low64, cs, 1.0) + partner(wk_) * jnp.where(low64, sn, 0.0)
        k0 = jnp.where(low64, kv, 0.0)
        v1 = jnp.where(low64, 0.0, kv)
        ka[b] = k0.astype(BF16)
        kb[b] = pltpu.roll(k0, 64, 1).astype(BF16)
        va[b] = pltpu.roll(v1, 64, 1).astype(BF16)
        vb[b] = v1.astype(BF16)
        return 0
    lax.fori_loop(0, 8, rope_step, 0)

    def rs_new():
        return sems.take(4), sems.take(3)

    def rs_first(r, base, ch):
        copy(part.at[r, ch, 1 - k], sibb.at[r, ch], base[0] + ch, base[0] + ch, sib).start()

    def rs_second(r, base, ch):
        got(sibb.at[r, ch], base[0] + ch)
        part[r, ch, k] = (part[r, ch, k].astype(F32) + sibb[r, ch].astype(F32)).astype(BF16)
        dz = lax.rem(ch - z + 4, 4)

        @pl.when(dz > 0)
        def _():
            copy(part.at[r, ch, k], rin.at[r, dz - 1], base[1] + dz - 1, base[1] + dz - 1,
                 (s, ch * 2 + k)).start()

    def rs_finish(r, base):
        for i in range(3):
            got(rin.at[r, i], base[1] + i)

        def done():
            for i in range(4):
                sent(part.at[r, 0, 0], base[0] + i)
            for i in range(3):
                sent(part.at[r, 0, 0], base[1] + i)
        drain.append(done)
        total = part[r, z, k].astype(F32)
        for i in range(3):
            total = total + rin[r, i].astype(F32)
        return total

    st0, st1 = starts[0, 0], starts[0, 1]

    def limits(ch):
        row = ch * 256 + iota((256, 1), 0)
        lim = jnp.where((row >= st0) & (row < st0 + PIECE), st0 + PIECE - 1, row)
        return jnp.where((row >= st1) & (row < st1 + PIECE), st1 + PIECE - 1, lim)

    def keys(ref, length):
        return ref[0:length // 128].reshape(length, 128)

    def attend(ch, length):
        q = qr[pl.ds(2 * ch, 2)].reshape(256, 128)
        allowed = iota((256, length), 1) <= limits(ch)
        out = None
        for h, (kk, vv) in enumerate(((ka, va), (kb, vb))):
            sc = jnp.where(allowed, dot(q, keys(kk, length), 1, 1), MASKED)
            e = jnp.exp(sc - jnp.max(sc, axis=-1, keepdims=True))
            p = (e * (1.0 / jnp.sum(e, axis=-1, keepdims=True))).astype(BF16)
            pb[h, ch, :, 0:length] = p
            o = dot(p, keys(vv, length), 1, 0)
            out = o if out is None else out + o
        at[ch] = out.astype(BF16)

    got_w(0, wob)
    rs_mid = rs_new()

    def fwd_step(n, _):
        ch = lax.rem(z + 1 + n, 4)

        @pl.when(ch < 2)
        def _():
            attend(ch, 512)

        @pl.when(ch >= 2)
        def _():
            attend(ch, 1024)
        o = dot(at[ch], wob[...].reshape(1024, 128), 1, 1)
        part[0, ch] = o.astype(BF16).reshape(2, 128, 1024)
        rs_first(0, rs_mid, ch)

        @pl.when(n > 0)
        def _():
            rs_second(0, rs_mid, lax.rem(z + n, 4))
        return 0
    lax.fori_loop(0, 4, fwd_step, 0)
    rs_second(0, rs_mid, z)

    got_w(1, wdb)

    def draw_step(n, _):
        ch = ag_chip(dyb, dybase, n, gray(n))
        drawb[ch] = dot(dyb[pl.ds(2 * ch, 2)].reshape(256, 1024), wdb[...].reshape(1024, 512), 1, 0)
        return 0
    lax.fori_loop(0, 4, draw_step, 0)

    mid = hid[...].astype(F32) + rs_finish(0, rs_mid)
    midb[...] = mid
    s2 = lax.rsqrt(jnp.mean(mid * mid, axis=-1, keepdims=True) + EPSILON)
    h_own = (mid * s2 * gain_m).astype(BF16)
    hb[c] = h_own
    logits = dot(rout[...], h_own, 1, 1)
    e8 = jnp.exp(logits - jnp.max(logits, axis=0, keepdims=True))
    gates = e8 / jnp.sum(e8, axis=0, keepdims=True)
    er = iota((8, 128), 0)
    member = jnp.zeros((8, 128), F32)
    for j in range(4):
        member = member + jnp.where(rt[j:j + 1, :] == er, 1.0, 0.0)
    gtb[c] = gates * member
    gbase = sems.take(7)
    for dc in range(1, 8):
        copy(gtb.at[c], gtb.at[c], gbase + dc - 1, gbase + dc - 1, cpeer(dc)).start()
    hbase = ag_start(hb)
    got_w(2, wib)
    for dc in range(1, 8):
        got(gtb.at[0], gbase + dc - 1)

    one_c = jnp.where(iota((8, 128), 0) == c, 1.0, 0.0)
    rs_res, rs_dh = rs_new(), rs_new()

    def expert_step(n, _):
        dz = gray(n)
        ch = ag_chip(hb, hbase, n, dz)
        gu = dot(hb[pl.ds(2 * ch, 2)].reshape(256, 1024), wib[...].reshape(1024, 1024), 1, 0)
        g, u = gu[:, :512], gu[:, 512:]
        sig = 1.0 / (1.0 + jnp.exp(-g))
        sw = g * sig
        act = sw * u
        gate = jnp.concatenate([dot(gtb[2 * ch], one_c, 0, 0, HI), dot(gtb[2 * ch + 1], one_c, 0, 0, HI)], axis=0)
        gate = jnp.concatenate([gate] * 4, axis=1)
        draw = drawb[ch]
        ag = (act * gate).astype(BF16)
        agb[ch] = ag
        rows = dot(jnp.ones((8, 512), F32), act * draw, 1, 1, HI)
        dgs[2 * ch] = rows[:, 0:128]
        dgs[2 * ch + 1] = rows[:, 128:256]
        d_act = draw * gate
        dgub[ch, :, 0:512] = (d_act * u * sig * (1.0 + g * (1.0 - sig))).astype(BF16)
        dgub[ch, :, 512:1024] = (d_act * sw).astype(BF16)
        dh = dot(dgub[ch], wib[...].reshape(1024, 1024), 1, 1)
        part[1, ch] = dh.astype(BF16).reshape(2, 128, 1024)
        rs_first(1, rs_dh, ch)
        rs = dot(agb[ch], wdb[...].reshape(1024, 512), 1, 1)
        part[2, ch] = rs.astype(BF16).reshape(2, 128, 1024)
        rs_first(2, rs_res, ch)

        @pl.when(n > 0)
        def _():
            before = lax.rem(z - gray(n - 1) + 4, 4)
            rs_second(1, rs_dh, before)
            rs_second(2, rs_res, before)
        return 0
    lax.fori_loop(0, 4, expert_step, 0)
    dbase = sems.take(7)
    dgr[c] = dgs[c]
    for dc in range(1, 8):
        dev = cpeer(dc)
        copy(dgs.at[dev[1]], dgr.at[c], dbase + dc - 1, dbase + dc - 1, dev).start()
    last = lax.rem(z + 2, 4)
    rs_second(1, rs_dh, last)
    rs_second(2, rs_res, last)

    gs = sems.take(45)

    def send_g(a, src, dst):
        dst[s] = src[s]

        def body(ds, _):
            dev = speer(ds)
            copy(src.at[dev[0]], dst.at[s], gs + 15 * a + ds - 1, gs + 15 * a + ds - 1, dev).start()
            return 0
        lax.fori_loop(1, 16, body, 0)

        def done():
            def wait(ds, _):
                sent(src.at[0], gs + 15 * a + ds - 1)
                return 0
            lax.fori_loop(1, 16, wait, 0)
        drain.append(done)

    def got_g(a, dst):
        def body(ds, _):
            got(dst.at[0], gs + 15 * a + ds - 1)
            return 0
        lax.fori_loop(1, 16, body, 0)

    def gdn_step(i, _):
        cols = pl.ds(pl.multiple_of(i * 256, 256), 256)
        g = dot(dyb[:, :, cols].reshape(1024, 256), agb[...].reshape(1024, 512), 0, 0)
        gdn_s[pl.ds(4 * i, 4)] = g.astype(BF16).reshape(4, 64, 512)
        return 0
    lax.fori_loop(0, 4, gdn_step, 0)
    send_g(1, gdn_s, gdn_r)

    for dc in range(1, 8):
        got(dgr.at[0], dbase + dc - 1)
    dg = jnp.concatenate([dgr[e, 0:1, :] for e in range(8)], axis=0) * member
    d_logits = (gates * (dg - jnp.sum(gates * dg, axis=0, keepdims=True))).astype(BF16)
    d_h = rs_finish(1, rs_dh) + dot(d_logits, rout[...], 0, 0)
    mid = midb[...]
    s2 = lax.rsqrt(jnp.mean(mid * mid, axis=-1, keepdims=True) + EPSILON)
    n2 = mid * s2
    up = d_h * gain_m
    d_mid = og[...].astype(F32) + s2 * (up - n2 * jnp.mean(up * n2, axis=-1, keepdims=True))
    gi_o[...] = d_mid
    dbb[c] = d_mid.astype(BF16)
    bbase = ag_start(dbb)
    g_router = dot(d_logits, hb[c], 1, 0)
    g_mlp = jnp.sum(d_h * n2, axis=0, keepdims=True)
    for p in range(8):
        cut = slice(128 * p, 128 * p + 128)
        sm3[p, 0:8, :] = g_router[:, cut]
        sm3[p, 9:10, :] = g_mlp[:, cut]

    def gin_step(i, _):
        cols = pl.ds(pl.multiple_of(i * 256, 256), 256)
        g = dot(hb[:, :, cols].reshape(1024, 256), dgub[...].reshape(1024, 1024), 0, 0)
        gin_s[pl.ds(4 * i, 4)] = g.astype(BF16).reshape(4, 64, 1024)
        return 0
    lax.fori_loop(0, 4, gin_step, 0)
    send_g(0, gin_s, gin_r)
    res_o[...] = (midb[...] + rs_finish(2, rs_res)).astype(BF16)

    dkv[...] = jnp.zeros_like(dkv)
    low256 = iota((256, 128), 1) < 64

    def attend_back(ch, length):
        da = dab[ch]
        q = qr[pl.ds(2 * ch, 2)].reshape(256, 128).astype(F32)
        daf = da.astype(F32)
        dq = None
        left, right = [], []
        for h, (kk, vv) in enumerate(((ka, va), (kb, vb))):
            p = pb[h, ch, :, 0:length]
            pf = p.astype(F32)
            dp = dot(da, keys(vv, length), 1, 1)
            ds = (pf * (dp - jnp.sum(pf * dp, axis=-1, keepdims=True))).astype(BF16)
            o = dot(ds, keys(kk, length), 1, 0)
            dq = o if dq is None else dq + o
            qh = jnp.where(low256, q if h == 0 else pltpu.roll(q, 64, 1), 0.0)
            dh_ = jnp.where(low256, 0.0, daf if h == 1 else pltpu.roll(daf, 64, 1))
            left += [ds, p]
            right += [qh.astype(BF16), dh_.astype(BF16)]
        dqb[ch] = dq * 0.125
        for l, r in zip(left, right):
            dkv[0:length, :] += dot(l, r, 0, 0)

    def bwd_step(n, _):
        ch = ag_chip(dbb, bbase, n, gray(n))
        dab[ch] = dot(dbb[pl.ds(2 * ch, 2)].reshape(256, 1024), wob[...].reshape(1024, 128), 1, 0).astype(BF16)

        @pl.when(ch < 2)
        def _():
            attend_back(ch, 512)

        @pl.when(ch >= 2)
        def _():
            attend_back(ch, 1024)
        return 0
    lax.fori_loop(0, 4, bwd_step, 0)

    acc[...] = jnp.zeros_like(acc)

    def unrope_step(ch, _):
        for kk in range(2):
            b = 2 * ch + kk
            rows = slice(128 * kk, 128 * kk + 128)
            cs, sn = tables(b)
            wq_ = dqb[ch, rows, :]
            wk_ = dkv[pl.ds(pl.multiple_of(b * 128, 128), 128), :]
            dq = wq_ * cs - partner(wq_) * sn
            dk = wk_ * jnp.where(low64, cs, 1.0) - partner(wk_) * jnp.where(low64, sn, 0.0)
            dn = jnp.concatenate([dq, dk], axis=1)
            normed = qkvb[ch, rows, :]
            acc[1:2, 0:256] += jnp.sum(dn * normed, axis=0, keepdims=True)
            dnb[ch, rows, :] = dn * gains
        put_rows(st2, ch, dot(sel8, dnb[ch] * qkvb[ch], 1, 1, HI))
        return 0
    lax.fori_loop(0, 4, unrope_step, 0)
    finish2 = all_reduce(st2, stb.at[1])

    def go_step(i, _):
        cols = pl.ds(pl.multiple_of(i * 256, 256), 256)
        g = dot(dbb[:, :, cols].reshape(1024, 256), at[...].reshape(1024, 128), 0, 0)
        go_s[pl.ds(4 * i, 4)] = g.astype(BF16).reshape(4, 64, 128)
        return 0
    lax.fori_loop(0, 4, go_step, 0)
    send_g(2, go_s, go_r)
    st2[...] = finish2() * count

    rs_dx = rs_new()

    def dx_step(n, _):
        ch = lax.rem(z + 1 + n, 4)
        for kk in range(2):
            b = 2 * ch + kk
            rows = slice(128 * kk, 128 * kk + 128)
            mean = dot(st2[...], pick(b), 0, 0, HI)
            d = scb[ch, rows, :] * (dnb[ch, rows, :] - qkvb[ch, rows, :] * mean)
            dqkv[ch, rows, :] = d.astype(BF16)
        dx = dot(dqkv[ch], wqb[...].reshape(256, 1024), 1, 0)
        part[3, ch] = dx.astype(BF16).reshape(2, 128, 1024)
        rs_first(3, rs_dx, ch)
        acc[0:1, :] += jnp.sum(dx * xl[pl.ds(2 * ch, 2)].reshape(256, 1024).astype(F32), axis=0, keepdims=True)

        @pl.when(n > 0)
        def _():
            rs_second(3, rs_dx, lax.rem(z + n, 4))
        return 0
    lax.fori_loop(0, 4, dx_step, 0)
    rs_second(3, rs_dx, z)

    g_attn = acc[0:1, :] / gain_a
    for p in range(8):
        sm3[p, 8:9, :] = g_attn[:, 128 * p:128 * p + 128]
        sm3[p, 10:16, :] = jnp.zeros((6, 128), F32)
    m1, m2, m3 = sems.take(7), sems.take(15), sems.take(7)
    sm1[c] = sm3[c]
    for dc in range(1, 8):
        dev = cpeer(dc)
        copy(sm3.at[dev[1]], sm1.at[c], m1 + dc - 1, m1 + dc - 1, dev).start()

    g = dot(dqkv[...].reshape(1024, 256), xl[...].reshape(1024, 1024), 0, 0)
    gq_s[...] = g.astype(BF16).reshape(16, 16, 1024)
    qg = sems.take(16)
    qr_sem = sems.take(16)

    @pl.when(mine)
    def _():
        gq_r[s] = gq_s[ts]

    def send_gq(j, _):
        dev = owner(j)

        @pl.when(not_me(dev))
        def _():
            copy(gq_s.at[j], gq_r.at[s], qg + j, qr_sem + s, dev).start()
        return 0
    lax.fori_loop(0, 16, send_gq, 0)

    for dc in range(1, 8):
        got(sm1.at[0], m1 + dc - 1)
    tot = jnp.sum(sm1[...], axis=0)
    r16 = iota((16, 128), 0)
    tot = tot + jnp.where(r16 == 10, acc[1:2, 0:128], 0.0) + jnp.where(r16 == 11, acc[1:2, 128:256], 0.0)
    sm2[s] = tot

    def send_m(ds, _):
        copy(sm2.at[s], sm2.at[s], m2 + ds - 1, m2 + ds - 1, speer(ds)).start()
        return 0
    lax.fori_loop(1, 16, send_m, 0)

    a2 = sems.take(21)
    for a, (src, tot_ref, out, width) in enumerate(((gin_r, gsum_in, gin_o, 1024), (gdn_r, gsum_dn, gdn_o, 512),
                                                    (go_r, gsum_o, go_o, 128))):
        got_g(a, src)

        def add(i, t, src=src):
            return t + src[i].astype(F32)
        tot_ref[...] = lax.fori_loop(1, 16, add, src[0].astype(F32)).reshape(8, 8, width)
        out[c] = tot_ref[c]
        for dc in range(1, 8):
            dev = cpeer(dc)
            copy(tot_ref.at[dev[1]], out.at[c], a2 + 7 * a + dc - 1, a2 + 7 * a + dc - 1, dev).start()

    def got_m(ds, _):
        got(sm2.at[0], m2 + ds - 1)
        return 0
    lax.fori_loop(1, 16, got_m, 0)
    sm_o[c] = jnp.sum(sm2[...], axis=0)
    for dc in range(1, 8):
        copy(sm_o.at[c], sm_o.at[c], m3 + dc - 1, m3 + dc - 1, cpeer(dc)).start()

    d_x = rs_finish(3, rs_dx)
    x = hid[...].astype(F32)
    s1 = lax.rsqrt(jnp.mean(x * x, axis=-1, keepdims=True) + EPSILON)
    n1 = x * s1
    up = d_x * gain_a
    gi_o[...] += s1 * (up - n1 * jnp.mean(up * n1, axis=-1, keepdims=True))

    def wait_gq(j, _):
        @pl.when(not_me((j, tg)))
        def _():
            got(gq_r.at[0], qr_sem + j)
        return 0
    lax.fori_loop(0, 16, wait_gq, 0)

    def add_q(i, t):
        return t + gq_r[i].astype(F32)
    gq_o[...] = lax.fori_loop(1, 16, add_q, gq_r[0].astype(F32))

    for a, out in enumerate((gin_o, gdn_o, go_o)):
        for dc in range(1, 8):
            got(out.at[0], a2 + 7 * a + dc - 1)
    for dc in range(1, 8):
        got(sm_o.at[0], m3 + dc - 1)
    for done in drain:
        done()
    for a, src in enumerate((wo, wd, wi)):
        for dc in range(1, 8):
            sent(src.at[0], w1 + 7 * a + dc - 1)
    for a, full in enumerate((wob, wdb, wib)):
        def wait(ds, _, a=a, full=full):
            sent(full.at[0], ws + 15 * a + ds - 1)
            return 0
        lax.fori_loop(1, 16, wait, 0)

    def wait_qs(j, _):
        @pl.when(not_me((j, tg)))
        def _():
            sent(wq, qs + j)

        @pl.when(not_me(owner(j)))
        def _():
            sent(gq_s.at[0], qg + j)
        return 0
    lax.fori_loop(0, 16, wait_qs, 0)
    for dc in range(1, 8):
        sent(gtb.at[0], gbase + dc - 1)
        sent(dgs.at[0], dbase + dc - 1)
        sent(sm3.at[0], m1 + dc - 1)
        sent(sm_o.at[0], m3 + dc - 1)
        for a, tot_ref in enumerate((gsum_in, gsum_dn, gsum_o)):
            sent(tot_ref.at[0], a2 + 7 * a + dc - 1)

    def wait_m(ds, _):
        sent(sm2.at[0], m2 + ds - 1)
        return 0
    lax.fori_loop(1, 16, wait_m, 0)


def local(hidden_in, positions, starts, routes, qkv_weight, out_weight, expert_in, expert_out,
          router, attn_gain, query_gain, key_gain, mlp_gain, out_grad):
    par1 = jnp.stack([attn_gain, mlp_gain]).astype(F32)
    par2 = jnp.concatenate([query_gain.astype(F32).reshape(8, 128), key_gain.astype(F32).reshape(8, 64),
                            jnp.ones((8, 64), F32)], axis=1)
    lane = jnp.arange(128)
    freq = ROPE_BASE ** (-(lane % 32).astype(F32) * 2.0 / 64)
    ang = positions[0].astype(F32)[:, None] * freq
    tbl = jnp.where((lane // 32) % 2 == 0, jnp.cos(ang), jnp.sin(ang))
    wo = out_weight.reshape(8, 8, 128).transpose(1, 0, 2)
    wi = expert_in.transpose(1, 0, 2)
    wd = expert_out.transpose(1, 0, 2)
    V = pltpu.VMEM
    scratch = dict(
        xl=V((8, 128, 1024), BF16), dyb=V((8, 128, 1024), BF16), hb=V((8, 128, 1024), BF16),
        dbb=V((8, 128, 1024), BF16), tb=V((8, 128, 128), F32), wqb=V((16, 16, 1024), BF16),
        wo1=V((8, 8, 128), BF16), wi1=V((8, 8, 1024), BF16), wd1=V((8, 8, 512), BF16),
        wob=V((16, 64, 128), BF16), wib=V((16, 64, 1024), BF16), wdb=V((16, 64, 512), BF16),
        qkvb=V((4, 256, 256), F32), scb=V((4, 256, 256), F32), qr=V((8, 128, 128), BF16),
        ka=V((8, 128, 128), BF16), kb=V((8, 128, 128), BF16), va=V((8, 128, 128), BF16), vb=V((8, 128, 128), BF16),
        at=V((4, 256, 128), BF16), pb=V((2, 4, 256, 1024), BF16), drawb=V((4, 256, 512), F32),
        dgub=V((4, 256, 1024), BF16), agb=V((4, 256, 512), BF16),
        part=V((4, 4, 2, 128, 1024), BF16), sibb=V((4, 4, 128, 1024), BF16), rin=V((4, 3, 128, 1024), BF16),
        st=V((16, 128), F32), stb=V((2, 8, 16, 128), F32), st2=V((16, 128), F32), gtb=V((8, 8, 128), F32),
        dgs=V((8, 8, 128), F32), dgr=V((8, 8, 128), F32), midb=V((128, 1024), F32), dab=V((4, 256, 128), BF16),
        dqb=V((4, 256, 128), F32), dkv=V((1024, 128), F32), dnb=V((4, 256, 256), F32), dqkv=V((4, 256, 256), BF16),
        gin_s=V((16, 64, 1024), BF16), gin_r=V((16, 64, 1024), BF16), gdn_s=V((16, 64, 512), BF16),
        gdn_r=V((16, 64, 512), BF16), go_s=V((16, 64, 128), BF16), go_r=V((16, 64, 128), BF16),
        gq_s=V((16, 16, 1024), BF16), gq_r=V((16, 16, 1024), BF16),
        gsum_in=V((8, 8, 1024), F32), gsum_dn=V((8, 8, 512), F32), gsum_o=V((8, 8, 128), F32),
        sm3=V((8, 16, 128), F32), sm1=V((8, 16, 128), F32), sm2=V((16, 16, 128), F32), acc=V((8, 1024), F32),
        send=pltpu.SemaphoreType.DMA((SEMS,)), recv=pltpu.SemaphoreType.DMA((SEMS,)))
    vm = pl.BlockSpec(memory_space=pltpu.VMEM)
    outs = pl.pallas_call(
        kernel,
        out_shape=[jax.ShapeDtypeStruct(sh, dt) for sh, dt in (
            ((128, 1024), BF16), ((128, 1024), F32), ((16, 1024), F32), ((8, 8, 128), F32),
            ((8, 8, 1024), F32), ((8, 8, 512), F32), ((8, 16, 128), F32))],
        in_specs=[vm] * 9 + [pl.BlockSpec(memory_space=pltpu.SMEM)] + [vm] * 2,
        out_specs=[vm] * 7,
        scratch_shapes=list(scratch.values()),
        compiler_params=pltpu.CompilerParams(collective_id=0, has_side_effects=True,
                                             vmem_limit_bytes=60 * 2**20),
        name="layer",
    )(hidden_in[0], out_grad[0], qkv_weight, wo, wi, wd, par1, par2, tbl, starts, routes[0].T, router.T)
    res, gi, gq, go, gin, gdn, sm = outs
    rows = sm.transpose(1, 0, 2)
    return (res[None], gi[None], gq, go.transpose(1, 0, 2).reshape(8, 1024), gin.transpose(1, 0, 2),
            gdn.transpose(1, 0, 2), rows[0:8].reshape(8, 1024).T, rows[8].reshape(1024), rows[10].reshape(1024),
            rows[11, :, :64].reshape(512), rows[9].reshape(1024))


def solution(mesh):
    t = ("seq", "ctx")
    in_specs = (P("seq", "ctx", None), P("seq", "ctx"), P("seq", None), P("seq", "ctx", None),
                P(t, None), P(t, None), P(t, None, None), P(t, None, None),
                P(), P(), P(), P(), P(), P("seq", "ctx", None))
    out_specs = (P("seq", "ctx", None), P("seq", "ctx", None), P(t, None), P(t, None),
                 P(t, None, None), P(t, None, None), P(), P(), P(), P(), P())
    return jax.shard_map(local, mesh=mesh, in_specs=in_specs, out_specs=out_specs, check_vma=False)
```

```python
import functools

import jax
import jax.numpy as jnp
from jax import lax
from jax.experimental import pallas as pl
from jax.experimental.pallas import tpu as pltpu
from jax.sharding import PartitionSpec as P

PIECE = 256
EPSILON = 1e-06
ROPE_BASE = 10000.0
MASKED = -1e30
F32 = jnp.float32
BF16 = jnp.bfloat16
MESH = pl.DeviceIdType.MESH
SENDS, RECVS = 36, 74


def dot(a, b, ca, cb):
    return lax.dot_general(a, b, (((ca,), (cb,)), ((), ())), preferred_element_type=F32)


def iota(shape, axis):
    return lax.broadcasted_iota(jnp.int32, shape, axis)


class Copies:
    def __init__(self, send, recv, dev):
        self.send, self.recv, self.dev = send, recv, dev
        self.drains, self.sends, self.recvs = [], 0, 0

    def group(self, count, total):
        first, mine = self.recvs, self.sends
        self.recvs += count
        self.sends += 1
        assert self.recvs <= RECVS and self.sends <= SENDS
        return Group(self, first, mine, total)


class Group:
    def __init__(self, owner, first, mine, total):
        self.owner, self.first, self.mine = owner, first, mine
        if total is not None:
            owner.drains.append((self, total))

    def make(self, src, dst, i, dev):
        return pltpu.make_async_remote_copy(
            src_ref=src, dst_ref=dst, send_sem=self.owner.send.at[self.mine],
            recv_sem=self.owner.recv.at[self.first + i], device_id=dev, device_id_type=MESH)

    def put(self, src, dst, i, dev):
        self.make(src, dst, i, dev).start()

    def got(self, dst, i=0):
        self.make(dst, dst, i, self.owner.dev).wait_recv()

    def sent(self, src):
        self.make(src, src, 0, self.owner.dev).wait_send()


def kernel(hid, og, wq, wo, wd, par1, par2, tbl, starts, rt, rout,
           res_o, gi_o, gq_o, go_o, gw_o, sm_o,
           xl, dyb, hb, dbb, tb, wqb, wo1, wd1, wob, wb,
           qkvb, scb, qr, ka, kb, va, vb, at, pb, drawb, dgub, agb,
           part, sibb, rin, st, stb, st2, gtb, dgs, dgr, midb, dab, dkv, dqkv,
           g_s, g_r1, g_p, g_r2, go_s, go_r, gq_s, gq_r, gq_t, gsum, gsum_o,
           sm3, sm1, sm2, acc, send, recv):
    s, c = lax.axis_index("seq"), lax.axis_index("ctx")
    z, k = lax.div(c, 2), lax.rem(c, 2)
    y, x_ = lax.div(s, 4), lax.rem(s, 4)
    sib = (s, z * 2 + 1 - k)
    cp = Copies(send, recv, sib)
    dnb, dqb = drawb.at[:, :, 0:256], drawb.at[:, :, 256:384]

    def zdev(dz):
        return (s, lax.rem(z + dz, 4) * 2 + k)

    def cpeer(dc):
        return (s, lax.rem(c + dc, 8))

    def speer(ds):
        return (lax.rem(s + ds, 16), c)

    def near(d):
        return jnp.where(k == 0, y * 4 + lax.rem(x_ + d, 4), lax.rem(y + d, 4) * 4 + x_)

    def far(d):
        return jnp.where(k == 0, lax.rem(y + d, 4) * 4 + x_, y * 4 + lax.rem(x_ + d, 4))

    def cross(a, b):
        return jnp.where(k == 0, lax.rem(y + b, 4) * 4 + lax.rem(x_ + a, 4),
                         lax.rem(y + a, 4) * 4 + lax.rem(x_ + b, 4))

    c4, r4 = lax.div(c, 4), lax.rem(c, 4)
    tg = jnp.where(s < 8, s, jnp.where(s < 12, 2 * (s - 8) + c4, 2 * (s - 12) + c4))
    ts = jnp.where(s < 8, c, jnp.where(s < 12, 8 + r4, 12 + r4))
    mine = (tg == c) & (ts == s)

    def owner(j):
        half = lax.div(c, 2)
        odd = 4 * lax.rem(c, 2)
        os = jnp.where(j < 8, c, jnp.where(j < 12, 8 + half, 12 + half))
        oc = jnp.where(j < 8, j, jnp.where(j < 12, odd + j - 8, odd + j - 12))
        return os, oc

    home = owner(s)
    tk = lax.rem(tg, 2)
    ty, tx = lax.div(ts, 4), lax.rem(ts, 4)

    def aim(a):
        return jnp.where(tk == 0, ty * 4 + lax.rem(tx + a, 4), lax.rem(ty + a, 4) * 4 + tx), tg

    def not_me(dev):
        return jnp.logical_or(dev[0] != s, dev[1] != c)

    bar = pltpu.get_barrier_semaphore()

    for a in range(4):
        source = owner(near(a))

        @pl.when(not_me(source))
        def _(source=source):
            pl.semaphore_signal(bar, inc=1, device_id=source, device_id_type=MESH)
    for dc in range(1, 8):
        pl.semaphore_signal(bar, inc=1, device_id=cpeer(dc), device_id_type=MESH)
    for d in range(1, 4):
        pl.semaphore_signal(bar, inc=1, device_id=(near(d), c), device_id_type=MESH)
        pl.semaphore_signal(bar, inc=1, device_id=(far(d), c), device_id_type=MESH)

    gain_a = par1[0:1, :]
    gain_m = par1[1:2, :]
    gains = par2[pl.ds(c, 1), :]
    x = hid[...].astype(F32)
    s1 = lax.rsqrt(jnp.mean(x * x, axis=-1, keepdims=True) + EPSILON)
    xl[c] = (x * s1 * gain_a).astype(BF16)
    tb[c] = tbl[...]
    dyb[c] = og[...]
    wo1[c] = wo[c]
    wd1[c] = wd[c]

    selfish = jnp.int32(0)
    for a in range(4):
        selfish = selfish + jnp.where(not_me(aim(a)), 0, 1)

    @pl.when(selfish > 0)
    def _():
        wqb[ts] = wq[...]
    pl.semaphore_wait(bar, 17 - selfish)

    def ag_start(buf):
        g = cp.group(7, buf.at[0:7])
        for dz in (1, 3, 2):
            g.put(buf.at[c], buf.at[c], dz - 1, zdev(dz))
        g.put(buf.at[c], buf.at[c], 3, sib)
        return g

    def gray(n):
        return jnp.where(n == 2, 3, jnp.where(n == 3, 2, n))

    def ag_pass(buf, g, n):
        dz = gray(n)
        b = lax.rem(z - dz + 4, 4) * 2 + k
        g.got(buf.at[b], dz - 1)
        g.put(buf.at[b], buf.at[b], 3 + dz, sib)

    def ag_have(buf, g, n):
        dz = gray(n)
        ch = lax.rem(z - dz + 4, 4)
        g.got(buf.at[ch * 2 + 1 - k], 3 + dz)
        return ch

    def ag_next(buf, g, n):
        @pl.when(n < 3)
        def _():
            ag_pass(buf, g, n + 1)

    def xy_start(buf):
        near_g = cp.group(1, buf.at[0:3])
        far_g = cp.group(1, buf.at[0:12])
        for d in (1, 3, 2):
            near_g.put(buf.at[s], buf.at[s], 0, (near(d), c))
        for d in (1, 3, 2):
            far_g.put(buf.at[s], buf.at[s], 0, (far(d), c))
        return near_g, far_g

    def xy_pass(buf, g):
        g[0].got(buf.at[0:3])
        for a in (1, 3, 2):
            block = near(a)
            for d in (1, 3, 2):
                g[1].put(buf.at[block], buf.at[block], 0, (far(d), c))

    def xy_have(buf, g):
        g[1].got(buf.at[0:12])

    def ctx_put(src, dst, own=True):
        g = cp.group(1, dst.at[0:7])
        for dc in range(1, 8):
            dev = cpeer(dc)
            g.put(src.at[dev[1]] if own else src.at[c], dst.at[c], 0, dev)
        return g

    home_g = cp.group(4, None)
    for a in (0, 1, 3, 2):
        dev = aim(a)

        @pl.when(not_me(dev))
        def _(dev=dev, a=a):
            home_g.put(wq, wqb.at[ts], a, dev)
    wo_g = ctx_put(wo, wo1)
    wd_g = ctx_put(wd, wd1)
    x_g = ag_start(xl)
    tb_g = ctx_put(tb, tb, False)

    wq_g = cp.group(1, wqb.at[0:12])
    for a in range(4):
        block = near(a)

        @pl.when(not_me(owner(block)))
        def _(a=a):
            home_g.got(wqb.at[0], (4 - a) % 4)
        for d in (1, 3, 2):
            wq_g.put(wqb.at[block], wqb.at[block], 0, (far(d), c))
    wo_g.got(wo1.at[0:7])
    wob[s] = wo1[...].astype(F32).reshape(64, 128).astype(BF16)
    wo_x = xy_start(wob)
    wd_g.got(wd1.at[0:7])
    wb[s] = wd1[...].astype(F32).reshape(64, 1536).astype(BF16)
    w_x = xy_start(wb)
    ag_pass(xl, x_g, 1)
    ag_pass(xl, x_g, 2)
    xy_pass(wob, wo_x)
    wq_g.got(wqb.at[0:12])

    def wi_full():
        return wb[:, :, 0:1024].reshape(1024, 1024)

    def wd_full():
        return wb[:, :, 1024:1536].reshape(1024, 512)

    lane = iota((1, 256), 1)

    def halves(v):
        high = v.astype(BF16)
        return high, (v - high.astype(F32)).astype(BF16)

    def split(v):
        return jnp.concatenate(halves(v), axis=0)

    def row_sums(ones, v):
        high, low = halves(v)
        return dot(ones, high, 1, 1) + dot(ones, low, 1, 1)

    sel8 = jnp.where(iota((8, 256), 0) == 0, jnp.where(iota((8, 256), 1) < 128, 1.0, 0.0),
                     jnp.where((iota((8, 256), 0) == 1) & (iota((8, 256), 1) >= 128)
                               & (iota((8, 256), 1) < 192), 1.0, 0.0)).astype(BF16)

    def put_rows(ref, ch, rows):
        ref[pl.ds(2 * ch, 1), :] = rows[0:1, 0:128]
        ref[pl.ds(2 * ch + 1, 1), :] = rows[0:1, 128:256]
        ref[pl.ds(8 + 2 * ch, 1), :] = rows[1:2, 0:128]
        ref[pl.ds(9 + 2 * ch, 1), :] = rows[1:2, 128:256]

    def qkv_step(n, _):
        @pl.when(n == 2)
        def _():
            ag_pass(xl, x_g, 3)
        ch = ag_have(xl, x_g, n)
        qkv = dot(xl[pl.ds(2 * ch, 2)].reshape(256, 1024), wqb[...].reshape(256, 1024), 1, 1)
        qkvb[ch] = qkv
        put_rows(st, ch, row_sums(sel8, qkv * qkv))
        return 0
    lax.fori_loop(0, 4, qkv_step, 0)

    def all_reduce(own, slots):
        slots[c] = own[...]
        g = ctx_put(slots, slots, False)

        def finish():
            g.got(slots.at[0:7])
            return jnp.sum(slots[...], axis=0)
        return finish

    row16 = iota((16, 128), 0)
    count = jnp.where(row16 < 8, 1.0 / 1024, 1.0 / 512)
    finish = all_reduce(st, stb.at[0])
    dy_g = ag_start(dyb)
    xy_pass(wb, w_x)
    tb_g.got(tb.at[0:7])
    scale_parts = split(lax.rsqrt(finish() * count + EPSILON))

    def pick(b):
        r, l = lax.rem(iota((32, 256), 0), 16), iota((32, 256), 1)
        return jnp.where(((r == b) & (l < 128)) | ((r == 8 + b) & (l >= 128) & (l < 192)), 1.0, 0.0).astype(BF16)

    even = lax.rem(lax.div(iota((128, 128), 1), 32), 2) == 0
    low64 = iota((128, 128), 1) < 64

    def tables(b):
        t = tb[b]
        r = pltpu.roll(t, 64, 1)
        low = iota((64, 128), 1) < 64
        t = jnp.concatenate([jnp.where(low, t, r), jnp.where(low, r, t)], axis=0)
        t2 = pltpu.roll(t, 32, 1)
        return jnp.where(even, t, t2), jnp.where(even, -t2, t)

    def partner(w):
        return jnp.where(even, pltpu.roll(w, 96, 1), pltpu.roll(w, 32, 1))

    def rope_step(b, _):
        rows = pl.ds(lax.rem(b, 2) * 128, 128)
        ch = lax.div(b, 2)
        scale = dot(scale_parts, pick(b), 0, 0) + jnp.where(lane >= 192, 1.0, 0.0)
        scb[ch, rows, :] = scale
        normed = qkvb[ch, rows, :] * scale
        qkvb[ch, rows, :] = normed
        w = normed * gains
        cs, sn = tables(b)
        wq_, wk_ = w[:, :128], w[:, 128:]
        qr[b] = ((wq_ * cs + partner(wq_) * sn) * 0.125).astype(BF16)
        kv = wk_ * jnp.where(low64, cs, 1.0) + partner(wk_) * jnp.where(low64, sn, 0.0)
        k0 = jnp.where(low64, kv, 0.0)
        v1 = jnp.where(low64, 0.0, kv)
        ka[b] = k0.astype(BF16)
        kb[b] = pltpu.roll(k0, 64, 1).astype(BF16)
        va[b] = pltpu.roll(v1, 64, 1).astype(BF16)
        vb[b] = v1.astype(BF16)
        return 0
    lax.fori_loop(0, 8, rope_step, 0)

    def rs_new(r):
        return cp.group(4, sibb.at[r]), cp.group(1, rin.at[r])

    def rs_first(r, g, ch):
        g[0].put(part.at[r, ch, 1 - k], sibb.at[r, ch], ch, sib)

    def rs_second(r, g, ch):
        g[0].got(sibb.at[r, ch], ch)
        part[r, ch, k] = (part[r, ch, k].astype(F32) + sibb[r, ch].astype(F32)).astype(BF16)
        dz = lax.rem(ch - z + 4, 4)

        @pl.when(dz > 0)
        def _():
            g[1].put(part.at[r, ch, k], rin.at[r, dz - 1], 0, (s, ch * 2 + k))

    def rs_finish(r, g):
        g[1].got(rin.at[r])
        total = part[r, z, k].astype(F32)
        for i in range(3):
            total = total + rin[r, i].astype(F32)
        return total

    st0, st1 = starts[0, 0], starts[0, 1]

    def limits(ch):
        row = ch * 256 + iota((256, 1), 0)
        lim = jnp.where((row >= st0) & (row < st0 + PIECE), st0 + PIECE - 1, row)
        return jnp.where((row >= st1) & (row < st1 + PIECE), st1 + PIECE - 1, lim)

    def keys(ref, length):
        return ref[0:length // 128].reshape(length, 128)

    def attend(ch, length):
        q = qr[pl.ds(2 * ch, 2)].reshape(256, 128)
        allowed = iota((256, length), 1) <= limits(ch)
        out = None
        for h, (kk, vv) in enumerate(((ka, va), (kb, vb))):
            sc = jnp.where(allowed, dot(q, keys(kk, length), 1, 1), MASKED)
            e = jnp.exp(sc - jnp.max(sc, axis=-1, keepdims=True))
            p = (e * (1.0 / jnp.sum(e, axis=-1, keepdims=True))).astype(BF16)
            pb[h, ch, :, 0:length] = p
            o = dot(p, keys(vv, length), 1, 0)
            out = o if out is None else out + o
        at[ch] = out.astype(BF16)

    mid_g = rs_new(0)

    def fwd_step(n, _):
        ch = lax.rem(z + 1 + n, 4)

        @pl.when(ch < 2)
        def _():
            attend(ch, 512)

        @pl.when(ch >= 2)
        def _():
            attend(ch, 1024)

        @pl.when(n == 0)
        def _():
            xy_have(wob, wo_x)
        o = dot(at[ch], wob[...].reshape(1024, 128), 1, 1)
        part[0, ch] = o.astype(BF16).reshape(2, 128, 1024)
        rs_first(0, mid_g, ch)

        @pl.when(n > 0)
        def _():
            rs_second(0, mid_g, lax.rem(z + n, 4))
        return 0
    lax.fori_loop(0, 4, fwd_step, 0)
    rs_second(0, mid_g, z)

    ag_pass(dyb, dy_g, 1)
    ag_pass(dyb, dy_g, 2)
    ag_pass(dyb, dy_g, 3)
    xy_have(wb, w_x)

    def draw_step(n, _):
        ch = ag_have(dyb, dy_g, n)
        drawb[ch] = dot(dyb[pl.ds(2 * ch, 2)].reshape(256, 1024), wd_full(), 1, 0)
        return 0
    lax.fori_loop(0, 4, draw_step, 0)

    mid = hid[...].astype(F32) + rs_finish(0, mid_g)
    midb[...] = mid
    s2 = lax.rsqrt(jnp.mean(mid * mid, axis=-1, keepdims=True) + EPSILON)
    h_own = (mid * s2 * gain_m).astype(BF16)
    hb[c] = h_own
    logits = dot(rout[...], h_own, 1, 1)
    e8 = jnp.exp(logits - jnp.max(logits, axis=0, keepdims=True))
    gates = e8 / jnp.sum(e8, axis=0, keepdims=True)
    er = iota((8, 128), 0)
    member = jnp.zeros((8, 128), F32)
    for j in range(4):
        member = member + jnp.where(rt[j:j + 1, :] == er, 1.0, 0.0)
    gtb[c] = gates * member
    gt_g = ctx_put(gtb, gtb, False)
    h_g = ag_start(hb)

    one_c = jnp.where(lax.rem(iota((16, 128), 0), 8) == c, 1.0, 0.0).astype(BF16)
    dh_g, res_g = rs_new(1), rs_new(2)

    def expert_step(n, _):
        ch = ag_have(hb, h_g, n)
        gu = dot(hb[pl.ds(2 * ch, 2)].reshape(256, 1024), wi_full(), 1, 0)
        g, u = gu[:, :512], gu[:, 512:]
        sig = 1.0 / (1.0 + jnp.exp(-g))
        sw = g * sig
        act = sw * u

        @pl.when(n == 0)
        def _():
            gt_g.got(gtb.at[0:7])
        gate = jnp.concatenate([dot(split(gtb[2 * ch]), one_c, 0, 0), dot(split(gtb[2 * ch + 1]), one_c, 0, 0)], axis=0)
        gate = jnp.concatenate([gate] * 4, axis=1)
        draw = drawb[ch]
        agb[ch] = (act * gate).astype(BF16)
        rows = row_sums(jnp.ones((8, 512), BF16), act * draw)
        dgs[2 * ch] = rows[:, 0:128]
        dgs[2 * ch + 1] = rows[:, 128:256]
        d_act = draw * gate
        dgub[ch, :, 0:512] = (d_act * u * sig * (1.0 + g * (1.0 - sig))).astype(BF16)
        dgub[ch, :, 512:1024] = (d_act * sw).astype(BF16)
        dh = dot(dgub[ch], wi_full(), 1, 1)
        part[1, ch] = dh.astype(BF16).reshape(2, 128, 1024)
        rs_first(1, dh_g, ch)
        rs = dot(agb[ch], wd_full(), 1, 1)
        part[2, ch] = rs.astype(BF16).reshape(2, 128, 1024)
        rs_first(2, res_g, ch)
        ag_next(hb, h_g, n)
        rs_second(1, dh_g, ch)
        return 0
    lax.fori_loop(0, 4, expert_step, 0)
    dgr[c] = dgs[c]
    dg_g = ctx_put(dgs, dgr)

    def gw_step(i, _):
        cols = pl.ds(pl.multiple_of(i * 256, 256), 256)
        g = dot(dyb[:, :, cols].reshape(1024, 256), agb[...].reshape(1024, 512), 0, 0)
        g_s[pl.ds(4 * i, 4), :, 1024:1536] = g.astype(BF16).reshape(4, 64, 512)
        g = dot(hb[:, :, cols].reshape(1024, 256), dgub[...].reshape(1024, 1024), 0, 0)
        g_s[pl.ds(4 * i, 4), :, 0:1024] = g.astype(BF16).reshape(4, 64, 1024)
        return 0
    lax.fori_loop(0, 4, gw_step, 0)
    g1, g2 = cp.group(1, g_s.at[0:12]), cp.group(1, g_s.at[0:3])
    for d in (1, 3, 2):
        for e in range(4):
            g1.put(g_s.at[cross(d, e)], g_r1.at[d - 1, e], 0, (near(d), c))

    dg_g.got(dgr.at[0:7])
    dg = jnp.concatenate([dgr[e, 0:1, :] for e in range(8)], axis=0) * member
    d_logits = (gates * (dg - jnp.sum(gates * dg, axis=0, keepdims=True))).astype(BF16)
    d_h = rs_finish(1, dh_g) + dot(d_logits, rout[...], 0, 0)
    mid = midb[...]
    s2 = lax.rsqrt(jnp.mean(mid * mid, axis=-1, keepdims=True) + EPSILON)
    n2 = mid * s2
    up = d_h * gain_m
    d_mid = og[...].astype(F32) + s2 * (up - n2 * jnp.mean(up * n2, axis=-1, keepdims=True))
    gi_o[...] = d_mid
    dbb[c] = d_mid.astype(BF16)
    db_g = ag_start(dbb)
    for i in range(4):
        rs_second(2, res_g, lax.rem(z + 1 + i, 4))
    g_router = dot(d_logits, hb[c], 1, 0)
    g_mlp = jnp.sum(d_h * n2, axis=0, keepdims=True)
    for p in range(8):
        edge = slice(128 * p, 128 * p + 128)
        sm3[p, 0:8, :] = g_router[:, edge]
        sm3[p, 9:10, :] = g_mlp[:, edge]

    dkv[...] = jnp.zeros_like(dkv)
    low256 = iota((256, 128), 1) < 64

    def attend_back(ch, length):
        da = dab[ch]
        q = qr[pl.ds(2 * ch, 2)].reshape(256, 128).astype(F32)
        daf = da.astype(F32)
        dq = None
        left, right = [], []
        for h, (kk, vv) in enumerate(((ka, va), (kb, vb))):
            p = pb[h, ch, :, 0:length]
            pf = p.astype(F32)
            dp = dot(da, keys(vv, length), 1, 1)
            ds = (pf * (dp - jnp.sum(pf * dp, axis=-1, keepdims=True))).astype(BF16)
            o = dot(ds, keys(kk, length), 1, 0)
            dq = o if dq is None else dq + o
            qh = jnp.where(low256, q if h == 0 else pltpu.roll(q, 64, 1), 0.0)
            dh_ = jnp.where(low256, 0.0, daf if h == 1 else pltpu.roll(daf, 64, 1))
            left += [ds, p]
            right += [qh.astype(BF16), dh_.astype(BF16)]
        dqb[ch] = dq * 0.125
        for l, r in zip(left, right):
            dkv[0:length, :] += dot(l, r, 0, 0)

    def bwd_step(n, _):
        ch = ag_have(dbb, db_g, n)
        dab[ch] = dot(dbb[pl.ds(2 * ch, 2)].reshape(256, 1024), wob[...].reshape(1024, 128), 1, 0).astype(BF16)

        @pl.when(ch < 2)
        def _():
            attend_back(ch, 512)

        @pl.when(ch >= 2)
        def _():
            attend_back(ch, 1024)
        ag_next(dbb, db_g, n)
        return 0
    lax.fori_loop(0, 4, bwd_step, 0)
    g1.got(g_s.at[0:12])

    def fold(e, _):
        own = g_s[cross(0, e)].astype(F32)
        for i in range(3):
            own = own + g_r1[i, e].astype(F32)
        g_p[e] = own.astype(BF16)
        return 0
    lax.fori_loop(0, 4, fold, 0)
    for d in (1, 3, 2):
        g2.put(g_p.at[d], g_r2.at[d - 1], 0, (far(d), c))

    acc[...] = jnp.zeros_like(acc)

    def unrope_step(ch, _):
        for kk in range(2):
            b = 2 * ch + kk
            rows = slice(128 * kk, 128 * kk + 128)
            cs, sn = tables(b)
            wq_ = dqb[ch, rows, :]
            wk_ = dkv[pl.ds(pl.multiple_of(b * 128, 128), 128), :]
            dq = wq_ * cs - partner(wq_) * sn
            dk = wk_ * jnp.where(low64, cs, 1.0) - partner(wk_) * jnp.where(low64, sn, 0.0)
            dn = jnp.concatenate([dq, dk], axis=1)
            normed = qkvb[ch, rows, :]
            acc[1:2, 0:256] += jnp.sum(dn * normed, axis=0, keepdims=True)
            dnb[ch, rows, :] = dn * gains
        put_rows(st2, ch, row_sums(sel8, dnb[ch] * qkvb[ch]))
        return 0
    lax.fori_loop(0, 4, unrope_step, 0)
    finish2 = all_reduce(st2, stb.at[1])

    def go_step(i, _):
        cols = pl.ds(pl.multiple_of(i * 256, 256), 256)
        g = dot(dbb[:, :, cols].reshape(1024, 256), at[...].reshape(1024, 128), 0, 0)
        go_s[pl.ds(4 * i, 4)] = g.astype(BF16).reshape(4, 64, 128)
        return 0
    lax.fori_loop(0, 4, go_step, 0)

    def seq_put(src, dst, spread=True):
        g = cp.group(1, dst.at[0:15])

        def body(ds, _):
            dev = speer(ds)
            g.put(src.at[dev[0]] if spread else src.at[s], dst.at[s], 0, dev)
            return 0
        lax.fori_loop(1, 16, body, 0)
        return g
    go_r[s] = go_s[s]
    go_g = seq_put(go_s, go_r)
    g2.got(g_s.at[0:3])
    gsum[...] = (g_p[0].astype(F32) + g_r2[0].astype(F32) + g_r2[1].astype(F32)
                 + g_r2[2].astype(F32)).reshape(8, 8, 1536)
    gw_o[c] = gsum[c]
    gw_g = ctx_put(gsum, gw_o)
    mean_parts = split(finish2() * count)

    def dqkv_step(b, _):
        rows = pl.ds(lax.rem(b, 2) * 128, 128)
        ch = lax.div(b, 2)
        mean = dot(mean_parts, pick(b), 0, 0)
        d = scb[ch, rows, :] * (dnb[ch, rows, :] - qkvb[ch, rows, :] * mean)
        dqkv[ch, rows, :] = d.astype(BF16)
        return 0
    lax.fori_loop(0, 8, dqkv_step, 0)
    g = dot(dqkv[...].reshape(1024, 256), xl[...].reshape(1024, 1024), 0, 0)
    gq_s[...] = g.astype(BF16).reshape(16, 16, 1024)
    gq_r[s] = gq_s[s]
    gq_g = seq_put(gq_s, gq_r)
    g_attn = jnp.sum(g * wqb[...].reshape(256, 1024).astype(F32), axis=0, keepdims=True) / gain_a
    for p in range(8):
        sm3[p, 8:9, :] = g_attn[:, 128 * p:128 * p + 128]
        sm3[p, 10:16, :] = jnp.zeros((6, 128), F32)
    sm1[c] = sm3[c]
    m1_g = ctx_put(sm3, sm1)

    dx_g = rs_new(3)

    def dx_step(n, _):
        ch = lax.rem(z + 1 + n, 4)
        dx = dot(dqkv[ch], wqb[...].reshape(256, 1024), 1, 0)
        part[3, ch] = dx.astype(BF16).reshape(2, 128, 1024)
        rs_first(3, dx_g, ch)

        @pl.when(n > 0)
        def _():
            rs_second(3, dx_g, lax.rem(z + n, 4))
        return 0
    lax.fori_loop(0, 4, dx_step, 0)
    rs_second(3, dx_g, z)

    m1_g.got(sm1.at[0:7])
    tot = jnp.sum(sm1[...], axis=0)
    r16 = iota((16, 128), 0)
    tot = tot + jnp.where(r16 == 10, acc[1:2, 0:128], 0.0) + jnp.where(r16 == 11, acc[1:2, 128:256], 0.0)
    sm2[s] = tot
    m2_g = seq_put(sm2, sm2, False)
    gq_g.got(gq_r.at[0:15])

    def add_q(i, t):
        return t + gq_r[i].astype(F32)
    gq_t[...] = lax.fori_loop(1, 16, add_q, gq_r[0].astype(F32))
    back_g = cp.group(1, None)

    @pl.when(mine)
    def _():
        gq_o[...] = gq_t[...]

    @pl.when(jnp.logical_not(mine))
    def _():
        back_g.put(gq_t, gq_o, 0, home)
    go_g.got(go_r.at[0:15])

    def add_o(i, t):
        return t + go_r[i].astype(F32)
    gsum_o[...] = lax.fori_loop(1, 16, add_o, go_r[0].astype(F32)).reshape(8, 8, 128)
    go_o[c] = gsum_o[c]
    go2_g = ctx_put(gsum_o, go_o)
    res_o[...] = (midb[...] + rs_finish(2, res_g)).astype(BF16)
    m2_g.got(sm2.at[0:15])
    sm_o[c] = jnp.sum(sm2[...], axis=0)
    m3_g = ctx_put(sm_o, sm_o, False)

    x = hid[...].astype(F32)
    s1 = lax.rsqrt(jnp.mean(x * x, axis=-1, keepdims=True) + EPSILON)
    n1 = x * s1
    up = rs_finish(3, dx_g) * gain_a
    gi_o[...] += s1 * (up - n1 * jnp.mean(up * n1, axis=-1, keepdims=True))

    @pl.when(jnp.logical_not(mine))
    def _():
        back_g.got(gq_o)
        back_g.sent(gq_t)
    for a in range(4):
        @pl.when(not_me(aim(a)))
        def _():
            home_g.sent(wq)
    gw_g.got(gw_o.at[0:7])
    go2_g.got(go_o.at[0:7])
    m3_g.got(sm_o.at[0:7])
    for group, total in cp.drains:
        group.sent(total)


def local(hidden_in, positions, starts, routes, qkv_weight, out_weight, expert_in, expert_out,
          router, attn_gain, query_gain, key_gain, mlp_gain, out_grad):
    par1 = jnp.stack([attn_gain, mlp_gain]).astype(F32)
    par2 = jnp.concatenate([query_gain.astype(F32).reshape(8, 128), key_gain.astype(F32).reshape(8, 64),
                            jnp.ones((8, 64), F32)], axis=1)
    lane = jnp.arange(128)
    freq = ROPE_BASE ** (-(lane % 32).astype(F32) * 2.0 / 64)
    ang = positions[0].astype(F32)[:, None] * freq
    tbl = jnp.where(lane < 32, jnp.cos(ang), jnp.sin(ang))[:, :64]
    tbl = jnp.concatenate([tbl[:64], tbl[64:]], axis=1)
    wo = out_weight.reshape(8, 8, 128).transpose(1, 0, 2)
    wd = jnp.concatenate([expert_in, expert_out], axis=2).transpose(1, 0, 2)
    V = pltpu.VMEM
    scratch = dict(
        xl=V((8, 128, 1024), BF16), dyb=V((8, 128, 1024), BF16), hb=V((8, 128, 1024), BF16),
        dbb=V((8, 128, 1024), BF16), tb=V((8, 64, 128), F32), wqb=V((16, 16, 1024), BF16),
        wo1=V((8, 8, 128), BF16), wd1=V((8, 8, 1536), BF16), wob=V((16, 64, 128), BF16), wb=V((16, 64, 1536), BF16),
        qkvb=V((4, 256, 256), F32), scb=V((4, 256, 256), F32), qr=V((8, 128, 128), BF16),
        ka=V((8, 128, 128), BF16), kb=V((8, 128, 128), BF16), va=V((8, 128, 128), BF16), vb=V((8, 128, 128), BF16),
        at=V((4, 256, 128), BF16), pb=V((2, 4, 256, 1024), BF16), drawb=V((4, 256, 512), F32),
        dgub=V((4, 256, 1024), BF16), agb=V((4, 256, 512), BF16),
        part=V((4, 4, 2, 128, 1024), BF16), sibb=V((4, 4, 128, 1024), BF16), rin=V((4, 3, 128, 1024), BF16),
        st=V((16, 128), F32), stb=V((2, 8, 16, 128), F32), st2=V((16, 128), F32), gtb=V((8, 8, 128), F32),
        dgs=V((8, 8, 128), F32), dgr=V((8, 8, 128), F32), midb=V((128, 1024), F32), dab=V((4, 256, 128), BF16),
        dkv=V((1024, 128), F32), dqkv=V((4, 256, 256), BF16),
        g_s=V((16, 64, 1536), BF16), g_r1=V((3, 4, 64, 1536), BF16), g_p=V((4, 64, 1536), BF16),
        g_r2=V((3, 64, 1536), BF16), go_s=V((16, 64, 128), BF16), go_r=V((16, 64, 128), BF16),
        gq_s=V((16, 16, 1024), BF16), gq_r=V((16, 16, 1024), BF16), gq_t=V((16, 1024), F32),
        gsum=V((8, 8, 1536), F32), gsum_o=V((8, 8, 128), F32),
        sm3=V((8, 16, 128), F32), sm1=V((8, 16, 128), F32), sm2=V((16, 16, 128), F32), acc=V((8, 1024), F32),
        send=pltpu.SemaphoreType.DMA((SENDS,)), recv=pltpu.SemaphoreType.DMA((RECVS,)))
    vm = pl.BlockSpec(memory_space=pltpu.VMEM)
    outs = pl.pallas_call(
        kernel,
        out_shape=[jax.ShapeDtypeStruct(sh, dt) for sh, dt in (
            ((128, 1024), BF16), ((128, 1024), F32), ((16, 1024), F32), ((8, 8, 128), F32),
            ((8, 8, 1536), F32), ((8, 16, 128), F32))],
        in_specs=[vm] * 8 + [pl.BlockSpec(memory_space=pltpu.SMEM)] + [vm] * 2,
        out_specs=[vm] * 6,
        scratch_shapes=list(scratch.values()),
        compiler_params=pltpu.CompilerParams(collective_id=0, has_side_effects=True,
                                             vmem_limit_bytes=60 * 2**20),
        name="layer",
    )(hidden_in[0], out_grad[0], qkv_weight, wo, wd, par1, par2, tbl, starts, routes[0].T, router.T)
    res, gi, gq, go, gw, sm = outs
    gw = gw.transpose(1, 0, 2)
    rows = sm.transpose(1, 0, 2)
    return (res[None], gi[None], gq, go.transpose(1, 0, 2).reshape(8, 1024), gw[:, :, :1024],
            gw[:, :, 1024:], rows[0:8].reshape(8, 1024).T, rows[8].reshape(1024), rows[10].reshape(1024),
            rows[11, :, :64].reshape(512), rows[9].reshape(1024))


def solution(mesh):
    t = ("seq", "ctx")
    in_specs = (P("seq", "ctx", None), P("seq", "ctx"), P("seq", None), P("seq", "ctx", None),
                P(t, None), P(t, None), P(t, None, None), P(t, None, None),
                P(), P(), P(), P(), P(), P("seq", "ctx", None))
    out_specs = (P("seq", "ctx", None), P("seq", "ctx", None), P(t, None), P(t, None),
                 P(t, None, None), P(t, None, None), P(), P(), P(), P(), P())
    return jax.shard_map(local, mesh=mesh, in_specs=in_specs, out_specs=out_specs, check_vma=False)
```

```python
import jax
import jax.numpy as jnp
import numpy as np
from jax import lax
from jax.experimental import pallas as pl
from jax.experimental.pallas import tpu as pltpu
from jax.sharding import PartitionSpec as P

PIECE = 256
EPSILON = 1e-06
ROPE_BASE = 10000.0
MASKED = -1e30
F32 = jnp.float32
BF16 = jnp.bfloat16
MESH = pl.DeviceIdType.MESH
SENDS, RECVS = 36, 86


def dot(a, b, ca, cb):
    return lax.dot_general(a, b, (((ca,), (cb,)), ((), ())), preferred_element_type=F32)


def iota(shape, axis):
    return lax.broadcasted_iota(jnp.int32, shape, axis)


class Copies:
    def __init__(self, send, recv, dev):
        self.send, self.recv, self.dev = send, recv, dev
        self.drains, self.sends, self.recvs = [], 0, 0

    def group(self, count, total):
        first, mine = self.recvs, self.sends
        self.recvs += count
        self.sends += 1
        assert self.recvs <= RECVS and self.sends <= SENDS
        return Group(self, first, mine, total)


class Group:
    def __init__(self, owner, first, mine, total):
        self.owner, self.first, self.mine = owner, first, mine
        if total is not None:
            owner.drains.append((self, total))

    def make(self, src, dst, i, dev):
        return pltpu.make_async_remote_copy(
            src_ref=src, dst_ref=dst, send_sem=self.owner.send.at[self.mine],
            recv_sem=self.owner.recv.at[self.first + i], device_id=dev, device_id_type=MESH)

    def put(self, src, dst, i, dev):
        self.make(src, dst, i, dev).start()

    def got(self, dst, i=0):
        self.make(dst, dst, i, self.owner.dev).wait_recv()

    def sent(self, src):
        self.make(src, src, 0, self.owner.dev).wait_send()


def kernel(hid, og, wq, wo, wd, ag_in, mg_in, qg_in, kg_in, pos, freq, starts, rt, rout,
           res_o, gi_o, gq_o, go_o, gw_o, sm_o,
           xl, dyb, hb, dbb, tb, wqb, wo1, wd1, wof, wb,
           qkvb, scb, qr, ka, kb, va, vb, at, pb, drawb, dgub, agb,
           part, sibb, rin, st, stb, st2, gtb, dgs, dgr, midb, ao, da_s, dab, dkv, dqkv,
           g_s, g_r1, g_p, g_r2, go_s, go_r, gq_s, gq_r, gq_t, gsum, gsum_o,
           sm3, sm1, sm2, acc, send, recv):
    s, c = lax.axis_index("seq"), lax.axis_index("ctx")
    z, k = lax.div(c, 2), lax.rem(c, 2)
    y, x_ = lax.div(s, 4), lax.rem(s, 4)
    sib = (s, z * 2 + 1 - k)
    cp = Copies(send, recv, sib)
    dnb, dqb = drawb.at[:, :, 0:256], drawb.at[:, :, 256:384]

    def zdev(dz):
        return (s, lax.rem(z + dz, 4) * 2 + k)

    def cpeer(dc):
        return (s, lax.rem(c + dc, 8))

    def speer(ds):
        return (lax.rem(s + ds, 16), c)

    def near(d):
        return jnp.where(k == 0, y * 4 + lax.rem(x_ + d, 4), lax.rem(y + d, 4) * 4 + x_)

    def far(d):
        return jnp.where(k == 0, lax.rem(y + d, 4) * 4 + x_, y * 4 + lax.rem(x_ + d, 4))

    def cross(a, b):
        return jnp.where(k == 0, lax.rem(y + b, 4) * 4 + lax.rem(x_ + a, 4),
                         lax.rem(y + a, 4) * 4 + lax.rem(x_ + b, 4))

    c4, r4 = lax.div(c, 4), lax.rem(c, 4)
    tg = jnp.where(s < 8, s, jnp.where(s < 12, 2 * (s - 8) + c4, 2 * (s - 12) + c4))
    ts = jnp.where(s < 8, c, jnp.where(s < 12, 8 + r4, 12 + r4))
    mine = (tg == c) & (ts == s)

    def owner(j):
        half = lax.div(c, 2)
        odd = 4 * lax.rem(c, 2)
        os = jnp.where(j < 8, c, jnp.where(j < 12, 8 + half, 12 + half))
        oc = jnp.where(j < 8, j, jnp.where(j < 12, odd + j - 8, odd + j - 12))
        return os, oc

    home = owner(s)
    tk = lax.rem(tg, 2)
    ty, tx = lax.div(ts, 4), lax.rem(ts, 4)

    def aim(a):
        return jnp.where(tk == 0, ty * 4 + lax.rem(tx + a, 4), lax.rem(ty + a, 4) * 4 + tx), tg

    def not_me(dev):
        return jnp.logical_or(dev[0] != s, dev[1] != c)

    bar = pltpu.get_barrier_semaphore()

    for a in range(4):
        source = owner(near(a))

        @pl.when(not_me(source))
        def _(source=source):
            pl.semaphore_signal(bar, inc=1, device_id=source, device_id_type=MESH)
    for dc in range(1, 8):
        pl.semaphore_signal(bar, inc=1, device_id=cpeer(dc), device_id_type=MESH)
    for d in range(1, 4):
        pl.semaphore_signal(bar, inc=1, device_id=(near(d), c), device_id_type=MESH)
        pl.semaphore_signal(bar, inc=1, device_id=(far(d), c), device_id_type=MESH)

    gain_a = ag_in[...].astype(F32).reshape(1, 1024)
    gain_m = mg_in[...].astype(F32).reshape(1, 1024)
    gq_all = qg_in[...].astype(F32).reshape(1, 1024)
    gk_all = kg_in[...].astype(F32).reshape(1, 512)
    gain_q = gq_all[:, 0:128]
    pair = gk_all[:, 0:128]
    for b in range(1, 8):
        gain_q = jnp.where(c == b, gq_all[:, 128 * b:128 * b + 128], gain_q)
    for b in range(1, 4):
        pair = jnp.where(z == b, gk_all[:, 128 * b:128 * b + 128], pair)
    pair = jnp.where(k == 0, pair, pltpu.roll(pair, 64, 1))
    gains = jnp.concatenate([gain_q,
                             jnp.where(iota((1, 128), 1) < 64, pair, 1.0)], axis=1)
    column = jnp.transpose(jnp.broadcast_to(pos[...].astype(F32), (128, 128)))
    lane64 = iota((64, 128), 1)
    angle = jnp.where(lane64 < 64, column[:64], column[64:]) * freq[...]
    tb[c] = jnp.where(lax.rem(lane64, 64) < 32, jnp.cos(angle), jnp.sin(angle))
    x = hid[...].astype(F32)
    s1 = lax.rsqrt(jnp.mean(x * x, axis=-1, keepdims=True) + EPSILON)
    xl[c] = (x * s1 * gain_a).astype(BF16)
    dyb[c] = og[...]
    wo1[c] = wo[c]
    wd1[c] = wd[c]

    selfish = jnp.int32(0)
    for a in range(4):
        selfish = selfish + jnp.where(not_me(aim(a)), 0, 1)

    @pl.when(selfish > 0)
    def _():
        wqb[ts] = wq[...]
    pl.semaphore_wait(bar, 17 - selfish)

    def ag_start(view, total):
        g = cp.group(7, total)
        for dz in (1, 3, 2):
            g.put(view(c), view(c), dz - 1, zdev(dz))
        g.put(view(c), view(c), 3, sib)
        return g

    def gray(n):
        return jnp.where(n == 2, 3, jnp.where(n == 3, 2, n))

    def ag_pass(view, g, n):
        dz = gray(n)
        b = lax.rem(z - dz + 4, 4) * 2 + k
        g.got(view(b), dz - 1)
        g.put(view(b), view(b), 3 + dz, sib)

    def ag_have(view, g, n):
        dz = gray(n)
        ch = lax.rem(z - dz + 4, 4)
        g.got(view(ch * 2 + 1 - k), 3 + dz)
        return ch

    def ag_next(view, g, n):
        @pl.when(n < 3)
        def _():
            ag_pass(view, g, n + 1)

    def rows_of(buf):
        return lambda b: buf.at[b]

    def xy_start(view, total):
        near_g = cp.group(1, total(3))
        far_g = cp.group(1, total(12))
        for d in (1, 3, 2):
            near_g.put(view(s), view(s), 0, (near(d), c))
        for d in (1, 3, 2):
            far_g.put(view(s), view(s), 0, (far(d), c))
        return near_g, far_g

    def xy_pass(view, total, g):
        g[0].got(total(3))
        for a in (1, 3, 2):
            block = near(a)
            for d in (1, 3, 2):
                g[1].put(view(block), view(block), 0, (far(d), c))

    def out_cols(b):
        return wof.at[:, :, pl.ds(pl.multiple_of(b * 128, 128), 128)]

    def out_block(b):
        return wof.at[b, :, pl.ds(pl.multiple_of(c * 128, 128), 128)]

    def out_total(n):
        return wof.at[0:n, :, 0:128]

    def ctx_put(src, dst, own=True):
        g = cp.group(1, dst.at[0:7])
        for dc in range(1, 8):
            dev = cpeer(dc)
            g.put(src.at[dev[1]] if own else src.at[c], dst.at[c], 0, dev)
        return g

    home_g = cp.group(4, None)
    for a in (0, 1, 3, 2):
        dev = aim(a)

        @pl.when(not_me(dev))
        def _(dev=dev, a=a):
            home_g.put(wq, wqb.at[ts], a, dev)
    wo_g = ctx_put(wo, wo1)
    wd_g = ctx_put(wd, wd1)
    x_g = ag_start(rows_of(xl), xl.at[0:7])
    tb_g = ctx_put(tb, tb, False)

    wq_g = cp.group(1, wqb.at[0:12])
    for a in range(4):
        block = near(a)

        @pl.when(not_me(owner(block)))
        def _(a=a):
            home_g.got(wqb.at[0], (4 - a) % 4)
        for d in (1, 3, 2):
            wq_g.put(wqb.at[block], wqb.at[block], 0, (far(d), c))
    wo_g.got(wo1.at[0:7])
    out_block(s)[...] = wo1[...].astype(F32).reshape(64, 128).astype(BF16)
    wo_x = xy_start(out_block, out_total)
    wd_g.got(wd1.at[0:7])
    wb[s] = wd1[...].astype(F32).reshape(64, 1536).astype(BF16)
    w_x = xy_start(rows_of(wb), lambda n: wb.at[0:n])
    ag_pass(rows_of(xl), x_g, 1)
    ag_pass(rows_of(xl), x_g, 2)
    xy_pass(out_block, out_total, wo_x)
    wo_x[1].got(out_total(12))
    wo_z = ag_start(out_cols, wof.at[:, :, 0:896])
    wq_g.got(wqb.at[0:12])

    def wi_full():
        return wb[:, :, 0:1024].reshape(1024, 1024)

    def wd_full():
        return wb[:, :, 1024:1536].reshape(1024, 512)

    lane = iota((1, 256), 1)

    def halves(v):
        high = v.astype(BF16)
        return high, (v - high.astype(F32)).astype(BF16)

    def split(v):
        return jnp.concatenate(halves(v), axis=0)

    def row_sums(ones, v):
        high, low = halves(v)
        return dot(ones, high, 1, 1) + dot(ones, low, 1, 1)

    sel8 = jnp.where(iota((8, 256), 0) == 0, jnp.where(iota((8, 256), 1) < 128, 1.0, 0.0),
                     jnp.where((iota((8, 256), 0) == 1) & (iota((8, 256), 1) >= 128)
                               & (iota((8, 256), 1) < 192), 1.0, 0.0)).astype(BF16)

    def put_rows(ref, ch, rows):
        ref[pl.ds(2 * ch, 1), :] = rows[0:1, 0:128]
        ref[pl.ds(2 * ch + 1, 1), :] = rows[0:1, 128:256]
        ref[pl.ds(8 + 2 * ch, 1), :] = rows[1:2, 0:128]
        ref[pl.ds(9 + 2 * ch, 1), :] = rows[1:2, 128:256]

    def qkv_step(n, _):
        @pl.when(n == 2)
        def _():
            ag_pass(rows_of(xl), x_g, 3)
        ch = ag_have(rows_of(xl), x_g, n)
        qkv = dot(xl[pl.ds(2 * ch, 2)].reshape(256, 1024), wqb[...].reshape(256, 1024), 1, 1)
        qkvb[ch] = qkv
        put_rows(st, ch, row_sums(sel8, qkv * qkv))
        return 0
    lax.fori_loop(0, 4, qkv_step, 0)

    def all_reduce(own, slots):
        slots[c] = own[...]
        g = ctx_put(slots, slots, False)

        def finish():
            g.got(slots.at[0:7])
            return jnp.sum(slots[...], axis=0)
        return finish

    row16 = iota((16, 128), 0)
    count = jnp.where(row16 < 8, 1.0 / 1024, 1.0 / 512)
    finish = all_reduce(st, stb.at[0])
    xy_pass(rows_of(wb), lambda n: wb.at[0:n], w_x)
    tb_g.got(tb.at[0:7])
    scale_parts = split(lax.rsqrt(finish() * count + EPSILON))

    def pick(b):
        r, l = lax.rem(iota((32, 256), 0), 16), iota((32, 256), 1)
        return jnp.where(((r == b) & (l < 128)) | ((r == 8 + b) & (l >= 128) & (l < 192)), 1.0, 0.0).astype(BF16)

    even = lax.rem(lax.div(iota((128, 128), 1), 32), 2) == 0
    low64 = iota((128, 128), 1) < 64

    def tables(b):
        t = tb[b]
        r = pltpu.roll(t, 64, 1)
        low = iota((64, 128), 1) < 64
        t = jnp.concatenate([jnp.where(low, t, r), jnp.where(low, r, t)], axis=0)
        t2 = pltpu.roll(t, 32, 1)
        return jnp.where(even, t, t2), jnp.where(even, -t2, t)

    def partner(w):
        return jnp.where(even, pltpu.roll(w, 96, 1), pltpu.roll(w, 32, 1))

    def rope_step(b, _):
        rows = pl.ds(lax.rem(b, 2) * 128, 128)
        ch = lax.div(b, 2)
        scale = dot(scale_parts, pick(b), 0, 0) + jnp.where(lane >= 192, 1.0, 0.0)
        scb[ch, rows, :] = scale
        normed = qkvb[ch, rows, :] * scale
        qkvb[ch, rows, :] = normed
        w = normed * gains
        cs, sn = tables(b)
        wq_, wk_ = w[:, :128], w[:, 128:]
        qr[b] = ((wq_ * cs + partner(wq_) * sn) * 0.125).astype(BF16)
        kv = wk_ * jnp.where(low64, cs, 1.0) + partner(wk_) * jnp.where(low64, sn, 0.0)
        k0 = jnp.where(low64, kv, 0.0)
        v1 = jnp.where(low64, 0.0, kv)
        ka[b] = k0.astype(BF16)
        kb[b] = pltpu.roll(k0, 64, 1).astype(BF16)
        va[b] = pltpu.roll(v1, 64, 1).astype(BF16)
        vb[b] = v1.astype(BF16)
        return 0
    lax.fori_loop(0, 8, rope_step, 0)

    def rs_new(r):
        return cp.group(4, sibb.at[r]), cp.group(1, rin.at[r])

    def rs_first(r, g, ch):
        g[0].put(part.at[r, ch, 1 - k], sibb.at[r, ch], ch, sib)

    def rs_second(r, g, ch):
        g[0].got(sibb.at[r, ch], ch)
        part[r, ch, k] = (part[r, ch, k].astype(F32) + sibb[r, ch].astype(F32)).astype(BF16)
        dz = lax.rem(ch - z + 4, 4)

        @pl.when(dz > 0)
        def _():
            g[1].put(part.at[r, ch, k], rin.at[r, dz - 1], 0, (s, ch * 2 + k))

    def rs_finish(r, g):
        g[1].got(rin.at[r])
        total = part[r, z, k].astype(F32)
        for i in range(3):
            total = total + rin[r, i].astype(F32)
        return total

    st0, st1 = starts[0, 0], starts[0, 1]

    def limits(ch):
        row = ch * 256 + iota((256, 1), 0)
        lim = jnp.where((row >= st0) & (row < st0 + PIECE), st0 + PIECE - 1, row)
        return jnp.where((row >= st1) & (row < st1 + PIECE), st1 + PIECE - 1, lim)

    def keys(ref, length):
        return ref[0:length // 128].reshape(length, 128)

    def attend(ch, length):
        q = qr[pl.ds(2 * ch, 2)].reshape(256, 128)
        allowed = iota((256, length), 1) <= limits(ch)
        out = None
        for h, (kk, vv) in enumerate(((ka, va), (kb, vb))):
            sc = jnp.where(allowed, dot(q, keys(kk, length), 1, 1), MASKED)
            e = jnp.exp(sc - jnp.max(sc, axis=-1, keepdims=True))
            p = (e * (1.0 / jnp.sum(e, axis=-1, keepdims=True))).astype(BF16)
            pb[h, ch, :, 0:length] = p
            o = dot(p, keys(vv, length), 1, 0)
            out = o if out is None else out + o
        at[pl.ds(2 * ch, 2)] = out.astype(BF16).reshape(2, 128, 128)

    def step_chip(n):
        return lax.rem(z + jnp.where(n == 0, 2, jnp.where(n == 1, 1, jnp.where(n == 2, 3, 0))), 4)

    def heads_put(src, dst, g, b):
        @pl.when(b != c)
        def _():
            g.put(src.at[b], dst.at[c], 0, (s, b))

        @pl.when(b == c)
        def _():
            dst[c] = src[c]

    ao_g = cp.group(1, ao.at[0:7])

    def fwd_step(n, _):
        ch = step_chip(n)

        @pl.when(ch < 2)
        def _():
            attend(ch, 512)

        @pl.when(ch >= 2)
        def _():
            attend(ch, 1024)
        heads_put(at, ao, ao_g, 2 * ch + k)
        heads_put(at, ao, ao_g, 2 * ch + 1 - k)
        return 0
    lax.fori_loop(0, 4, fwd_step, 0)

    dy_g = ag_start(rows_of(dyb), dyb.at[0:7])
    for n in (1, 2, 3):
        ag_pass(out_cols, wo_z, n)

    for n in range(4):
        ag_have(out_cols, wo_z, n)
    ao_g.got(ao.at[0:7])
    wide = jnp.concatenate([ao[b] for b in range(8)], axis=1)
    mid = hid[...].astype(F32) + dot(wide, wof[...].reshape(1024, 1024), 1, 1)
    midb[...] = mid
    s2 = lax.rsqrt(jnp.mean(mid * mid, axis=-1, keepdims=True) + EPSILON)
    h_own = (mid * s2 * gain_m).astype(BF16)
    hb[c] = h_own
    logits = dot(rout[...], h_own, 1, 1)
    e8 = jnp.exp(logits - jnp.max(logits, axis=0, keepdims=True))
    gates = e8 / jnp.sum(e8, axis=0, keepdims=True)
    er = iota((8, 128), 0)
    member = jnp.zeros((8, 128), F32)
    for j in range(4):
        member = member + jnp.where(rt[j:j + 1, :] == er, 1.0, 0.0)
    gtb[c] = gates * member
    gt_g = cp.group(7, gtb.at[0:7])
    for dc in (1, 7, 2, 6, 3, 5, 4):
        gt_g.put(gtb.at[c], gtb.at[c], dc - 1, cpeer(dc))
    h_g = ag_start(rows_of(hb), hb.at[0:7])
    ag_pass(rows_of(dyb), dy_g, 1)
    w_x[1].got(wb.at[0:12])

    one_c = jnp.where(lax.rem(iota((16, 128), 0), 8) == c, 1.0, 0.0).astype(BF16)
    dh_g, res_g = rs_new(0), rs_new(1)

    def expert_step(n, _):
        ch = ag_have(rows_of(hb), h_g, n)
        gu = dot(hb[pl.ds(2 * ch, 2)].reshape(256, 1024), wi_full(), 1, 0)
        g, u = gu[:, :512], gu[:, 512:]
        sig = 1.0 / (1.0 + jnp.exp(-g))
        sw = g * sig
        act = sw * u

        for b in (2 * ch, 2 * ch + 1):
            @pl.when(b != c)
            def _(b=b):
                gt_g.got(gtb.at[0], lax.rem(c - b + 8, 8) - 1)
        gate = jnp.concatenate([dot(split(gtb[2 * ch]), one_c, 0, 0), dot(split(gtb[2 * ch + 1]), one_c, 0, 0)], axis=0)
        gate = jnp.concatenate([gate] * 4, axis=1)
        ag_have(rows_of(dyb), dy_g, n)
        draw = dot(dyb[pl.ds(2 * ch, 2)].reshape(256, 1024), wd_full(), 1, 0)
        agb[ch] = (act * gate).astype(BF16)
        rows = row_sums(jnp.ones((8, 512), BF16), act * draw)
        dgs[2 * ch] = rows[:, 0:128]
        dgs[2 * ch + 1] = rows[:, 128:256]
        d_act = draw * gate
        dgub[ch, :, 0:512] = (d_act * u * sig * (1.0 + g * (1.0 - sig))).astype(BF16)
        dgub[ch, :, 512:1024] = (d_act * sw).astype(BF16)
        dh = dot(dgub[ch], wi_full(), 1, 1)
        part[0, ch] = dh.astype(BF16).reshape(2, 128, 1024)
        rs_first(0, dh_g, ch)
        rs = dot(agb[ch], wd_full(), 1, 1)
        part[1, ch] = rs.astype(BF16).reshape(2, 128, 1024)
        rs_first(1, res_g, ch)
        ag_next(rows_of(hb), h_g, n)

        @pl.when(n < 2)
        def _():
            ag_pass(rows_of(dyb), dy_g, n + 2)
        rs_second(0, dh_g, ch)
        return 0
    lax.fori_loop(0, 4, expert_step, 0)
    dgr[c] = dgs[c]
    dg_g = ctx_put(dgs, dgr)

    def gw_step(i, _):
        cols = pl.ds(pl.multiple_of(i * 256, 256), 256)
        g = dot(dyb[:, :, cols].reshape(1024, 256), agb[...].reshape(1024, 512), 0, 0)
        g_s[pl.ds(4 * i, 4), :, 1024:1536] = g.astype(BF16).reshape(4, 64, 512)
        g = dot(hb[:, :, cols].reshape(1024, 256), dgub[...].reshape(1024, 1024), 0, 0)
        g_s[pl.ds(4 * i, 4), :, 0:1024] = g.astype(BF16).reshape(4, 64, 1024)
        return 0
    lax.fori_loop(0, 4, gw_step, 0)
    g1, g2 = cp.group(1, g_s.at[0:12]), cp.group(1, g_s.at[0:3])
    for d in (1, 3, 2):
        for e in range(4):
            g1.put(g_s.at[cross(d, e)], g_r1.at[d - 1, e], 0, (near(d), c))

    dg_g.got(dgr.at[0:7])
    dg = jnp.concatenate([dgr[e, 0:1, :] for e in range(8)], axis=0) * member
    d_logits = (gates * (dg - jnp.sum(gates * dg, axis=0, keepdims=True))).astype(BF16)
    d_h = rs_finish(0, dh_g) + dot(d_logits, rout[...], 0, 0)
    mid = midb[...]
    s2 = lax.rsqrt(jnp.mean(mid * mid, axis=-1, keepdims=True) + EPSILON)
    n2 = mid * s2
    up = d_h * gain_m
    d_mid = og[...].astype(F32) + s2 * (up - n2 * jnp.mean(up * n2, axis=-1, keepdims=True))
    gi_o[...] = d_mid
    d_branch = d_mid.astype(BF16)
    d_attn = dot(d_branch, wof[...].reshape(1024, 1024), 1, 0).astype(BF16)
    for b in range(8):
        da_s[b] = d_attn[:, 128 * b:128 * b + 128]
    da_g = cp.group(1, dab.at[0:7])
    dab[c] = da_s[c]
    for dc in (4, 3, 5, 2, 6, 1, 7):
        dev = cpeer(dc)
        da_g.put(da_s.at[dev[1]], dab.at[c], 0, dev)
    dbb[c] = d_branch
    db_g = ag_start(rows_of(dbb), dbb.at[0:7])
    for i in range(4):
        rs_second(1, res_g, lax.rem(z + 1 + i, 4))
    g_router = dot(d_logits, hb[c], 1, 0)
    g_mlp = jnp.sum(d_h * n2, axis=0, keepdims=True)
    for p in range(8):
        edge = slice(128 * p, 128 * p + 128)
        sm3[p, 0:8, :] = g_router[:, edge]
        sm3[p, 9:10, :] = g_mlp[:, edge]

    dkv[...] = jnp.zeros_like(dkv)
    low256 = iota((256, 128), 1) < 64

    def attend_back(ch, length):
        da = dab[pl.ds(2 * ch, 2)].reshape(256, 128)
        q = qr[pl.ds(2 * ch, 2)].reshape(256, 128).astype(F32)
        daf = da.astype(F32)
        dq = None
        left, right = [], []
        for h, (kk, vv) in enumerate(((ka, va), (kb, vb))):
            p = pb[h, ch, :, 0:length]
            pf = p.astype(F32)
            dp = dot(da, keys(vv, length), 1, 1)
            ds = (pf * (dp - jnp.sum(pf * dp, axis=-1, keepdims=True))).astype(BF16)
            o = dot(ds, keys(kk, length), 1, 0)
            dq = o if dq is None else dq + o
            qh = jnp.where(low256, q if h == 0 else pltpu.roll(q, 64, 1), 0.0)
            dh_ = jnp.where(low256, 0.0, daf if h == 1 else pltpu.roll(daf, 64, 1))
            left += [ds, p]
            right += [qh.astype(BF16), dh_.astype(BF16)]
        dqb[ch] = dq * 0.125
        for l, r in zip(left, right):
            dkv[0:length, :] += dot(l, r, 0, 0)

    def bwd_step(n, _):
        ch = n

        @pl.when(ch < 2)
        def _():
            attend_back(ch, 512)

        @pl.when(ch >= 2)
        def _():
            attend_back(ch, 1024)
        return 0
    da_g.got(dab.at[0:7])
    lax.fori_loop(0, 4, bwd_step, 0)
    for n in (1, 2, 3):
        ag_pass(rows_of(dbb), db_g, n)

    acc[...] = jnp.zeros_like(acc)

    def unrope_step(ch, _):
        for kk in range(2):
            b = 2 * ch + kk
            rows = slice(128 * kk, 128 * kk + 128)
            cs, sn = tables(b)
            wq_ = dqb[ch, rows, :]
            wk_ = dkv[pl.ds(pl.multiple_of(b * 128, 128), 128), :]
            dq = wq_ * cs - partner(wq_) * sn
            dk = wk_ * jnp.where(low64, cs, 1.0) - partner(wk_) * jnp.where(low64, sn, 0.0)
            dn = jnp.concatenate([dq, dk], axis=1)
            normed = qkvb[ch, rows, :]
            acc[1:2, 0:256] += jnp.sum(dn * normed, axis=0, keepdims=True)
            dnb[ch, rows, :] = dn * gains
        put_rows(st2, ch, row_sums(sel8, dnb[ch] * qkvb[ch]))
        return 0
    lax.fori_loop(0, 4, unrope_step, 0)
    finish2 = all_reduce(st2, stb.at[1])

    g1.got(g_s.at[0:12])

    def fold(e, _):
        own = g_s[cross(0, e)].astype(F32)
        for i in range(3):
            own = own + g_r1[i, e].astype(F32)
        g_p[e] = own.astype(BF16)
        return 0
    lax.fori_loop(0, 4, fold, 0)
    for d in (1, 3, 2):
        g2.put(g_p.at[d], g_r2.at[d - 1], 0, (far(d), c))

    for n in range(4):
        ag_have(rows_of(dbb), db_g, n)
    def go_step(i, _):
        cols = pl.ds(pl.multiple_of(i * 256, 256), 256)
        g = dot(dbb[:, :, cols].reshape(1024, 256), at[...].reshape(1024, 128), 0, 0)
        go_s[pl.ds(4 * i, 4)] = g.astype(BF16).reshape(4, 64, 128)
        return 0
    lax.fori_loop(0, 4, go_step, 0)

    def seq_put(src, dst, spread=True):
        g = cp.group(1, dst.at[0:15])

        def body(ds, _):
            dev = speer(ds)
            g.put(src.at[dev[0]] if spread else src.at[s], dst.at[s], 0, dev)
            return 0
        lax.fori_loop(1, 16, body, 0)
        return g
    go_r[s] = go_s[s]
    go_g = seq_put(go_s, go_r)
    mean_parts = split(finish2() * count)

    def dqkv_step(b, _):
        rows = pl.ds(lax.rem(b, 2) * 128, 128)
        ch = lax.div(b, 2)
        mean = dot(mean_parts, pick(b), 0, 0)
        d = scb[ch, rows, :] * (dnb[ch, rows, :] - qkvb[ch, rows, :] * mean)
        dqkv[ch, rows, :] = d.astype(BF16)
        return 0
    lax.fori_loop(0, 8, dqkv_step, 0)
    g = dot(dqkv[...].reshape(1024, 256), xl[...].reshape(1024, 1024), 0, 0)
    gq_s[...] = g.astype(BF16).reshape(16, 16, 1024)
    gq_r[s] = gq_s[s]
    gq_g = seq_put(gq_s, gq_r)
    g_attn = jnp.sum(g * wqb[...].reshape(256, 1024).astype(F32), axis=0, keepdims=True) / gain_a
    for p in range(8):
        sm3[p, 8:9, :] = g_attn[:, 128 * p:128 * p + 128]
        sm3[p, 10:16, :] = jnp.zeros((6, 128), F32)
    sm1[c] = sm3[c]
    m1_g = ctx_put(sm3, sm1)

    dx_g = rs_new(2)

    def dx_step(n, _):
        ch = step_chip(n)
        dx = dot(dqkv[ch], wqb[...].reshape(256, 1024), 1, 0)
        part[2, ch] = dx.astype(BF16).reshape(2, 128, 1024)
        rs_first(2, dx_g, ch)

        @pl.when(n > 0)
        def _():
            rs_second(2, dx_g, step_chip(n - 1))
        return 0
    lax.fori_loop(0, 4, dx_step, 0)
    rs_second(2, dx_g, z)
    g2.got(g_s.at[0:3])
    gsum[...] = (g_p[0].astype(F32) + g_r2[0].astype(F32) + g_r2[1].astype(F32)
                 + g_r2[2].astype(F32)).reshape(8, 8, 1536)
    gw_o[c] = gsum[c]
    gw_g = ctx_put(gsum, gw_o)

    m1_g.got(sm1.at[0:7])
    tot = jnp.sum(sm1[...], axis=0)
    r16 = iota((16, 128), 0)
    tot = tot + jnp.where(r16 == 10, acc[1:2, 0:128], 0.0) + jnp.where(r16 == 11, acc[1:2, 128:256], 0.0)
    sm2[s] = tot
    m2_g = seq_put(sm2, sm2, False)
    gq_g.got(gq_r.at[0:15])

    def add_q(i, t):
        return t + gq_r[i].astype(F32)
    gq_t[...] = lax.fori_loop(1, 16, add_q, gq_r[0].astype(F32))
    back_g = cp.group(1, None)

    @pl.when(mine)
    def _():
        gq_o[...] = gq_t[...]

    @pl.when(jnp.logical_not(mine))
    def _():
        back_g.put(gq_t, gq_o, 0, home)
    go_g.got(go_r.at[0:15])

    def add_o(i, t):
        return t + go_r[i].astype(F32)
    gsum_o[...] = lax.fori_loop(1, 16, add_o, go_r[0].astype(F32)).reshape(8, 8, 128)
    go_o[c] = gsum_o[c]
    go2_g = ctx_put(gsum_o, go_o)
    res_o[...] = (midb[...] + rs_finish(1, res_g)).astype(BF16)
    m2_g.got(sm2.at[0:15])
    sm_o[c] = jnp.sum(sm2[...], axis=0)
    m3_g = ctx_put(sm_o, sm_o, False)

    x = hid[...].astype(F32)
    s1 = lax.rsqrt(jnp.mean(x * x, axis=-1, keepdims=True) + EPSILON)
    n1 = x * s1
    up = rs_finish(2, dx_g) * gain_a
    gi_o[...] += s1 * (up - n1 * jnp.mean(up * n1, axis=-1, keepdims=True))

    @pl.when(jnp.logical_not(mine))
    def _():
        back_g.got(gq_o)
        back_g.sent(gq_t)
    for a in range(4):
        @pl.when(not_me(aim(a)))
        def _():
            home_g.sent(wq)
    gw_g.got(gw_o.at[0:7])
    go2_g.got(go_o.at[0:7])
    m3_g.got(sm_o.at[0:7])
    for group, total in cp.drains:
        group.sent(total)


def place(res, gi, gq, go, gw, sm, res_o, gi_o, gq_o, go_o, gin_o, gdn_o, gr_o, ga_o, gqg_o, gkg_o, gm_o):
    res_o[...] = res[...]
    gi_o[...] = gi[...]
    gq_o[...] = gq[...]
    for b in range(8):
        cols = slice(128 * b, 128 * b + 128)
        go_o[:, cols] = go[b]
        gin_o[:, b, :] = gw[b, :, 0:1024]
        gdn_o[:, b, :] = gw[b, :, 1024:1536]
        gr_o[:, cols] = sm[b, 0:8, :]
        ga_o[b:b + 1, :] = sm[b, 8:9, :]
        gm_o[b:b + 1, :] = sm[b, 9:10, :]
        gqg_o[b:b + 1, :] = sm[b, 10:11, :]
    for b in range(4):
        gkg_o[b:b + 1, :] = jnp.where(iota((1, 128), 1) < 64, sm[2 * b, 11:12, :],
                                      pltpu.roll(sm[2 * b + 1, 11:12, :], 64, 1))


def local(hidden_in, positions, starts, routes, qkv_weight, out_weight, expert_in, expert_out,
          router, attn_gain, query_gain, key_gain, mlp_gain, out_grad):
    lanes = np.arange(128, dtype=np.float32) % 32
    freq = (np.float32(ROPE_BASE) ** (-lanes * np.float32(2.0) / np.float32(64))).astype(np.float32)[None]
    wo = out_weight.reshape(8, 8, 128).transpose(1, 0, 2)
    wd = jnp.concatenate([expert_in, expert_out], axis=2).transpose(1, 0, 2)
    V = pltpu.VMEM
    scratch = dict(
        xl=V((8, 128, 1024), BF16), dyb=V((8, 128, 1024), BF16), hb=V((8, 128, 1024), BF16),
        dbb=V((8, 128, 1024), BF16), tb=V((8, 64, 128), F32), wqb=V((16, 16, 1024), BF16),
        wo1=V((8, 8, 128), BF16), wd1=V((8, 8, 1536), BF16), wof=V((16, 64, 1024), BF16), wb=V((16, 64, 1536), BF16),
        qkvb=V((4, 256, 256), F32), scb=V((4, 256, 256), F32), qr=V((8, 128, 128), BF16),
        ka=V((8, 128, 128), BF16), kb=V((8, 128, 128), BF16), va=V((8, 128, 128), BF16), vb=V((8, 128, 128), BF16),
        at=V((8, 128, 128), BF16), pb=V((2, 4, 256, 1024), BF16), drawb=V((4, 256, 512), F32),
        dgub=V((4, 256, 1024), BF16), agb=V((4, 256, 512), BF16),
        part=V((3, 4, 2, 128, 1024), BF16), sibb=V((3, 4, 128, 1024), BF16), rin=V((3, 3, 128, 1024), BF16),
        st=V((16, 128), F32), stb=V((2, 8, 16, 128), F32), st2=V((16, 128), F32), gtb=V((8, 8, 128), F32),
        dgs=V((8, 8, 128), F32), dgr=V((8, 8, 128), F32), midb=V((128, 1024), F32), ao=V((8, 128, 128), BF16), da_s=V((8, 128, 128), BF16), dab=V((8, 128, 128), BF16),
        dkv=V((1024, 128), F32), dqkv=V((4, 256, 256), BF16),
        g_s=V((16, 64, 1536), BF16), g_r1=V((3, 4, 64, 1536), BF16), g_p=V((4, 64, 1536), BF16),
        g_r2=V((3, 64, 1536), BF16), go_s=V((16, 64, 128), BF16), go_r=V((16, 64, 128), BF16),
        gq_s=V((16, 16, 1024), BF16), gq_r=V((16, 16, 1024), BF16), gq_t=V((16, 1024), F32),
        gsum=V((8, 8, 1536), F32), gsum_o=V((8, 8, 128), F32),
        sm3=V((8, 16, 128), F32), sm1=V((8, 16, 128), F32), sm2=V((16, 16, 128), F32), acc=V((8, 1024), F32),
        send=pltpu.SemaphoreType.DMA((SENDS,)), recv=pltpu.SemaphoreType.DMA((RECVS,)))
    vm = pl.BlockSpec(memory_space=pltpu.VMEM)
    outs = pl.pallas_call(
        kernel,
        out_shape=[jax.ShapeDtypeStruct(sh, dt) for sh, dt in (
            ((128, 1024), BF16), ((128, 1024), F32), ((16, 1024), F32), ((8, 8, 128), F32),
            ((8, 8, 1536), F32), ((8, 16, 128), F32))],
        in_specs=[vm] * 11 + [pl.BlockSpec(memory_space=pltpu.SMEM)] + [vm] * 2,
        out_specs=[vm] * 6,
        scratch_shapes=list(scratch.values()),
        compiler_params=pltpu.CompilerParams(collective_id=0, has_side_effects=True,
                                             vmem_limit_bytes=60 * 2**20),
        name="layer",
    )(hidden_in[0], out_grad[0], qkv_weight, wo, wd, attn_gain, mlp_gain, query_gain, key_gain, positions, freq, starts, routes[0].T, router.T)
    shapes = (((128, 1024), BF16), ((128, 1024), F32), ((16, 1024), F32), ((8, 1024), F32), ((8, 8, 1024), F32),
              ((8, 8, 512), F32), ((8, 1024), F32), ((8, 128), F32), ((8, 128), F32), ((4, 128), F32), ((8, 128), F32))
    res, gi, gq, go, gin, gdn, gr, ga, gqg, gkg, gm = pl.pallas_call(
        place, out_shape=[jax.ShapeDtypeStruct(sh, dt) for sh, dt in shapes],
        in_specs=[vm] * 6, out_specs=[vm] * 11, name="place",
        compiler_params=pltpu.CompilerParams(vmem_limit_bytes=60 * 2**20),
    )(*outs)
    return (res[None], gi[None], gq, go, gin, gdn, gr.T, ga.reshape(1024), gqg.reshape(1024), gkg.reshape(512),
            gm.reshape(1024))


def solution(mesh):
    t = ("seq", "ctx")
    in_specs = (P("seq", "ctx", None), P("seq", "ctx"), P("seq", None), P("seq", "ctx", None),
                P(t, None), P(t, None), P(t, None, None), P(t, None, None),
                P(), P(), P(), P(), P(), P("seq", "ctx", None))
    out_specs = (P("seq", "ctx", None), P("seq", "ctx", None), P(t, None), P(t, None),
                 P(t, None, None), P(t, None, None), P(), P(), P(), P(), P())
    return jax.shard_map(local, mesh=mesh, in_specs=in_specs, out_specs=out_specs, check_vma=False)
```

```python
import jax
import jax.numpy as jnp
import numpy as np
from jax import lax
from jax.experimental import pallas as pl
from jax.experimental.pallas import tpu as pltpu
from jax.sharding import PartitionSpec as P

PIECE = 256
EPSILON = 1e-06
ROPE_BASE = 10000.0
MASKED = -1e30
F32 = jnp.float32
BF16 = jnp.bfloat16
MESH = pl.DeviceIdType.MESH
SENDS, RECVS = 36, 86


def dot(a, b, ca, cb):
    return lax.dot_general(a, b, (((ca,), (cb,)), ((), ())), preferred_element_type=F32)


def iota(shape, axis):
    return lax.broadcasted_iota(jnp.int32, shape, axis)


class Copies:
    def __init__(self, send, recv, dev):
        self.send, self.recv, self.dev = send, recv, dev
        self.drains, self.sends, self.recvs = [], 0, 0

    def group(self, count, total):
        first, mine = self.recvs, self.sends
        self.recvs += count
        self.sends += 1
        assert self.recvs <= RECVS and self.sends <= SENDS
        return Group(self, first, mine, total)


class Group:
    def __init__(self, owner, first, mine, total):
        self.owner, self.first, self.mine = owner, first, mine
        if total is not None:
            owner.drains.append((self, total))

    def make(self, src, dst, i, dev):
        return pltpu.make_async_remote_copy(
            src_ref=src, dst_ref=dst, send_sem=self.owner.send.at[self.mine],
            recv_sem=self.owner.recv.at[self.first + i], device_id=dev, device_id_type=MESH)

    def put(self, src, dst, i, dev):
        self.make(src, dst, i, dev).start()

    def got(self, dst, i=0):
        self.make(dst, dst, i, self.owner.dev).wait_recv()

    def sent(self, src):
        self.make(src, src, 0, self.owner.dev).wait_send()


def kernel(hid, og, wq, wo, wd, ag_in, mg_in, qg_in, kg_in, pos, freq, starts, rt, rout,
           res_o, gi_o, gq_o, go_o, gw_o, sm_o,
           xl, dyb, hb, dbb, tb, wqb, wo1, wd1, wof, wb,
           qkvb, scb, qr, ka, kb, va, vb, at, pb, drawb, dgub, agb,
           part, sibb, rin, st, stb, st2, gtb, dgs, dgr, midb, ao, da_s, dab, dkv, dqkv,
           g_s, g_r1, g_p, g_r2, go_s, go_r, gq_s, gq_r, gq_t, gsum, gsum_o,
           sm3, sm1, sm2, acc, send, recv):
    s, c = lax.axis_index("seq"), lax.axis_index("ctx")
    z, k = lax.div(c, 2), lax.rem(c, 2)
    y, x_ = lax.div(s, 4), lax.rem(s, 4)
    sib = (s, z * 2 + 1 - k)
    cp = Copies(send, recv, sib)
    dnb, dqb = drawb.at[:, :, 0:256], drawb.at[:, :, 256:384]

    def zdev(dz):
        return (s, lax.rem(z + dz, 4) * 2 + k)

    def cpeer(dc):
        return (s, lax.rem(c + dc, 8))

    def speer(ds):
        return (lax.rem(s + ds, 16), c)

    def near(d):
        return jnp.where(k == 0, y * 4 + lax.rem(x_ + d, 4), lax.rem(y + d, 4) * 4 + x_)

    def far(d):
        return jnp.where(k == 0, lax.rem(y + d, 4) * 4 + x_, y * 4 + lax.rem(x_ + d, 4))

    def cross(a, b):
        return jnp.where(k == 0, lax.rem(y + b, 4) * 4 + lax.rem(x_ + a, 4),
                         lax.rem(y + a, 4) * 4 + lax.rem(x_ + b, 4))

    c4, r4 = lax.div(c, 4), lax.rem(c, 4)
    tg = jnp.where(s < 8, s, jnp.where(s < 12, 2 * (s - 8) + c4, 2 * (s - 12) + c4))
    ts = jnp.where(s < 8, c, jnp.where(s < 12, 8 + r4, 12 + r4))
    mine = (tg == c) & (ts == s)

    def owner(j):
        half = lax.div(c, 2)
        odd = 4 * lax.rem(c, 2)
        os = jnp.where(j < 8, c, jnp.where(j < 12, 8 + half, 12 + half))
        oc = jnp.where(j < 8, j, jnp.where(j < 12, odd + j - 8, odd + j - 12))
        return os, oc

    home = owner(s)
    tk = lax.rem(tg, 2)
    ty, tx = lax.div(ts, 4), lax.rem(ts, 4)

    def aim(a):
        return jnp.where(tk == 0, ty * 4 + lax.rem(tx + a, 4), lax.rem(ty + a, 4) * 4 + tx), tg

    def not_me(dev):
        return jnp.logical_or(dev[0] != s, dev[1] != c)

    bar = pltpu.get_barrier_semaphore()

    for a in range(4):
        source = owner(near(a))

        @pl.when(not_me(source))
        def _(source=source):
            pl.semaphore_signal(bar, inc=1, device_id=source, device_id_type=MESH)
    for dc in range(1, 8):
        pl.semaphore_signal(bar, inc=1, device_id=cpeer(dc), device_id_type=MESH)
    for d in range(1, 4):
        pl.semaphore_signal(bar, inc=1, device_id=(near(d), c), device_id_type=MESH)
        pl.semaphore_signal(bar, inc=1, device_id=(far(d), c), device_id_type=MESH)

    gain_a = ag_in[...].astype(F32).reshape(1, 1024)
    gain_m = mg_in[...].astype(F32).reshape(1, 1024)
    gq_all = qg_in[...].astype(F32).reshape(1, 1024)
    gk_all = kg_in[...].astype(F32).reshape(1, 512)
    gain_q = gq_all[:, 0:128]
    pair = gk_all[:, 0:128]
    for b in range(1, 8):
        gain_q = jnp.where(c == b, gq_all[:, 128 * b:128 * b + 128], gain_q)
    for b in range(1, 4):
        pair = jnp.where(z == b, gk_all[:, 128 * b:128 * b + 128], pair)
    pair = jnp.where(k == 0, pair, pltpu.roll(pair, 64, 1))
    gains = jnp.concatenate([gain_q,
                             jnp.where(iota((1, 128), 1) < 64, pair, 1.0)], axis=1)
    column = jnp.transpose(jnp.broadcast_to(pos[...].astype(F32), (128, 128)))
    lane64 = iota((64, 128), 1)
    angle = jnp.where(lane64 < 64, column[:64], column[64:]) * freq[...]
    tb[c] = jnp.where(lax.rem(lane64, 64) < 32, jnp.cos(angle), jnp.sin(angle))
    x = hid[...].astype(F32)
    s1 = lax.rsqrt(jnp.mean(x * x, axis=-1, keepdims=True) + EPSILON)
    xl[c] = (x * s1 * gain_a).astype(BF16)
    dyb[c] = og[...]
    wo1[c] = wo[c]
    wd1[c] = wd[c]

    selfish = jnp.int32(0)
    for a in range(4):
        selfish = selfish + jnp.where(not_me(aim(a)), 0, 1)

    @pl.when(selfish > 0)
    def _():
        wqb[ts] = wq[...]
    pl.semaphore_wait(bar, 17 - selfish)

    def ag_start(view, total):
        g = cp.group(7, total)
        for dz in (1, 3):
            g.put(view(c), view(c), dz - 1, zdev(dz))
        g.put(view(c), view(c), 3, sib)
        return g

    def gray(n):
        return jnp.where(n == 2, 3, jnp.where(n == 3, 2, n))

    def ag_pass(view, g, n):
        dz = (0, 1, 3, 2)[n]
        block = view(lax.rem(z - dz + 4, 4) * 2 + k)
        g.got(block, dz - 1)
        if n < 3:
            size = block.shape[0] // 2
            half = block.at[pl.ds(size * (n - 1), size)]
            g.put(half, half, 1, zdev(dz))
        g.put(block, block, 3 + dz, sib)

    def ag_have(view, g, n):
        dz = gray(n)
        ch = lax.rem(z - dz + 4, 4)
        g.got(view(ch * 2 + 1 - k), 3 + dz)
        return ch

    def rows_of(buf):
        return lambda b: buf.at[b]

    def xy_start(view, total):
        near_g = cp.group(1, total(3))
        far_g = cp.group(1, total(12))
        for d in (1, 3, 2):
            near_g.put(view(s), view(s), 0, (near(d), c))
        for d in (1, 3, 2):
            far_g.put(view(s), view(s), 0, (far(d), c))
        return near_g, far_g

    def xy_pass(view, total, g):
        g[0].got(total(3))
        for a in (1, 3, 2):
            block = near(a)
            for d in (1, 3, 2):
                g[1].put(view(block), view(block), 0, (far(d), c))

    def out_cols(b):
        return wof.at[:, :, pl.ds(pl.multiple_of(b * 128, 128), 128)]

    def out_block(b):
        return wof.at[b, :, pl.ds(pl.multiple_of(c * 128, 128), 128)]

    def out_total(n):
        return wof.at[0:n, :, 0:128]

    def ctx_put(src, dst, own=True):
        g = cp.group(1, dst.at[0:7])
        for dc in range(1, 8):
            dev = cpeer(dc)
            g.put(src.at[dev[1]] if own else src.at[c], dst.at[c], 0, dev)
        return g

    home_g = cp.group(4, None)
    for a in (0, 1, 3, 2):
        dev = aim(a)

        @pl.when(not_me(dev))
        def _(dev=dev, a=a):
            home_g.put(wq, wqb.at[ts], a, dev)
    wo_g = ctx_put(wo, wo1)
    wd_g = ctx_put(wd, wd1)
    x_g = ag_start(rows_of(xl), xl.at[0:7])
    tb_g = ctx_put(tb, tb, False)

    wq_g = cp.group(1, wqb.at[0:12])
    for a in range(4):
        block = near(a)

        @pl.when(not_me(owner(block)))
        def _(a=a):
            home_g.got(wqb.at[0], (4 - a) % 4)
        for d in (1, 3, 2):
            wq_g.put(wqb.at[block], wqb.at[block], 0, (far(d), c))
    wo_g.got(wo1.at[0:7])
    out_block(s)[...] = wo1[...].astype(F32).reshape(64, 128).astype(BF16)
    wo_x = xy_start(out_block, out_total)
    wd_g.got(wd1.at[0:7])
    wb[s] = wd1[...].astype(F32).reshape(64, 1536).astype(BF16)
    w_x = xy_start(rows_of(wb), lambda n: wb.at[0:n])
    ag_pass(rows_of(xl), x_g, 1)
    ag_pass(rows_of(xl), x_g, 2)
    xy_pass(out_block, out_total, wo_x)
    wo_x[1].got(out_total(12))
    wo_z = ag_start(out_cols, wof.at[:, :, 0:896])
    wq_g.got(wqb.at[0:12])

    def wi_full():
        return wb[:, :, 0:1024].reshape(1024, 1024)

    def wd_full():
        return wb[:, :, 1024:1536].reshape(1024, 512)

    lane = iota((1, 256), 1)

    def halves(v):
        high = v.astype(BF16)
        return high, (v - high.astype(F32)).astype(BF16)

    def split(v):
        return jnp.concatenate(halves(v), axis=0)

    def row_sums(ones, v):
        high, low = halves(v)
        return dot(ones, high, 1, 1) + dot(ones, low, 1, 1)

    sel8 = jnp.where(iota((8, 256), 0) == 0, jnp.where(iota((8, 256), 1) < 128, 1.0, 0.0),
                     jnp.where((iota((8, 256), 0) == 1) & (iota((8, 256), 1) >= 128)
                               & (iota((8, 256), 1) < 192), 1.0, 0.0)).astype(BF16)

    def put_rows(ref, ch, rows):
        ref[pl.ds(2 * ch, 1), :] = rows[0:1, 0:128]
        ref[pl.ds(2 * ch + 1, 1), :] = rows[0:1, 128:256]
        ref[pl.ds(8 + 2 * ch, 1), :] = rows[1:2, 0:128]
        ref[pl.ds(9 + 2 * ch, 1), :] = rows[1:2, 128:256]

    def qkv_step(n, _):
        @pl.when(n == 2)
        def _():
            ag_pass(rows_of(xl), x_g, 3)
        ch = ag_have(rows_of(xl), x_g, n)
        qkv = dot(xl[pl.ds(2 * ch, 2)].reshape(256, 1024), wqb[...].reshape(256, 1024), 1, 1)
        qkvb[ch] = qkv
        put_rows(st, ch, row_sums(sel8, qkv * qkv))
        return 0
    lax.fori_loop(0, 4, qkv_step, 0)

    def all_reduce(own, slots):
        slots[c] = own[...]
        g = ctx_put(slots, slots, False)

        def finish():
            g.got(slots.at[0:7])
            return jnp.sum(slots[...], axis=0)
        return finish

    row16 = iota((16, 128), 0)
    count = jnp.where(row16 < 8, 1.0 / 1024, 1.0 / 512)
    finish = all_reduce(st, stb.at[0])
    dy_g = ag_start(rows_of(dyb), dyb.at[0:7])
    xy_pass(rows_of(wb), lambda n: wb.at[0:n], w_x)
    tb_g.got(tb.at[0:7])
    scale_parts = split(lax.rsqrt(finish() * count + EPSILON))

    def pick(b):
        r, l = lax.rem(iota((32, 256), 0), 16), iota((32, 256), 1)
        return jnp.where(((r == b) & (l < 128)) | ((r == 8 + b) & (l >= 128) & (l < 192)), 1.0, 0.0).astype(BF16)

    even = lax.rem(lax.div(iota((128, 128), 1), 32), 2) == 0
    low64 = iota((128, 128), 1) < 64

    def tables(b):
        t = tb[b]
        r = pltpu.roll(t, 64, 1)
        low = iota((64, 128), 1) < 64
        t = jnp.concatenate([jnp.where(low, t, r), jnp.where(low, r, t)], axis=0)
        t2 = pltpu.roll(t, 32, 1)
        return jnp.where(even, t, t2), jnp.where(even, -t2, t)

    def partner(w):
        return jnp.where(even, pltpu.roll(w, 96, 1), pltpu.roll(w, 32, 1))

    def rope_step(b, _):
        rows = pl.ds(lax.rem(b, 2) * 128, 128)
        ch = lax.div(b, 2)
        scale = dot(scale_parts, pick(b), 0, 0) + jnp.where(lane >= 192, 1.0, 0.0)
        scb[ch, rows, :] = scale
        normed = qkvb[ch, rows, :] * scale
        qkvb[ch, rows, :] = normed
        w = normed * gains
        cs, sn = tables(b)
        wq_, wk_ = w[:, :128], w[:, 128:]
        qr[b] = ((wq_ * cs + partner(wq_) * sn) * 0.125).astype(BF16)
        kv = wk_ * jnp.where(low64, cs, 1.0) + partner(wk_) * jnp.where(low64, sn, 0.0)
        k0 = jnp.where(low64, kv, 0.0)
        v1 = jnp.where(low64, 0.0, kv)
        ka[b] = k0.astype(BF16)
        kb[b] = pltpu.roll(k0, 64, 1).astype(BF16)
        va[b] = pltpu.roll(v1, 64, 1).astype(BF16)
        vb[b] = v1.astype(BF16)
        return 0
    lax.fori_loop(0, 8, rope_step, 0)
    ag_pass(out_cols, wo_z, 1)
    ag_pass(out_cols, wo_z, 2)

    def rs_new(r):
        return cp.group(4, sibb.at[r]), cp.group(1, rin.at[r])

    def rs_first(r, g, ch):
        g[0].put(part.at[r, ch, 1 - k], sibb.at[r, ch], ch, sib)

    def rs_second(r, g, ch):
        g[0].got(sibb.at[r, ch], ch)
        part[r, ch, k] = (part[r, ch, k].astype(F32) + sibb[r, ch].astype(F32)).astype(BF16)
        dz = lax.rem(ch - z + 4, 4)

        @pl.when(dz > 0)
        def _():
            g[1].put(part.at[r, ch, k], rin.at[r, dz - 1], 0, (s, ch * 2 + k))

    def rs_finish(r, g):
        g[1].got(rin.at[r])
        total = part[r, z, k].astype(F32)
        for i in range(3):
            total = total + rin[r, i].astype(F32)
        return total

    st0, st1 = starts[0, 0], starts[0, 1]

    def limits(ch):
        row = ch * 256 + iota((256, 1), 0)
        lim = jnp.where((row >= st0) & (row < st0 + PIECE), st0 + PIECE - 1, row)
        return jnp.where((row >= st1) & (row < st1 + PIECE), st1 + PIECE - 1, lim)

    def keys(ref, length):
        return ref[0:length // 128].reshape(length, 128)

    def attend(ch, length):
        q = qr[pl.ds(2 * ch, 2)].reshape(256, 128)
        allowed = iota((256, length), 1) <= limits(ch)
        out = None
        for h, (kk, vv) in enumerate(((ka, va), (kb, vb))):
            sc = jnp.where(allowed, dot(q, keys(kk, length), 1, 1), MASKED)
            e = jnp.exp(sc - jnp.max(sc, axis=-1, keepdims=True))
            p = (e * (1.0 / jnp.sum(e, axis=-1, keepdims=True))).astype(BF16)
            pb[h, ch, :, 0:length] = p
            o = dot(p, keys(vv, length), 1, 0)
            out = o if out is None else out + o
        at[pl.ds(2 * ch, 2)] = out.astype(BF16).reshape(2, 128, 128)

    def step_chip(n):
        return lax.rem(z + jnp.where(n == 0, 2, jnp.where(n == 1, 1, jnp.where(n == 2, 3, 0))), 4)

    def heads_put(src, dst, g, b):
        @pl.when(b != c)
        def _():
            g.put(src.at[b], dst.at[c], 0, (s, b))

        @pl.when(b == c)
        def _():
            dst[c] = src[c]

    ao_g = cp.group(1, ao.at[0:7])

    def fwd_step(n, _):
        ch = step_chip(n)

        @pl.when(ch < 2)
        def _():
            attend(ch, 512)

        @pl.when(ch >= 2)
        def _():
            attend(ch, 1024)
        heads_put(at, ao, ao_g, 2 * ch + k)

        @pl.when(n == 2)
        def _():
            ag_pass(out_cols, wo_z, 3)
            ag_pass(rows_of(dyb), dy_g, 1)
            ag_pass(rows_of(dyb), dy_g, 2)
        heads_put(at, ao, ao_g, 2 * ch + 1 - k)
        return 0
    lax.fori_loop(0, 4, fwd_step, 0)

    ag_pass(rows_of(dyb), dy_g, 3)

    for n in range(4):
        ag_have(out_cols, wo_z, n)
    ao_g.got(ao.at[0:7])
    wide = jnp.concatenate([ao[b] for b in range(8)], axis=1)
    mid = hid[...].astype(F32) + dot(wide, wof[...].reshape(1024, 1024), 1, 1)
    midb[...] = mid
    s2 = lax.rsqrt(jnp.mean(mid * mid, axis=-1, keepdims=True) + EPSILON)
    h_own = (mid * s2 * gain_m).astype(BF16)
    hb[c] = h_own
    logits = dot(rout[...], h_own, 1, 1)
    e8 = jnp.exp(logits - jnp.max(logits, axis=0, keepdims=True))
    gates = e8 / jnp.sum(e8, axis=0, keepdims=True)
    er = iota((8, 128), 0)
    member = jnp.zeros((8, 128), F32)
    for j in range(4):
        member = member + jnp.where(rt[j:j + 1, :] == er, 1.0, 0.0)
    gtb[c] = gates * member
    gt_g = cp.group(7, gtb.at[0:7])
    for dc in (1, 7, 2, 6, 3, 5, 4):
        gt_g.put(gtb.at[c], gtb.at[c], dc - 1, cpeer(dc))
    h_g = ag_start(rows_of(hb), hb.at[0:7])
    w_x[1].got(wb.at[0:12])

    def draw_step(n, _):
        ch = ag_have(rows_of(dyb), dy_g, n)
        drawb[ch] = dot(dyb[pl.ds(2 * ch, 2)].reshape(256, 1024), wd_full(), 1, 0)
        return 0
    lax.fori_loop(0, 4, draw_step, 0)

    one_c = jnp.where(lax.rem(iota((16, 128), 0), 8) == c, 1.0, 0.0).astype(BF16)
    dh_g, res_g = rs_new(0), rs_new(1)

    def expert_step(n, _):
        ch = ag_have(rows_of(hb), h_g, n)
        gu = dot(hb[pl.ds(2 * ch, 2)].reshape(256, 1024), wi_full(), 1, 0)
        g, u = gu[:, :512], gu[:, 512:]
        sig = 1.0 / (1.0 + jnp.exp(-g))
        sw = g * sig
        act = sw * u

        for b in (2 * ch, 2 * ch + 1):
            @pl.when(b != c)
            def _(b=b):
                gt_g.got(gtb.at[0], lax.rem(c - b + 8, 8) - 1)
        gate = jnp.concatenate([dot(split(gtb[2 * ch]), one_c, 0, 0), dot(split(gtb[2 * ch + 1]), one_c, 0, 0)], axis=0)
        gate = jnp.concatenate([gate] * 4, axis=1)
        draw = drawb[ch]
        agb[ch] = (act * gate).astype(BF16)
        rows = row_sums(jnp.ones((8, 512), BF16), act * draw)
        dgs[2 * ch] = rows[:, 0:128]
        dgs[2 * ch + 1] = rows[:, 128:256]
        d_act = draw * gate
        dgub[ch, :, 0:512] = (d_act * u * sig * (1.0 + g * (1.0 - sig))).astype(BF16)
        dgub[ch, :, 512:1024] = (d_act * sw).astype(BF16)
        dh = dot(dgub[ch], wi_full(), 1, 1)
        part[0, ch] = dh.astype(BF16).reshape(2, 128, 1024)
        rs_first(0, dh_g, ch)
        rs = dot(agb[ch], wd_full(), 1, 1)
        part[1, ch] = rs.astype(BF16).reshape(2, 128, 1024)
        rs_first(1, res_g, ch)

        @pl.when(n == 0)
        def _():
            ag_pass(rows_of(hb), h_g, 1)
            ag_pass(rows_of(hb), h_g, 2)

        @pl.when(n == 2)
        def _():
            ag_pass(rows_of(hb), h_g, 3)
        rs_second(0, dh_g, ch)
        return 0
    lax.fori_loop(0, 4, expert_step, 0)
    dgr[c] = dgs[c]
    dg_g = ctx_put(dgs, dgr)

    def gw_step(i, _):
        cols = pl.ds(pl.multiple_of(i * 256, 256), 256)
        g = dot(dyb[:, :, cols].reshape(1024, 256), agb[...].reshape(1024, 512), 0, 0)
        g_s[pl.ds(4 * i, 4), :, 1024:1536] = g.astype(BF16).reshape(4, 64, 512)
        g = dot(hb[:, :, cols].reshape(1024, 256), dgub[...].reshape(1024, 1024), 0, 0)
        g_s[pl.ds(4 * i, 4), :, 0:1024] = g.astype(BF16).reshape(4, 64, 1024)
        return 0
    lax.fori_loop(0, 4, gw_step, 0)
    g1, g2 = cp.group(1, g_s.at[0:12]), cp.group(1, g_s.at[0:3])
    for d in (1, 3, 2):
        for e in range(4):
            g1.put(g_s.at[cross(d, e)], g_r1.at[d - 1, e], 0, (near(d), c))

    for i in range(4):
        rs_second(1, res_g, lax.rem(z + 1 + i, 4))

    dg_g.got(dgr.at[0:7])
    dg = jnp.concatenate([dgr[e, 0:1, :] for e in range(8)], axis=0) * member
    d_logits = (gates * (dg - jnp.sum(gates * dg, axis=0, keepdims=True))).astype(BF16)
    d_h = rs_finish(0, dh_g) + dot(d_logits, rout[...], 0, 0)
    mid = midb[...]
    s2 = lax.rsqrt(jnp.mean(mid * mid, axis=-1, keepdims=True) + EPSILON)
    n2 = mid * s2
    up = d_h * gain_m
    d_mid = og[...].astype(F32) + s2 * (up - n2 * jnp.mean(up * n2, axis=-1, keepdims=True))
    gi_o[...] = d_mid
    d_branch = d_mid.astype(BF16)
    d_attn = dot(d_branch, wof[...].reshape(1024, 1024), 1, 0).astype(BF16)
    for b in range(8):
        da_s[b] = d_attn[:, 128 * b:128 * b + 128]
    da_g = cp.group(1, dab.at[0:7])
    dab[c] = da_s[c]
    for dc in (4, 3, 5, 2, 6, 1, 7):
        dev = cpeer(dc)
        da_g.put(da_s.at[dev[1]], dab.at[c], 0, dev)
    dbb[c] = d_branch
    db_g = ag_start(rows_of(dbb), dbb.at[0:7])
    g_router = dot(d_logits, hb[c], 1, 0)
    g_mlp = jnp.sum(d_h * n2, axis=0, keepdims=True)
    for p in range(8):
        edge = slice(128 * p, 128 * p + 128)
        sm3[p, 0:8, :] = g_router[:, edge]
        sm3[p, 9:10, :] = g_mlp[:, edge]

    dkv[...] = jnp.zeros_like(dkv)
    low256 = iota((256, 128), 1) < 64

    def attend_back(ch, length):
        da = dab[pl.ds(2 * ch, 2)].reshape(256, 128)
        q = qr[pl.ds(2 * ch, 2)].reshape(256, 128).astype(F32)
        daf = da.astype(F32)
        dq = None
        left, right = [], []
        for h, (kk, vv) in enumerate(((ka, va), (kb, vb))):
            p = pb[h, ch, :, 0:length]
            pf = p.astype(F32)
            dp = dot(da, keys(vv, length), 1, 1)
            ds = (pf * (dp - jnp.sum(pf * dp, axis=-1, keepdims=True))).astype(BF16)
            o = dot(ds, keys(kk, length), 1, 0)
            dq = o if dq is None else dq + o
            qh = jnp.where(low256, q if h == 0 else pltpu.roll(q, 64, 1), 0.0)
            dh_ = jnp.where(low256, 0.0, daf if h == 1 else pltpu.roll(daf, 64, 1))
            left += [ds, p]
            right += [qh.astype(BF16), dh_.astype(BF16)]
        dqb[ch] = dq * 0.125
        for l, r in zip(left, right):
            dkv[0:length, :] += dot(l, r, 0, 0)

    def bwd_step(n, _):
        ch = n

        @pl.when(n == 2)
        def _():
            ag_pass(rows_of(dbb), db_g, 1)
            ag_pass(rows_of(dbb), db_g, 2)

        @pl.when(ch < 2)
        def _():
            attend_back(ch, 512)

        @pl.when(ch >= 2)
        def _():
            attend_back(ch, 1024)
        return 0
    da_g.got(dab.at[0:7])
    lax.fori_loop(0, 4, bwd_step, 0)

    acc[...] = jnp.zeros_like(acc)

    def unrope_step(ch, _):
        for kk in range(2):
            b = 2 * ch + kk
            rows = slice(128 * kk, 128 * kk + 128)
            cs, sn = tables(b)
            wq_ = dqb[ch, rows, :]
            wk_ = dkv[pl.ds(pl.multiple_of(b * 128, 128), 128), :]
            dq = wq_ * cs - partner(wq_) * sn
            dk = wk_ * jnp.where(low64, cs, 1.0) - partner(wk_) * jnp.where(low64, sn, 0.0)
            dn = jnp.concatenate([dq, dk], axis=1)
            normed = qkvb[ch, rows, :]
            acc[1:2, 0:256] += jnp.sum(dn * normed, axis=0, keepdims=True)
            dnb[ch, rows, :] = dn * gains
        put_rows(st2, ch, row_sums(sel8, dnb[ch] * qkvb[ch]))
        return 0
    lax.fori_loop(0, 4, unrope_step, 0)
    finish2 = all_reduce(st2, stb.at[1])

    g1.got(g_s.at[0:12])

    def fold(e, _):
        own = g_s[cross(0, e)].astype(F32)
        for i in range(3):
            own = own + g_r1[i, e].astype(F32)
        g_p[e] = own.astype(BF16)
        return 0
    lax.fori_loop(0, 4, fold, 0)
    for d in (1, 3, 2):
        g2.put(g_p.at[d], g_r2.at[d - 1], 0, (far(d), c))

    ag_pass(rows_of(dbb), db_g, 3)
    for n in range(4):
        ag_have(rows_of(dbb), db_g, n)
    def go_step(i, _):
        cols = pl.ds(pl.multiple_of(i * 256, 256), 256)
        g = dot(dbb[:, :, cols].reshape(1024, 256), at[...].reshape(1024, 128), 0, 0)
        go_s[pl.ds(4 * i, 4)] = g.astype(BF16).reshape(4, 64, 128)
        return 0
    lax.fori_loop(0, 4, go_step, 0)

    def seq_put(src, dst, spread=True):
        g = cp.group(1, dst.at[0:15])

        def body(ds, _):
            dev = speer(ds)
            g.put(src.at[dev[0]] if spread else src.at[s], dst.at[s], 0, dev)
            return 0
        lax.fori_loop(1, 16, body, 0)
        return g
    go_r[s] = go_s[s]
    go_g = seq_put(go_s, go_r)
    mean_parts = split(finish2() * count)

    def dqkv_step(b, _):
        rows = pl.ds(lax.rem(b, 2) * 128, 128)
        ch = lax.div(b, 2)
        mean = dot(mean_parts, pick(b), 0, 0)
        d = scb[ch, rows, :] * (dnb[ch, rows, :] - qkvb[ch, rows, :] * mean)
        dqkv[ch, rows, :] = d.astype(BF16)
        return 0
    lax.fori_loop(0, 8, dqkv_step, 0)
    g = dot(dqkv[...].reshape(1024, 256), xl[...].reshape(1024, 1024), 0, 0)
    gq_s[...] = g.astype(BF16).reshape(16, 16, 1024)
    gq_r[s] = gq_s[s]
    gq_g = seq_put(gq_s, gq_r)
    g_attn = jnp.sum(g * wqb[...].reshape(256, 1024).astype(F32), axis=0, keepdims=True) / gain_a
    for p in range(8):
        sm3[p, 8:9, :] = g_attn[:, 128 * p:128 * p + 128]
        sm3[p, 10:16, :] = jnp.zeros((6, 128), F32)
    sm1[c] = sm3[c]
    m1_g = ctx_put(sm3, sm1)

    dx_g = rs_new(2)

    def dx_step(n, _):
        ch = step_chip(n)
        dx = dot(dqkv[ch], wqb[...].reshape(256, 1024), 1, 0)
        part[2, ch] = dx.astype(BF16).reshape(2, 128, 1024)
        rs_first(2, dx_g, ch)

        @pl.when(n > 0)
        def _():
            rs_second(2, dx_g, step_chip(n - 1))
        return 0
    lax.fori_loop(0, 4, dx_step, 0)
    rs_second(2, dx_g, z)
    g2.got(g_s.at[0:3])
    gsum[...] = (g_p[0].astype(F32) + g_r2[0].astype(F32) + g_r2[1].astype(F32)
                 + g_r2[2].astype(F32)).reshape(8, 8, 1536)
    gw_o[c] = gsum[c]
    gw_g = ctx_put(gsum, gw_o)

    m1_g.got(sm1.at[0:7])
    tot = jnp.sum(sm1[...], axis=0)
    r16 = iota((16, 128), 0)
    tot = tot + jnp.where(r16 == 10, acc[1:2, 0:128], 0.0) + jnp.where(r16 == 11, acc[1:2, 128:256], 0.0)
    sm2[s] = tot
    m2_g = seq_put(sm2, sm2, False)
    gq_g.got(gq_r.at[0:15])

    def add_q(i, t):
        return t + gq_r[i].astype(F32)
    gq_t[...] = lax.fori_loop(1, 16, add_q, gq_r[0].astype(F32))
    back_g = cp.group(1, None)

    @pl.when(mine)
    def _():
        gq_o[...] = gq_t[...]

    @pl.when(jnp.logical_not(mine))
    def _():
        back_g.put(gq_t, gq_o, 0, home)
    go_g.got(go_r.at[0:15])

    def add_o(i, t):
        return t + go_r[i].astype(F32)
    gsum_o[...] = lax.fori_loop(1, 16, add_o, go_r[0].astype(F32)).reshape(8, 8, 128)
    go_o[c] = gsum_o[c]
    go2_g = ctx_put(gsum_o, go_o)
    res_o[...] = (midb[...] + rs_finish(1, res_g)).astype(BF16)
    m2_g.got(sm2.at[0:15])
    sm_o[c] = jnp.sum(sm2[...], axis=0)
    m3_g = ctx_put(sm_o, sm_o, False)

    x = hid[...].astype(F32)
    s1 = lax.rsqrt(jnp.mean(x * x, axis=-1, keepdims=True) + EPSILON)
    n1 = x * s1
    up = rs_finish(2, dx_g) * gain_a
    gi_o[...] += s1 * (up - n1 * jnp.mean(up * n1, axis=-1, keepdims=True))

    @pl.when(jnp.logical_not(mine))
    def _():
        back_g.got(gq_o)
        back_g.sent(gq_t)
    for a in range(4):
        @pl.when(not_me(aim(a)))
        def _():
            home_g.sent(wq)
    gw_g.got(gw_o.at[0:7])
    go2_g.got(go_o.at[0:7])
    m3_g.got(sm_o.at[0:7])
    for group, total in cp.drains:
        group.sent(total)


def place(res, gi, gq, go, gw, sm, res_o, gi_o, gq_o, go_o, gin_o, gdn_o, gr_o, ga_o, gqg_o, gkg_o, gm_o):
    res_o[...] = res[...]
    gi_o[...] = gi[...]
    gq_o[...] = gq[...]
    for b in range(8):
        cols = slice(128 * b, 128 * b + 128)
        go_o[:, cols] = go[b]
        gin_o[:, b, :] = gw[b, :, 0:1024]
        gdn_o[:, b, :] = gw[b, :, 1024:1536]
        gr_o[:, cols] = sm[b, 0:8, :]
        ga_o[b:b + 1, :] = sm[b, 8:9, :]
        gm_o[b:b + 1, :] = sm[b, 9:10, :]
        gqg_o[b:b + 1, :] = sm[b, 10:11, :]
    for b in range(4):
        gkg_o[b:b + 1, :] = jnp.where(iota((1, 128), 1) < 64, sm[2 * b, 11:12, :],
                                      pltpu.roll(sm[2 * b + 1, 11:12, :], 64, 1))


def local(hidden_in, positions, starts, routes, qkv_weight, out_weight, expert_in, expert_out,
          router, attn_gain, query_gain, key_gain, mlp_gain, out_grad):
    lanes = np.arange(128, dtype=np.float32) % 32
    freq = (np.float32(ROPE_BASE) ** (-lanes * np.float32(2.0) / np.float32(64))).astype(np.float32)[None]
    wo = out_weight.reshape(8, 8, 128).transpose(1, 0, 2)
    wd = jnp.concatenate([expert_in, expert_out], axis=2).transpose(1, 0, 2)
    V = pltpu.VMEM
    scratch = dict(
        xl=V((8, 128, 1024), BF16), dyb=V((8, 128, 1024), BF16), hb=V((8, 128, 1024), BF16),
        dbb=V((8, 128, 1024), BF16), tb=V((8, 64, 128), F32), wqb=V((16, 16, 1024), BF16),
        wo1=V((8, 8, 128), BF16), wd1=V((8, 8, 1536), BF16), wof=V((16, 64, 1024), BF16), wb=V((16, 64, 1536), BF16),
        qkvb=V((4, 256, 256), F32), scb=V((4, 256, 256), F32), qr=V((8, 128, 128), BF16),
        ka=V((8, 128, 128), BF16), kb=V((8, 128, 128), BF16), va=V((8, 128, 128), BF16), vb=V((8, 128, 128), BF16),
        at=V((8, 128, 128), BF16), pb=V((2, 4, 256, 1024), BF16), drawb=V((4, 256, 512), F32),
        dgub=V((4, 256, 1024), BF16), agb=V((4, 256, 512), BF16),
        part=V((3, 4, 2, 128, 1024), BF16), sibb=V((3, 4, 128, 1024), BF16), rin=V((3, 3, 128, 1024), BF16),
        st=V((16, 128), F32), stb=V((2, 8, 16, 128), F32), st2=V((16, 128), F32), gtb=V((8, 8, 128), F32),
        dgs=V((8, 8, 128), F32), dgr=V((8, 8, 128), F32), midb=V((128, 1024), F32), ao=V((8, 128, 128), BF16), da_s=V((8, 128, 128), BF16), dab=V((8, 128, 128), BF16),
        dkv=V((1024, 128), F32), dqkv=V((4, 256, 256), BF16),
        g_s=V((16, 64, 1536), BF16), g_r1=V((3, 4, 64, 1536), BF16), g_p=V((4, 64, 1536), BF16),
        g_r2=V((3, 64, 1536), BF16), go_s=V((16, 64, 128), BF16), go_r=V((16, 64, 128), BF16),
        gq_s=V((16, 16, 1024), BF16), gq_r=V((16, 16, 1024), BF16), gq_t=V((16, 1024), F32),
        gsum=V((8, 8, 1536), F32), gsum_o=V((8, 8, 128), F32),
        sm3=V((8, 16, 128), F32), sm1=V((8, 16, 128), F32), sm2=V((16, 16, 128), F32), acc=V((8, 1024), F32),
        send=pltpu.SemaphoreType.DMA((SENDS,)), recv=pltpu.SemaphoreType.DMA((RECVS,)))
    vm = pl.BlockSpec(memory_space=pltpu.VMEM)
    outs = pl.pallas_call(
        kernel,
        out_shape=[jax.ShapeDtypeStruct(sh, dt) for sh, dt in (
            ((128, 1024), BF16), ((128, 1024), F32), ((16, 1024), F32), ((8, 8, 128), F32),
            ((8, 8, 1536), F32), ((8, 16, 128), F32))],
        in_specs=[vm] * 11 + [pl.BlockSpec(memory_space=pltpu.SMEM)] + [vm] * 2,
        out_specs=[vm] * 6,
        scratch_shapes=list(scratch.values()),
        compiler_params=pltpu.CompilerParams(collective_id=0, has_side_effects=True,
                                             vmem_limit_bytes=60 * 2**20),
        name="layer",
    )(hidden_in[0], out_grad[0], qkv_weight, wo, wd, attn_gain, mlp_gain, query_gain, key_gain, positions, freq, starts, routes[0].T, router.T)
    shapes = (((128, 1024), BF16), ((128, 1024), F32), ((16, 1024), F32), ((8, 1024), F32), ((8, 8, 1024), F32),
              ((8, 8, 512), F32), ((8, 1024), F32), ((8, 128), F32), ((8, 128), F32), ((4, 128), F32), ((8, 128), F32))
    res, gi, gq, go, gin, gdn, gr, ga, gqg, gkg, gm = pl.pallas_call(
        place, out_shape=[jax.ShapeDtypeStruct(sh, dt) for sh, dt in shapes],
        in_specs=[vm] * 6, out_specs=[vm] * 11, name="place",
        compiler_params=pltpu.CompilerParams(vmem_limit_bytes=60 * 2**20),
    )(*outs)
    return (res[None], gi[None], gq, go, gin, gdn, gr.T, ga.reshape(1024), gqg.reshape(1024), gkg.reshape(512),
            gm.reshape(1024))


def solution(mesh):
    t = ("seq", "ctx")
    in_specs = (P("seq", "ctx", None), P("seq", "ctx"), P("seq", None), P("seq", "ctx", None),
                P(t, None), P(t, None), P(t, None, None), P(t, None, None),
                P(), P(), P(), P(), P(), P("seq", "ctx", None))
    out_specs = (P("seq", "ctx", None), P("seq", "ctx", None), P(t, None), P(t, None),
                 P(t, None, None), P(t, None, None), P(), P(), P(), P(), P())
    return jax.shard_map(local, mesh=mesh, in_specs=in_specs, out_specs=out_specs, check_vma=False)
```

```python
import jax
import jax.numpy as jnp
import numpy as np
from jax import lax
from jax.experimental import pallas as pl
from jax.experimental.pallas import tpu as pltpu
from jax.sharding import PartitionSpec as P

PIECE = 256
EPSILON = 1e-06
ROPE_BASE = 10000.0
MASKED = -1e30
F32 = jnp.float32
BF16 = jnp.bfloat16
MESH = pl.DeviceIdType.MESH
SENDS, RECVS = 36, 86


def dot(a, b, ca, cb):
    return lax.dot_general(a, b, (((ca,), (cb,)), ((), ())), preferred_element_type=F32)


def iota(shape, axis):
    return lax.broadcasted_iota(jnp.int32, shape, axis)


class Copies:
    def __init__(self, send, recv, dev):
        self.send, self.recv, self.dev = send, recv, dev
        self.drains, self.sends, self.recvs = [], 0, 0

    def group(self, count, total):
        first, mine = self.recvs, self.sends
        self.recvs += count
        self.sends += 1
        assert self.recvs <= RECVS and self.sends <= SENDS
        return Group(self, first, mine, total)


class Group:
    def __init__(self, owner, first, mine, total):
        self.owner, self.first, self.mine = owner, first, mine
        if total is not None:
            owner.drains.append((self, total))

    def make(self, src, dst, i, dev):
        return pltpu.make_async_remote_copy(
            src_ref=src, dst_ref=dst, send_sem=self.owner.send.at[self.mine],
            recv_sem=self.owner.recv.at[self.first + i], device_id=dev, device_id_type=MESH)

    def put(self, src, dst, i, dev):
        self.make(src, dst, i, dev).start()

    def got(self, dst, i=0):
        self.make(dst, dst, i, self.owner.dev).wait_recv()

    def sent(self, src):
        self.make(src, src, 0, self.owner.dev).wait_send()


def kernel(hid, og, wq, wo, wd, ag_in, mg_in, qg_in, kg_in, pos, freq, starts, rt, rout,
           res_o, gi_o, gq_o, go_o, gw_o, sm_o,
           xl, dyb, hb, dbb, tb, wqb, wo1, wd1, wof, wb,
           qkvb, scb, qr, ka, kb, va, vb, at, pb, drawb, dgub, agb,
           part, sibb, rin, st, stb, st2, gtb, dgs, dgr, midb, ao, da_s, dab, dkv, dqkv,
           g_s, g_r1, g_p, g_r2, go_s, go_r, gq_s, gq_r, gq_t, gsum, gsum_o,
           sm3, sm1, sm2, acc, send, recv):
    s, c = lax.axis_index("seq"), lax.axis_index("ctx")
    z, k = lax.div(c, 2), lax.rem(c, 2)
    y, x_ = lax.div(s, 4), lax.rem(s, 4)
    sib = (s, z * 2 + 1 - k)
    cp = Copies(send, recv, sib)
    dnb, dqb = drawb.at[:, :, 0:256], drawb.at[:, :, 256:384]

    def zdev(dz):
        return (s, lax.rem(z + dz, 4) * 2 + k)

    def cpeer(dc):
        return (s, lax.rem(c + dc, 8))

    def speer(ds):
        return (lax.rem(s + ds, 16), c)

    def near(d):
        return jnp.where(k == 0, y * 4 + lax.rem(x_ + d, 4), lax.rem(y + d, 4) * 4 + x_)

    def far(d):
        return jnp.where(k == 0, lax.rem(y + d, 4) * 4 + x_, y * 4 + lax.rem(x_ + d, 4))

    def cross(a, b):
        return jnp.where(k == 0, lax.rem(y + b, 4) * 4 + lax.rem(x_ + a, 4),
                         lax.rem(y + a, 4) * 4 + lax.rem(x_ + b, 4))

    c4, r4 = lax.div(c, 4), lax.rem(c, 4)
    tg = jnp.where(s < 8, s, jnp.where(s < 12, 2 * (s - 8) + c4, 2 * (s - 12) + c4))
    ts = jnp.where(s < 8, c, jnp.where(s < 12, 8 + r4, 12 + r4))
    mine = (tg == c) & (ts == s)

    def owner(j):
        half = lax.div(c, 2)
        odd = 4 * lax.rem(c, 2)
        os = jnp.where(j < 8, c, jnp.where(j < 12, 8 + half, 12 + half))
        oc = jnp.where(j < 8, j, jnp.where(j < 12, odd + j - 8, odd + j - 12))
        return os, oc

    home = owner(s)
    tk = lax.rem(tg, 2)
    ty, tx = lax.div(ts, 4), lax.rem(ts, 4)

    def aim(a):
        return jnp.where(tk == 0, ty * 4 + lax.rem(tx + a, 4), lax.rem(ty + a, 4) * 4 + tx), tg

    def not_me(dev):
        return jnp.logical_or(dev[0] != s, dev[1] != c)

    bar = pltpu.get_barrier_semaphore()

    for a in range(4):
        source = owner(near(a))

        @pl.when(not_me(source))
        def _(source=source):
            pl.semaphore_signal(bar, inc=1, device_id=source, device_id_type=MESH)
    for dc in range(1, 8):
        pl.semaphore_signal(bar, inc=1, device_id=cpeer(dc), device_id_type=MESH)
    for d in range(1, 4):
        pl.semaphore_signal(bar, inc=1, device_id=(near(d), c), device_id_type=MESH)
        pl.semaphore_signal(bar, inc=1, device_id=(far(d), c), device_id_type=MESH)

    gain_a = ag_in[...].astype(F32).reshape(1, 1024)
    gain_m = mg_in[...].astype(F32).reshape(1, 1024)
    gq_all = qg_in[...].astype(F32).reshape(1, 1024)
    gk_all = kg_in[...].astype(F32).reshape(1, 512)
    gain_q = gq_all[:, 0:128]
    pair = gk_all[:, 0:128]
    for b in range(1, 8):
        gain_q = jnp.where(c == b, gq_all[:, 128 * b:128 * b + 128], gain_q)
    for b in range(1, 4):
        pair = jnp.where(z == b, gk_all[:, 128 * b:128 * b + 128], pair)
    pair = jnp.where(k == 0, pair, pltpu.roll(pair, 64, 1))
    gains = jnp.concatenate([gain_q,
                             jnp.where(iota((1, 128), 1) < 64, pair, 1.0)], axis=1)
    column = jnp.transpose(jnp.broadcast_to(pos[...].astype(F32), (128, 128)))
    lane64 = iota((64, 128), 1)
    angle = jnp.where(lane64 < 64, column[:64], column[64:]) * freq[...]
    tb[c] = jnp.where(lax.rem(lane64, 64) < 32, jnp.cos(angle), jnp.sin(angle))
    x = hid[...].astype(F32)
    s1 = lax.rsqrt(jnp.mean(x * x, axis=-1, keepdims=True) + EPSILON)
    xl[c] = (x * s1 * gain_a).astype(BF16)
    dyb[c] = og[...]
    wo1[c] = wo[...]
    wd1[c] = wd[c]

    selfish = jnp.int32(0)
    for a in range(4):
        selfish = selfish + jnp.where(not_me(aim(a)), 0, 1)

    @pl.when(selfish > 0)
    def _():
        wqb[ts] = wq[...]
    pl.semaphore_wait(bar, 17 - selfish)

    def ag_start(view, total):
        g = cp.group(7, total)
        for dz in (1, 3):
            g.put(view(c), view(c), dz - 1, zdev(dz))
        g.put(view(c), view(c), 3, sib)
        return g

    def gray(n):
        return jnp.where(n == 2, 3, jnp.where(n == 3, 2, n))

    def ag_pass(view, g, n):
        dz = (0, 1, 3, 2)[n]
        block = view(lax.rem(z - dz + 4, 4) * 2 + k)
        g.got(block, dz - 1)
        if n < 3:
            size = block.shape[0] // 2
            half = block.at[pl.ds(size * (n - 1), size)]
            g.put(half, half, 1, zdev(dz))
        g.put(block, block, 3 + dz, sib)

    def ag_have(view, g, n):
        dz = gray(n)
        ch = lax.rem(z - dz + 4, 4)
        g.got(view(ch * 2 + 1 - k), 3 + dz)
        return ch

    def rows_of(buf):
        return lambda b: buf.at[b]

    def xy_start(view, total):
        near_g = cp.group(1, total(3))
        far_g = cp.group(1, total(12))
        for d in (1, 3, 2):
            near_g.put(view(s), view(s), 0, (near(d), c))
        for d in (1, 3, 2):
            far_g.put(view(s), view(s), 0, (far(d), c))
        return near_g, far_g

    def xy_pass(view, total, g):
        g[0].got(total(3))
        for a in (1, 3, 2):
            block = near(a)
            for d in (1, 3, 2):
                g[1].put(view(block), view(block), 0, (far(d), c))

    mine_rows = pl.ds(pl.multiple_of(32 * k, 32), 32)
    other_rows = pl.ds(pl.multiple_of(32 - 32 * k, 32), 32)

    def out_block(b):
        return wof.at[b, mine_rows]

    def out_total(n):
        return wof.at[0:n, 0:32]

    def ctx_put(src, dst, own=True):
        g = cp.group(1, dst.at[0:7])
        for dc in range(1, 8):
            dev = cpeer(dc)
            g.put(src.at[dev[1]] if own else src.at[c], dst.at[c], 0, dev)
        return g

    home_g = cp.group(4, None)
    for a in (0, 1, 3, 2):
        dev = aim(a)

        @pl.when(not_me(dev))
        def _(dev=dev, a=a):
            home_g.put(wq, wqb.at[ts], a, dev)
    wo_g = cp.group(1, wo1.at[0:7])
    for dc in range(1, 8):
        wo_g.put(wo, wo1.at[c], 0, cpeer(dc))
    wd_g = ctx_put(wd, wd1)
    x_g = ag_start(rows_of(xl), xl.at[0:7])
    tb_g = ctx_put(tb, tb, False)

    wq_g = cp.group(1, wqb.at[0:12])
    for a in range(4):
        block = near(a)

        @pl.when(not_me(owner(block)))
        def _(a=a):
            home_g.got(wqb.at[0], (4 - a) % 4)
        for d in (1, 3, 2):
            wq_g.put(wqb.at[block], wqb.at[block], 0, (far(d), c))
    wo_g.got(wo1.at[0:7])
    rows64 = wo1[...].astype(F32).reshape(64, 1024)
    wof[s, mine_rows] = jnp.where(k == 0, rows64[0:32], rows64[32:64]).astype(BF16)
    wo_x = xy_start(out_block, out_total)
    wd_g.got(wd1.at[0:7])
    wb[s] = wd1[...].astype(F32).reshape(64, 1536).astype(BF16)
    xy_pass(out_block, out_total, wo_x)
    w_x = xy_start(rows_of(wb), lambda n: wb.at[0:n])
    ag_pass(rows_of(xl), x_g, 1)
    ag_pass(rows_of(xl), x_g, 2)
    wq_g.got(wqb.at[0:12])

    def wi_full():
        return wb[:, :, 0:1024].reshape(1024, 1024)

    def wd_full():
        return wb[:, :, 1024:1536].reshape(1024, 512)

    lane = iota((1, 256), 1)

    def halves(v):
        high = v.astype(BF16)
        return high, (v - high.astype(F32)).astype(BF16)

    def split(v):
        return jnp.concatenate(halves(v), axis=0)

    def row_sums(ones, v):
        high, low = halves(v)
        return dot(ones, high, 1, 1) + dot(ones, low, 1, 1)

    sel8 = jnp.where(iota((8, 256), 0) == 0, jnp.where(iota((8, 256), 1) < 128, 1.0, 0.0),
                     jnp.where((iota((8, 256), 0) == 1) & (iota((8, 256), 1) >= 128)
                               & (iota((8, 256), 1) < 192), 1.0, 0.0)).astype(BF16)

    def put_rows(ref, ch, rows):
        ref[pl.ds(2 * ch, 1), :] = rows[0:1, 0:128]
        ref[pl.ds(2 * ch + 1, 1), :] = rows[0:1, 128:256]
        ref[pl.ds(8 + 2 * ch, 1), :] = rows[1:2, 0:128]
        ref[pl.ds(9 + 2 * ch, 1), :] = rows[1:2, 128:256]

    def qkv_step(n, _):
        @pl.when(n == 2)
        def _():
            ag_pass(rows_of(xl), x_g, 3)
        ch = ag_have(rows_of(xl), x_g, n)
        qkv = dot(xl[pl.ds(2 * ch, 2)].reshape(256, 1024), wqb[...].reshape(256, 1024), 1, 1)
        qkvb[ch] = qkv
        put_rows(st, ch, row_sums(sel8, qkv * qkv))
        return 0
    lax.fori_loop(0, 4, qkv_step, 0)

    def all_reduce(own, slots):
        slots[c] = own[...]
        g = ctx_put(slots, slots, False)

        def finish():
            g.got(slots.at[0:7])
            return jnp.sum(slots[...], axis=0)
        return finish

    row16 = iota((16, 128), 0)
    count = jnp.where(row16 < 8, 1.0 / 1024, 1.0 / 512)
    finish = all_reduce(st, stb.at[0])
    dy_g = ag_start(rows_of(dyb), dyb.at[0:7])
    xy_pass(rows_of(wb), lambda n: wb.at[0:n], w_x)
    tb_g.got(tb.at[0:7])
    scale_parts = split(lax.rsqrt(finish() * count + EPSILON))

    def pick(b):
        r, l = lax.rem(iota((32, 256), 0), 16), iota((32, 256), 1)
        return jnp.where(((r == b) & (l < 128)) | ((r == 8 + b) & (l >= 128) & (l < 192)), 1.0, 0.0).astype(BF16)

    even = lax.rem(lax.div(iota((128, 128), 1), 32), 2) == 0
    low64 = iota((128, 128), 1) < 64

    def tables(b):
        t = tb[b]
        r = pltpu.roll(t, 64, 1)
        low = iota((64, 128), 1) < 64
        t = jnp.concatenate([jnp.where(low, t, r), jnp.where(low, r, t)], axis=0)
        t2 = pltpu.roll(t, 32, 1)
        return jnp.where(even, t, t2), jnp.where(even, -t2, t)

    def partner(w):
        return jnp.where(even, pltpu.roll(w, 96, 1), pltpu.roll(w, 32, 1))

    def rope_step(b, _):
        rows = pl.ds(lax.rem(b, 2) * 128, 128)
        ch = lax.div(b, 2)
        scale = dot(scale_parts, pick(b), 0, 0) + jnp.where(lane >= 192, 1.0, 0.0)
        scb[ch, rows, :] = scale
        normed = qkvb[ch, rows, :] * scale
        qkvb[ch, rows, :] = normed
        w = normed * gains
        cs, sn = tables(b)
        wq_, wk_ = w[:, :128], w[:, 128:]
        qr[b] = ((wq_ * cs + partner(wq_) * sn) * 0.125).astype(BF16)
        kv = wk_ * jnp.where(low64, cs, 1.0) + partner(wk_) * jnp.where(low64, sn, 0.0)
        k0 = jnp.where(low64, kv, 0.0)
        v1 = jnp.where(low64, 0.0, kv)
        ka[b] = k0.astype(BF16)
        kb[b] = pltpu.roll(k0, 64, 1).astype(BF16)
        va[b] = pltpu.roll(v1, 64, 1).astype(BF16)
        vb[b] = v1.astype(BF16)
        return 0
    lax.fori_loop(0, 8, rope_step, 0)
    wo_x[1].got(out_total(12))
    wo_s = cp.group(1, wof.at[:, 0:32])
    wo_s.put(wof.at[:, mine_rows], wof.at[:, mine_rows], 0, sib)

    def rs_new(r):
        return cp.group(4, sibb.at[r]), cp.group(1, rin.at[r])

    def rs_first(r, g, ch):
        g[0].put(part.at[r, ch, 1 - k], sibb.at[r, ch], ch, sib)

    def rs_second(r, g, ch):
        g[0].got(sibb.at[r, ch], ch)
        part[r, ch, k] = (part[r, ch, k].astype(F32) + sibb[r, ch].astype(F32)).astype(BF16)
        dz = lax.rem(ch - z + 4, 4)

        @pl.when(dz > 0)
        def _():
            g[1].put(part.at[r, ch, k], rin.at[r, dz - 1], 0, (s, ch * 2 + k))

    def rs_finish(r, g):
        g[1].got(rin.at[r])
        total = part[r, z, k].astype(F32)
        for i in range(3):
            total = total + rin[r, i].astype(F32)
        return total

    st0, st1 = starts[0, 0], starts[0, 1]

    def limits(ch):
        row = ch * 256 + iota((256, 1), 0)
        lim = jnp.where((row >= st0) & (row < st0 + PIECE), st0 + PIECE - 1, row)
        return jnp.where((row >= st1) & (row < st1 + PIECE), st1 + PIECE - 1, lim)

    def keys(ref, length):
        return ref[0:length // 128].reshape(length, 128)

    def attend(ch, length):
        q = qr[pl.ds(2 * ch, 2)].reshape(256, 128)
        allowed = iota((256, length), 1) <= limits(ch)
        out = None
        for h, (kk, vv) in enumerate(((ka, va), (kb, vb))):
            sc = jnp.where(allowed, dot(q, keys(kk, length), 1, 1), MASKED)
            e = jnp.exp(sc - jnp.max(sc, axis=-1, keepdims=True))
            p = (e * (1.0 / jnp.sum(e, axis=-1, keepdims=True))).astype(BF16)
            pb[h, ch, :, 0:length] = p
            o = dot(p, keys(vv, length), 1, 0)
            out = o if out is None else out + o
        at[pl.ds(2 * ch, 2)] = out.astype(BF16).reshape(2, 128, 128)

    def step_chip(n):
        return lax.rem(z + jnp.where(n == 0, 2, jnp.where(n == 1, 1, jnp.where(n == 2, 3, 0))), 4)

    def heads_put(src, dst, g, b):
        @pl.when(b != c)
        def _():
            g.put(src.at[b], dst.at[c], 0, (s, b))

        @pl.when(b == c)
        def _():
            dst[c] = src[c]

    ao_g = cp.group(1, ao.at[0:7])

    def fwd_step(n, _):
        ch = step_chip(n)

        @pl.when(ch < 2)
        def _():
            attend(ch, 512)

        @pl.when(ch >= 2)
        def _():
            attend(ch, 1024)
        heads_put(at, ao, ao_g, 2 * ch + k)

        @pl.when(n == 2)
        def _():
            ag_pass(rows_of(dyb), dy_g, 1)
            ag_pass(rows_of(dyb), dy_g, 2)
        heads_put(at, ao, ao_g, 2 * ch + 1 - k)
        return 0
    lax.fori_loop(0, 4, fwd_step, 0)

    ag_pass(rows_of(dyb), dy_g, 3)

    wo_s.got(wof.at[:, other_rows])
    ao_g.got(ao.at[0:7])
    wide = jnp.concatenate([ao[b] for b in range(8)], axis=1)
    mid = hid[...].astype(F32) + dot(wide, wof[...].reshape(1024, 1024), 1, 1)
    midb[...] = mid
    s2 = lax.rsqrt(jnp.mean(mid * mid, axis=-1, keepdims=True) + EPSILON)
    h_own = (mid * s2 * gain_m).astype(BF16)
    hb[c] = h_own
    logits = dot(rout[...], h_own, 1, 1)
    e8 = jnp.exp(logits - jnp.max(logits, axis=0, keepdims=True))
    gates = e8 / jnp.sum(e8, axis=0, keepdims=True)
    er = iota((8, 128), 0)
    member = jnp.zeros((8, 128), F32)
    for j in range(4):
        member = member + jnp.where(rt[j:j + 1, :] == er, 1.0, 0.0)
    gtb[c] = gates * member
    gt_g = cp.group(7, gtb.at[0:7])
    for dc in (1, 7, 2, 6, 3, 5, 4):
        gt_g.put(gtb.at[c], gtb.at[c], dc - 1, cpeer(dc))
    h_g = ag_start(rows_of(hb), hb.at[0:7])
    w_x[1].got(wb.at[0:12])

    def draw_step(n, _):
        ch = ag_have(rows_of(dyb), dy_g, n)
        drawb[ch] = dot(dyb[pl.ds(2 * ch, 2)].reshape(256, 1024), wd_full(), 1, 0)
        return 0
    lax.fori_loop(0, 4, draw_step, 0)

    one_c = jnp.where(lax.rem(iota((16, 128), 0), 8) == c, 1.0, 0.0).astype(BF16)
    dh_g, res_g = rs_new(0), rs_new(1)

    def expert_step(n, _):
        ch = ag_have(rows_of(hb), h_g, n)
        gu = dot(hb[pl.ds(2 * ch, 2)].reshape(256, 1024), wi_full(), 1, 0)
        g, u = gu[:, :512], gu[:, 512:]
        sig = 1.0 / (1.0 + jnp.exp(-g))
        sw = g * sig
        act = sw * u

        for b in (2 * ch, 2 * ch + 1):
            @pl.when(b != c)
            def _(b=b):
                gt_g.got(gtb.at[0], lax.rem(c - b + 8, 8) - 1)
        gate = jnp.concatenate([dot(split(gtb[2 * ch]), one_c, 0, 0), dot(split(gtb[2 * ch + 1]), one_c, 0, 0)], axis=0)
        gate = jnp.concatenate([gate] * 4, axis=1)
        draw = drawb[ch]
        agb[ch] = (act * gate).astype(BF16)
        rows = row_sums(jnp.ones((8, 512), BF16), act * draw)
        dgs[2 * ch] = rows[:, 0:128]
        dgs[2 * ch + 1] = rows[:, 128:256]
        d_act = draw * gate
        dgub[ch, :, 0:512] = (d_act * u * sig * (1.0 + g * (1.0 - sig))).astype(BF16)
        dgub[ch, :, 512:1024] = (d_act * sw).astype(BF16)
        dh = dot(dgub[ch], wi_full(), 1, 1)
        part[0, ch] = dh.astype(BF16).reshape(2, 128, 1024)
        rs_first(0, dh_g, ch)
        rs = dot(agb[ch], wd_full(), 1, 1)
        part[1, ch] = rs.astype(BF16).reshape(2, 128, 1024)
        rs_first(1, res_g, ch)

        @pl.when(n == 0)
        def _():
            ag_pass(rows_of(hb), h_g, 1)
            ag_pass(rows_of(hb), h_g, 2)

        @pl.when(n == 2)
        def _():
            ag_pass(rows_of(hb), h_g, 3)
        rs_second(0, dh_g, ch)
        return 0
    lax.fori_loop(0, 4, expert_step, 0)
    dgr[c] = dgs[c]
    dg_g = ctx_put(dgs, dgr)

    def gw_step(i, _):
        cols = pl.ds(pl.multiple_of(i * 256, 256), 256)
        g = dot(dyb[:, :, cols].reshape(1024, 256), agb[...].reshape(1024, 512), 0, 0)
        g_s[pl.ds(4 * i, 4), :, 1024:1536] = g.astype(BF16).reshape(4, 64, 512)
        g = dot(hb[:, :, cols].reshape(1024, 256), dgub[...].reshape(1024, 1024), 0, 0)
        g_s[pl.ds(4 * i, 4), :, 0:1024] = g.astype(BF16).reshape(4, 64, 1024)
        return 0
    lax.fori_loop(0, 4, gw_step, 0)
    g1, g2 = cp.group(1, g_s.at[0:12]), cp.group(1, g_s.at[0:3])
    for d in (1, 3, 2):
        for e in range(4):
            g1.put(g_s.at[cross(d, e)], g_r1.at[d - 1, e], 0, (near(d), c))

    for i in range(4):
        rs_second(1, res_g, lax.rem(z + 1 + i, 4))

    dg_g.got(dgr.at[0:7])
    dg = jnp.concatenate([dgr[e, 0:1, :] for e in range(8)], axis=0) * member
    d_logits = (gates * (dg - jnp.sum(gates * dg, axis=0, keepdims=True))).astype(BF16)
    d_h = rs_finish(0, dh_g) + dot(d_logits, rout[...], 0, 0)
    mid = midb[...]
    s2 = lax.rsqrt(jnp.mean(mid * mid, axis=-1, keepdims=True) + EPSILON)
    n2 = mid * s2
    up = d_h * gain_m
    d_mid = og[...].astype(F32) + s2 * (up - n2 * jnp.mean(up * n2, axis=-1, keepdims=True))
    gi_o[...] = d_mid
    d_branch = d_mid.astype(BF16)
    d_attn = dot(d_branch, wof[...].reshape(1024, 1024), 1, 0).astype(BF16)
    for b in range(8):
        da_s[b] = d_attn[:, 128 * b:128 * b + 128]
    da_g = cp.group(1, dab.at[0:7])
    dab[c] = da_s[c]
    for dc in (4, 3, 5, 2, 6, 1, 7):
        dev = cpeer(dc)
        da_g.put(da_s.at[dev[1]], dab.at[c], 0, dev)
    dbb[c] = d_branch
    db_g = ag_start(rows_of(dbb), dbb.at[0:7])
    g_router = dot(d_logits, hb[c], 1, 0)
    g_mlp = jnp.sum(d_h * n2, axis=0, keepdims=True)
    for p in range(8):
        edge = slice(128 * p, 128 * p + 128)
        sm3[p, 0:8, :] = g_router[:, edge]
        sm3[p, 9:10, :] = g_mlp[:, edge]

    dkv[...] = jnp.zeros_like(dkv)
    low256 = iota((256, 128), 1) < 64

    def attend_back(ch, length):
        da = dab[pl.ds(2 * ch, 2)].reshape(256, 128)
        q = qr[pl.ds(2 * ch, 2)].reshape(256, 128).astype(F32)
        daf = da.astype(F32)
        dq = None
        left, right = [], []
        for h, (kk, vv) in enumerate(((ka, va), (kb, vb))):
            p = pb[h, ch, :, 0:length]
            pf = p.astype(F32)
            dp = dot(da, keys(vv, length), 1, 1)
            ds = (pf * (dp - jnp.sum(pf * dp, axis=-1, keepdims=True))).astype(BF16)
            o = dot(ds, keys(kk, length), 1, 0)
            dq = o if dq is None else dq + o
            qh = jnp.where(low256, q if h == 0 else pltpu.roll(q, 64, 1), 0.0)
            dh_ = jnp.where(low256, 0.0, daf if h == 1 else pltpu.roll(daf, 64, 1))
            left += [ds, p]
            right += [qh.astype(BF16), dh_.astype(BF16)]
        dqb[ch] = dq * 0.125
        for l, r in zip(left, right):
            dkv[0:length, :] += dot(l, r, 0, 0)

    def bwd_step(n, _):
        ch = n

        @pl.when(n == 2)
        def _():
            ag_pass(rows_of(dbb), db_g, 1)
            ag_pass(rows_of(dbb), db_g, 2)

        @pl.when(ch < 2)
        def _():
            attend_back(ch, 512)

        @pl.when(ch >= 2)
        def _():
            attend_back(ch, 1024)
        return 0
    da_g.got(dab.at[0:7])
    lax.fori_loop(0, 4, bwd_step, 0)

    acc[...] = jnp.zeros_like(acc)

    def unrope_step(ch, _):
        for kk in range(2):
            b = 2 * ch + kk
            rows = slice(128 * kk, 128 * kk + 128)
            cs, sn = tables(b)
            wq_ = dqb[ch, rows, :]
            wk_ = dkv[pl.ds(pl.multiple_of(b * 128, 128), 128), :]
            dq = wq_ * cs - partner(wq_) * sn
            dk = wk_ * jnp.where(low64, cs, 1.0) - partner(wk_) * jnp.where(low64, sn, 0.0)
            dn = jnp.concatenate([dq, dk], axis=1)
            normed = qkvb[ch, rows, :]
            acc[1:2, 0:256] += jnp.sum(dn * normed, axis=0, keepdims=True)
            dnb[ch, rows, :] = dn * gains
        put_rows(st2, ch, row_sums(sel8, dnb[ch] * qkvb[ch]))
        return 0
    lax.fori_loop(0, 4, unrope_step, 0)
    finish2 = all_reduce(st2, stb.at[1])

    g1.got(g_s.at[0:12])

    def fold(e, _):
        own = g_s[cross(0, e)].astype(F32)
        for i in range(3):
            own = own + g_r1[i, e].astype(F32)
        g_p[e] = own.astype(BF16)
        return 0
    lax.fori_loop(0, 4, fold, 0)
    for d in (1, 3, 2):
        g2.put(g_p.at[d], g_r2.at[d - 1], 0, (far(d), c))

    ag_pass(rows_of(dbb), db_g, 3)
    for n in range(4):
        ag_have(rows_of(dbb), db_g, n)
    def go_step(i, _):
        cols = pl.ds(pl.multiple_of(i * 256, 256), 256)
        g = dot(dbb[:, :, cols].reshape(1024, 256), at[...].reshape(1024, 128), 0, 0)
        go_s[pl.ds(4 * i, 4)] = g.astype(BF16).reshape(4, 64, 128)
        return 0
    lax.fori_loop(0, 4, go_step, 0)

    def seq_put(src, dst, spread=True):
        g = cp.group(1, dst.at[0:15])

        def body(ds, _):
            dev = speer(ds)
            g.put(src.at[dev[0]] if spread else src.at[s], dst.at[s], 0, dev)
            return 0
        lax.fori_loop(1, 16, body, 0)
        return g
    go_r[s] = go_s[s]
    go_g = seq_put(go_s, go_r)
    mean_parts = split(finish2() * count)

    def dqkv_step(b, _):
        rows = pl.ds(lax.rem(b, 2) * 128, 128)
        ch = lax.div(b, 2)
        mean = dot(mean_parts, pick(b), 0, 0)
        d = scb[ch, rows, :] * (dnb[ch, rows, :] - qkvb[ch, rows, :] * mean)
        dqkv[ch, rows, :] = d.astype(BF16)
        return 0
    lax.fori_loop(0, 8, dqkv_step, 0)
    g = dot(dqkv[...].reshape(1024, 256), xl[...].reshape(1024, 1024), 0, 0)
    gq_s[...] = g.astype(BF16).reshape(16, 16, 1024)
    gq_r[s] = gq_s[s]
    gq_g = seq_put(gq_s, gq_r)
    g_attn = jnp.sum(g * wqb[...].reshape(256, 1024).astype(F32), axis=0, keepdims=True) / gain_a
    for p in range(8):
        sm3[p, 8:9, :] = g_attn[:, 128 * p:128 * p + 128]
        sm3[p, 10:16, :] = jnp.zeros((6, 128), F32)
    sm1[c] = sm3[c]
    m1_g = ctx_put(sm3, sm1)

    dx_g = rs_new(2)

    def dx_step(n, _):
        ch = step_chip(n)
        dx = dot(dqkv[ch], wqb[...].reshape(256, 1024), 1, 0)
        part[2, ch] = dx.astype(BF16).reshape(2, 128, 1024)
        rs_first(2, dx_g, ch)

        @pl.when(n > 0)
        def _():
            rs_second(2, dx_g, step_chip(n - 1))
        return 0
    lax.fori_loop(0, 4, dx_step, 0)
    rs_second(2, dx_g, z)
    g2.got(g_s.at[0:3])
    gsum[...] = (g_p[0].astype(F32) + g_r2[0].astype(F32) + g_r2[1].astype(F32)
                 + g_r2[2].astype(F32)).reshape(8, 8, 1536)
    gw_o[c] = gsum[c]
    gw_g = ctx_put(gsum, gw_o)

    m1_g.got(sm1.at[0:7])
    tot = jnp.sum(sm1[...], axis=0)
    r16 = iota((16, 128), 0)
    tot = tot + jnp.where(r16 == 10, acc[1:2, 0:128], 0.0) + jnp.where(r16 == 11, acc[1:2, 128:256], 0.0)
    sm2[s] = tot
    m2_g = seq_put(sm2, sm2, False)
    gq_g.got(gq_r.at[0:15])

    def add_q(i, t):
        return t + gq_r[i].astype(F32)
    gq_t[...] = lax.fori_loop(1, 16, add_q, gq_r[0].astype(F32))
    back_g = cp.group(1, None)

    @pl.when(mine)
    def _():
        gq_o[...] = gq_t[...]

    @pl.when(jnp.logical_not(mine))
    def _():
        back_g.put(gq_t, gq_o, 0, home)
    go_g.got(go_r.at[0:15])

    def add_o(i, t):
        return t + go_r[i].astype(F32)
    gsum_o[...] = lax.fori_loop(1, 16, add_o, go_r[0].astype(F32)).reshape(8, 8, 128)
    go_o[c] = gsum_o[c]
    go2_g = ctx_put(gsum_o, go_o)
    res_o[...] = (midb[...] + rs_finish(1, res_g)).astype(BF16)
    m2_g.got(sm2.at[0:15])
    sm_o[c] = jnp.sum(sm2[...], axis=0)
    m3_g = ctx_put(sm_o, sm_o, False)

    x = hid[...].astype(F32)
    s1 = lax.rsqrt(jnp.mean(x * x, axis=-1, keepdims=True) + EPSILON)
    n1 = x * s1
    up = rs_finish(2, dx_g) * gain_a
    gi_o[...] += s1 * (up - n1 * jnp.mean(up * n1, axis=-1, keepdims=True))

    @pl.when(jnp.logical_not(mine))
    def _():
        back_g.got(gq_o)
        back_g.sent(gq_t)
    for a in range(4):
        @pl.when(not_me(aim(a)))
        def _():
            home_g.sent(wq)
    gw_g.got(gw_o.at[0:7])
    go2_g.got(go_o.at[0:7])
    m3_g.got(sm_o.at[0:7])
    for group, total in cp.drains:
        group.sent(total)


def place(res, gi, gq, go, gw, sm, res_o, gi_o, gq_o, go_o, gin_o, gdn_o, gr_o, ga_o, gqg_o, gkg_o, gm_o):
    res_o[...] = res[...]
    gi_o[...] = gi[...]
    gq_o[...] = gq[...]
    for b in range(8):
        cols = slice(128 * b, 128 * b + 128)
        go_o[:, cols] = go[b]
        gin_o[:, b, :] = gw[b, :, 0:1024]
        gdn_o[:, b, :] = gw[b, :, 1024:1536]
        gr_o[:, cols] = sm[b, 0:8, :]
        ga_o[b:b + 1, :] = sm[b, 8:9, :]
        gm_o[b:b + 1, :] = sm[b, 9:10, :]
        gqg_o[b:b + 1, :] = sm[b, 10:11, :]
    for b in range(4):
        gkg_o[b:b + 1, :] = jnp.where(iota((1, 128), 1) < 64, sm[2 * b, 11:12, :],
                                      pltpu.roll(sm[2 * b + 1, 11:12, :], 64, 1))


def local(hidden_in, positions, starts, routes, qkv_weight, out_weight, expert_in, expert_out,
          router, attn_gain, query_gain, key_gain, mlp_gain, out_grad):
    lanes = np.arange(128, dtype=np.float32) % 32
    freq = (np.float32(ROPE_BASE) ** (-lanes * np.float32(2.0) / np.float32(64))).astype(np.float32)[None]
    wd = jnp.concatenate([expert_in, expert_out], axis=2).transpose(1, 0, 2)
    V = pltpu.VMEM
    scratch = dict(
        xl=V((8, 128, 1024), BF16), dyb=V((8, 128, 1024), BF16), hb=V((8, 128, 1024), BF16),
        dbb=V((8, 128, 1024), BF16), tb=V((8, 64, 128), F32), wqb=V((16, 16, 1024), BF16),
        wo1=V((8, 8, 1024), BF16), wd1=V((8, 8, 1536), BF16), wof=V((16, 64, 1024), BF16), wb=V((16, 64, 1536), BF16),
        qkvb=V((4, 256, 256), F32), scb=V((4, 256, 256), F32), qr=V((8, 128, 128), BF16),
        ka=V((8, 128, 128), BF16), kb=V((8, 128, 128), BF16), va=V((8, 128, 128), BF16), vb=V((8, 128, 128), BF16),
        at=V((8, 128, 128), BF16), pb=V((2, 4, 256, 1024), BF16), drawb=V((4, 256, 512), F32),
        dgub=V((4, 256, 1024), BF16), agb=V((4, 256, 512), BF16),
        part=V((3, 4, 2, 128, 1024), BF16), sibb=V((3, 4, 128, 1024), BF16), rin=V((3, 3, 128, 1024), BF16),
        st=V((16, 128), F32), stb=V((2, 8, 16, 128), F32), st2=V((16, 128), F32), gtb=V((8, 8, 128), F32),
        dgs=V((8, 8, 128), F32), dgr=V((8, 8, 128), F32), midb=V((128, 1024), F32), ao=V((8, 128, 128), BF16), da_s=V((8, 128, 128), BF16), dab=V((8, 128, 128), BF16),
        dkv=V((1024, 128), F32), dqkv=V((4, 256, 256), BF16),
        g_s=V((16, 64, 1536), BF16), g_r1=V((3, 4, 64, 1536), BF16), g_p=V((4, 64, 1536), BF16),
        g_r2=V((3, 64, 1536), BF16), go_s=V((16, 64, 128), BF16), go_r=V((16, 64, 128), BF16),
        gq_s=V((16, 16, 1024), BF16), gq_r=V((16, 16, 1024), BF16), gq_t=V((16, 1024), F32),
        gsum=V((8, 8, 1536), F32), gsum_o=V((8, 8, 128), F32),
        sm3=V((8, 16, 128), F32), sm1=V((8, 16, 128), F32), sm2=V((16, 16, 128), F32), acc=V((8, 1024), F32),
        send=pltpu.SemaphoreType.DMA((SENDS,)), recv=pltpu.SemaphoreType.DMA((RECVS,)))
    vm = pl.BlockSpec(memory_space=pltpu.VMEM)
    outs = pl.pallas_call(
        kernel,
        out_shape=[jax.ShapeDtypeStruct(sh, dt) for sh, dt in (
            ((128, 1024), BF16), ((128, 1024), F32), ((16, 1024), F32), ((8, 8, 128), F32),
            ((8, 8, 1536), F32), ((8, 16, 128), F32))],
        in_specs=[vm] * 11 + [pl.BlockSpec(memory_space=pltpu.SMEM)] + [vm] * 2,
        out_specs=[vm] * 6,
        scratch_shapes=list(scratch.values()),
        compiler_params=pltpu.CompilerParams(collective_id=0, has_side_effects=True,
                                             vmem_limit_bytes=60 * 2**20),
        name="layer",
    )(hidden_in[0], out_grad[0], qkv_weight, out_weight, wd, attn_gain, mlp_gain, query_gain, key_gain, positions, freq, starts, routes[0].T, router.T)
    shapes = (((128, 1024), BF16), ((128, 1024), F32), ((16, 1024), F32), ((8, 1024), F32), ((8, 8, 1024), F32),
              ((8, 8, 512), F32), ((8, 1024), F32), ((8, 128), F32), ((8, 128), F32), ((4, 128), F32), ((8, 128), F32))
    res, gi, gq, go, gin, gdn, gr, ga, gqg, gkg, gm = pl.pallas_call(
        place, out_shape=[jax.ShapeDtypeStruct(sh, dt) for sh, dt in shapes],
        in_specs=[vm] * 6, out_specs=[vm] * 11, name="place",
        compiler_params=pltpu.CompilerParams(vmem_limit_bytes=60 * 2**20),
    )(*outs)
    return (res[None], gi[None], gq, go, gin, gdn, gr.T, ga.reshape(1024), gqg.reshape(1024), gkg.reshape(512),
            gm.reshape(1024))


def solution(mesh):
    t = ("seq", "ctx")
    in_specs = (P("seq", "ctx", None), P("seq", "ctx"), P("seq", None), P("seq", "ctx", None),
                P(t, None), P(t, None), P(t, None, None), P(t, None, None),
                P(), P(), P(), P(), P(), P("seq", "ctx", None))
    out_specs = (P("seq", "ctx", None), P("seq", "ctx", None), P(t, None), P(t, None),
                 P(t, None, None), P(t, None, None), P(), P(), P(), P(), P())
    return jax.shard_map(local, mesh=mesh, in_specs=in_specs, out_specs=out_specs, check_vma=False)
```

```python
import jax
import jax.numpy as jnp
import numpy as np
from jax import lax
from jax.experimental import pallas as pl
from jax.experimental.pallas import tpu as pltpu
from jax.sharding import PartitionSpec as P

PIECE = 256
EPSILON = 1e-06
ROPE_BASE = 10000.0
MASKED = -1e30
F32 = jnp.float32
BF16 = jnp.bfloat16
MESH = pl.DeviceIdType.MESH
SENDS, RECVS = 36, 86


def dot(a, b, ca, cb):
    return lax.dot_general(a, b, (((ca,), (cb,)), ((), ())), preferred_element_type=F32)


def iota(shape, axis):
    return lax.broadcasted_iota(jnp.int32, shape, axis)


class Copies:
    def __init__(self, send, recv, dev):
        self.send, self.recv, self.dev = send, recv, dev
        self.drains, self.sends, self.recvs = [], 0, 0

    def group(self, count, total):
        first, mine = self.recvs, self.sends
        self.recvs += count
        self.sends += 1
        assert self.recvs <= RECVS and self.sends <= SENDS
        return Group(self, first, mine, total)


class Group:
    def __init__(self, owner, first, mine, total):
        self.owner, self.first, self.mine = owner, first, mine
        if total is not None:
            owner.drains.append((self, total))

    def make(self, src, dst, i, dev):
        return pltpu.make_async_remote_copy(
            src_ref=src, dst_ref=dst, send_sem=self.owner.send.at[self.mine],
            recv_sem=self.owner.recv.at[self.first + i], device_id=dev, device_id_type=MESH)

    def put(self, src, dst, i, dev):
        self.make(src, dst, i, dev).start()

    def got(self, dst, i=0):
        self.make(dst, dst, i, self.owner.dev).wait_recv()

    def sent(self, src):
        self.make(src, src, 0, self.owner.dev).wait_send()


def kernel(hid, og, wq, wo, wd, ag_in, mg_in, qg_in, kg_in, pos, freq, starts, rt, rout,
           res_o, gi_o, gq_o, go_o, gw_o, sm_o,
           xl, dyb, hb, dbb, tb, wqb, wo1, wd1, wof, wb,
           qkvb, scb, qr, ka, kb, va, vb, at, pb, drawb, dgub, agb,
           part, sibb, rin, st, stb, st2, gtb, dgs, dgr, midb, ao, da_s, dab, dkv, dqkv,
           g_s, g_r1, g_p, g_r2, go_s, go_r, gq_s, gq_r, gq_t, gsum, gsum_o,
           sm3, sm1, sm2, acc, send, recv):
    s, c = lax.axis_index("seq"), lax.axis_index("ctx")
    z, k = lax.div(c, 2), lax.rem(c, 2)
    y, x_ = lax.div(s, 4), lax.rem(s, 4)
    sib = (s, z * 2 + 1 - k)
    cp = Copies(send, recv, sib)
    dnb, dqb = drawb.at[:, :, 0:256], drawb.at[:, :, 256:384]

    def zdev(dz):
        return (s, lax.rem(z + dz, 4) * 2 + k)

    def cpeer(dc):
        return (s, lax.rem(c + dc, 8))

    def speer(ds):
        return (lax.rem(s + ds, 16), c)

    def near(d):
        return jnp.where(k == 0, y * 4 + lax.rem(x_ + d, 4), lax.rem(y + d, 4) * 4 + x_)

    def far(d):
        return jnp.where(k == 0, lax.rem(y + d, 4) * 4 + x_, y * 4 + lax.rem(x_ + d, 4))

    def cross(a, b):
        return jnp.where(k == 0, lax.rem(y + b, 4) * 4 + lax.rem(x_ + a, 4),
                         lax.rem(y + a, 4) * 4 + lax.rem(x_ + b, 4))

    c4, r4 = lax.div(c, 4), lax.rem(c, 4)
    tg = jnp.where(s < 8, s, jnp.where(s < 12, 2 * (s - 8) + c4, 2 * (s - 12) + c4))
    ts = jnp.where(s < 8, c, jnp.where(s < 12, 8 + r4, 12 + r4))
    mine = (tg == c) & (ts == s)

    def owner(j):
        half = lax.div(c, 2)
        odd = 4 * lax.rem(c, 2)
        os = jnp.where(j < 8, c, jnp.where(j < 12, 8 + half, 12 + half))
        oc = jnp.where(j < 8, j, jnp.where(j < 12, odd + j - 8, odd + j - 12))
        return os, oc

    home = owner(s)
    tk = lax.rem(tg, 2)
    ty, tx = lax.div(ts, 4), lax.rem(ts, 4)

    def aim(a):
        return jnp.where(tk == 0, ty * 4 + lax.rem(tx + a, 4), lax.rem(ty + a, 4) * 4 + tx), tg

    def not_me(dev):
        return jnp.logical_or(dev[0] != s, dev[1] != c)

    bar = pltpu.get_barrier_semaphore()

    for a in range(4):
        source = owner(near(a))

        @pl.when(not_me(source))
        def _(source=source):
            pl.semaphore_signal(bar, inc=1, device_id=source, device_id_type=MESH)
    for dc in range(1, 8):
        pl.semaphore_signal(bar, inc=1, device_id=cpeer(dc), device_id_type=MESH)
    for d in range(1, 4):
        pl.semaphore_signal(bar, inc=1, device_id=(near(d), c), device_id_type=MESH)
        pl.semaphore_signal(bar, inc=1, device_id=(far(d), c), device_id_type=MESH)

    gain_a = ag_in[...].astype(F32).reshape(1, 1024)
    gain_m = mg_in[...].astype(F32).reshape(1, 1024)
    gq_all = qg_in[...].astype(F32).reshape(1, 1024)
    gk_all = kg_in[...].astype(F32).reshape(1, 512)
    gain_q = gq_all[:, 0:128]
    pair = gk_all[:, 0:128]
    for b in range(1, 8):
        gain_q = jnp.where(c == b, gq_all[:, 128 * b:128 * b + 128], gain_q)
    for b in range(1, 4):
        pair = jnp.where(z == b, gk_all[:, 128 * b:128 * b + 128], pair)
    pair = jnp.where(k == 0, pair, pltpu.roll(pair, 64, 1))
    gains = jnp.concatenate([gain_q,
                             jnp.where(iota((1, 128), 1) < 64, pair, 1.0)], axis=1)
    column = jnp.transpose(jnp.broadcast_to(pos[...].astype(F32), (128, 128)))
    lane64 = iota((64, 128), 1)
    angle = jnp.where(lane64 < 64, column[:64], column[64:]) * freq[...]
    tb[c] = jnp.where(lax.rem(lane64, 64) < 32, jnp.cos(angle), jnp.sin(angle))
    x = hid[...].astype(F32)
    s1 = lax.rsqrt(jnp.mean(x * x, axis=-1, keepdims=True) + EPSILON)
    xl[c] = (x * s1 * gain_a).astype(BF16)
    dyb[c] = og[...]
    wo1[c] = wo[...]
    wd1[c] = wd[c]

    selfish = jnp.int32(0)
    for a in range(4):
        selfish = selfish + jnp.where(not_me(aim(a)), 0, 1)

    @pl.when(selfish > 0)
    def _():
        wqb[ts] = wq[...]
    pl.semaphore_wait(bar, 17 - selfish)

    def ag_start(view, total):
        g = cp.group(7, total)
        for dz in (1, 3):
            g.put(view(c), view(c), dz - 1, zdev(dz))
        g.put(view(c), view(c), 3, sib)
        return g

    def gray(n):
        return jnp.where(n == 2, 3, jnp.where(n == 3, 2, n))

    def ag_pass(view, g, n):
        dz = (0, 1, 3, 2)[n]
        block = view(lax.rem(z - dz + 4, 4) * 2 + k)
        g.got(block, dz - 1)
        if n < 3:
            size = block.shape[0] // 2
            half = block.at[pl.ds(size * (n - 1), size)]
            g.put(half, half, 1, zdev(dz))
        g.put(block, block, 3 + dz, sib)

    def ag_have(view, g, n):
        dz = gray(n)
        ch = lax.rem(z - dz + 4, 4)
        g.got(view(ch * 2 + 1 - k), 3 + dz)
        return ch

    def rows_of(buf):
        return lambda b: buf.at[b]

    def xy_start(view, total):
        near_g = cp.group(1, total(3))
        far_g = cp.group(1, total(12))
        for d in (1, 3, 2):
            near_g.put(view(s), view(s), 0, (near(d), c))
        for d in (1, 3, 2):
            far_g.put(view(s), view(s), 0, (far(d), c))
        return near_g, far_g

    def xy_pass(view, total, g):
        g[0].got(total(3))
        for a in (1, 3, 2):
            block = near(a)
            for d in (1, 3, 2):
                g[1].put(view(block), view(block), 0, (far(d), c))

    mine_rows = pl.ds(pl.multiple_of(32 * k, 32), 32)
    other_rows = pl.ds(pl.multiple_of(32 - 32 * k, 32), 32)

    def out_block(b):
        return wof.at[b, mine_rows]

    def out_total(n):
        return wof.at[0:n, 0:32]

    def ctx_put(src, dst, own=True):
        g = cp.group(1, dst.at[0:7])
        for dc in range(1, 8):
            dev = cpeer(dc)
            g.put(src.at[dev[1]] if own else src.at[c], dst.at[c], 0, dev)
        return g

    home_g = cp.group(4, None)
    for a in (0, 1, 3, 2):
        dev = aim(a)

        @pl.when(not_me(dev))
        def _(dev=dev, a=a):
            home_g.put(wq, wqb.at[ts], a, dev)
    wo_g = cp.group(1, wo1.at[0:7])
    for dc in range(1, 8):
        wo_g.put(wo, wo1.at[c], 0, cpeer(dc))
    wd_g = ctx_put(wd, wd1)
    x_g = ag_start(rows_of(xl), xl.at[0:7])
    tb_g = ctx_put(tb, tb, False)

    wq_g = cp.group(1, wqb.at[0:12])
    for a in range(4):
        block = near(a)

        @pl.when(not_me(owner(block)))
        def _(a=a):
            home_g.got(wqb.at[0], (4 - a) % 4)
        for d in (1, 3, 2):
            wq_g.put(wqb.at[block], wqb.at[block], 0, (far(d), c))
    wo_g.got(wo1.at[0:7])
    rows64 = wo1[...].astype(F32).reshape(64, 1024)
    wof[s, mine_rows] = jnp.where(k == 0, rows64[0:32], rows64[32:64]).astype(BF16)
    wo_x = xy_start(out_block, out_total)
    wd_g.got(wd1.at[0:7])
    wb[s] = wd1[...].astype(F32).reshape(64, 1536).astype(BF16)
    xy_pass(out_block, out_total, wo_x)
    w_x = xy_start(rows_of(wb), lambda n: wb.at[0:n])
    ag_pass(rows_of(xl), x_g, 1)
    ag_pass(rows_of(xl), x_g, 2)
    wq_g.got(wqb.at[0:12])

    def wi_full():
        return wb[:, :, 0:1024].reshape(1024, 1024)

    def wd_full():
        return wb[:, :, 1024:1536].reshape(1024, 512)

    lane = iota((1, 256), 1)

    def halves(v):
        high = v.astype(BF16)
        return high, (v - high.astype(F32)).astype(BF16)

    def split(v):
        return jnp.concatenate(halves(v), axis=0)

    def row_sums(ones, v):
        high, low = halves(v)
        return dot(ones, high, 1, 1) + dot(ones, low, 1, 1)

    sel8 = jnp.where(iota((8, 256), 0) == 0, jnp.where(iota((8, 256), 1) < 128, 1.0, 0.0),
                     jnp.where((iota((8, 256), 0) == 1) & (iota((8, 256), 1) >= 128)
                               & (iota((8, 256), 1) < 192), 1.0, 0.0)).astype(BF16)

    def put_rows(ref, ch, rows):
        ref[pl.ds(2 * ch, 1), :] = rows[0:1, 0:128]
        ref[pl.ds(2 * ch + 1, 1), :] = rows[0:1, 128:256]
        ref[pl.ds(8 + 2 * ch, 1), :] = rows[1:2, 0:128]
        ref[pl.ds(9 + 2 * ch, 1), :] = rows[1:2, 128:256]

    def qkv_step(n, _):
        @pl.when(n == 2)
        def _():
            ag_pass(rows_of(xl), x_g, 3)
        ch = ag_have(rows_of(xl), x_g, n)
        qkv = dot(xl[pl.ds(2 * ch, 2)].reshape(256, 1024), wqb[...].reshape(256, 1024), 1, 1)
        qkvb[ch] = qkv
        put_rows(st, ch, row_sums(sel8, qkv * qkv))
        return 0
    lax.fori_loop(0, 4, qkv_step, 0)

    def all_reduce(own, slots):
        slots[c] = own[...]
        g = ctx_put(slots, slots, False)

        def finish():
            g.got(slots.at[0:7])
            return jnp.sum(slots[...], axis=0)
        return finish

    row16 = iota((16, 128), 0)
    count = jnp.where(row16 < 8, 1.0 / 1024, 1.0 / 512)
    finish = all_reduce(st, stb.at[0])
    dy_g = ag_start(rows_of(dyb), dyb.at[0:7])
    xy_pass(rows_of(wb), lambda n: wb.at[0:n], w_x)
    tb_g.got(tb.at[0:7])
    scale_parts = split(lax.rsqrt(finish() * count + EPSILON))

    def pick(b):
        r, l = lax.rem(iota((32, 256), 0), 16), iota((32, 256), 1)
        return jnp.where(((r == b) & (l < 128)) | ((r == 8 + b) & (l >= 128) & (l < 192)), 1.0, 0.0).astype(BF16)

    even = lax.rem(lax.div(iota((128, 128), 1), 32), 2) == 0
    low64 = iota((128, 128), 1) < 64

    def tables(b):
        t = tb[b]
        r = pltpu.roll(t, 64, 1)
        low = iota((64, 128), 1) < 64
        t = jnp.concatenate([jnp.where(low, t, r), jnp.where(low, r, t)], axis=0)
        t2 = pltpu.roll(t, 32, 1)
        return jnp.where(even, t, t2), jnp.where(even, -t2, t)

    def partner(w):
        return jnp.where(even, pltpu.roll(w, 96, 1), pltpu.roll(w, 32, 1))

    def rope_step(b, _):
        rows = pl.ds(lax.rem(b, 2) * 128, 128)
        ch = lax.div(b, 2)
        scale = dot(scale_parts, pick(b), 0, 0) + jnp.where(lane >= 192, 1.0, 0.0)
        scb[ch, rows, :] = scale
        normed = qkvb[ch, rows, :] * scale
        qkvb[ch, rows, :] = normed
        w = normed * gains
        cs, sn = tables(b)
        wq_, wk_ = w[:, :128], w[:, 128:]
        qr[b] = ((wq_ * cs + partner(wq_) * sn) * 0.125).astype(BF16)
        kv = wk_ * jnp.where(low64, cs, 1.0) + partner(wk_) * jnp.where(low64, sn, 0.0)
        k0 = jnp.where(low64, kv, 0.0)
        v1 = jnp.where(low64, 0.0, kv)
        ka[b] = k0.astype(BF16)
        kb[b] = pltpu.roll(k0, 64, 1).astype(BF16)
        va[b] = pltpu.roll(v1, 64, 1).astype(BF16)
        vb[b] = v1.astype(BF16)
        return 0
    lax.fori_loop(0, 8, rope_step, 0)
    wo_x[1].got(out_total(12))
    wo_s = cp.group(1, wof.at[:, 0:32])
    wo_s.put(wof.at[:, mine_rows], wof.at[:, mine_rows], 0, sib)

    def rs_new(r):
        return cp.group(4, sibb.at[r]), cp.group(1, rin.at[r])

    def rs_first(r, g, ch):
        g[0].put(part.at[r, ch, 1 - k], sibb.at[r, ch], ch, sib)

    def rs_second(r, g, ch):
        g[0].got(sibb.at[r, ch], ch)
        part[r, ch, k] = (part[r, ch, k].astype(F32) + sibb[r, ch].astype(F32)).astype(BF16)
        dz = lax.rem(ch - z + 4, 4)

        @pl.when(dz > 0)
        def _():
            g[1].put(part.at[r, ch, k], rin.at[r, dz - 1], 0, (s, ch * 2 + k))

    def rs_finish(r, g):
        g[1].got(rin.at[r])
        total = part[r, z, k].astype(F32)
        for i in range(3):
            total = total + rin[r, i].astype(F32)
        return total

    st0, st1 = starts[0, 0], starts[0, 1]

    def limits(ch):
        row = ch * 256 + iota((256, 1), 0)
        lim = jnp.where((row >= st0) & (row < st0 + PIECE), st0 + PIECE - 1, row)
        return jnp.where((row >= st1) & (row < st1 + PIECE), st1 + PIECE - 1, lim)

    def keys(ref, length):
        return ref[0:length // 128].reshape(length, 128)

    def attend(ch, length):
        q = qr[pl.ds(2 * ch, 2)].reshape(256, 128)
        allowed = iota((256, length), 1) <= limits(ch)
        out = None
        for h, (kk, vv) in enumerate(((ka, va), (kb, vb))):
            sc = jnp.where(allowed, dot(q, keys(kk, length), 1, 1), MASKED)
            e = jnp.exp(sc - jnp.max(sc, axis=-1, keepdims=True))
            p = (e * (1.0 / jnp.sum(e, axis=-1, keepdims=True))).astype(BF16)
            pb[h, ch, :, 0:length] = p
            o = dot(p, keys(vv, length), 1, 0)
            out = o if out is None else out + o
        at[pl.ds(2 * ch, 2)] = out.astype(BF16).reshape(2, 128, 128)

    def step_chip(n):
        return lax.rem(z + jnp.where(n == 0, 2, jnp.where(n == 1, 1, jnp.where(n == 2, 3, 0))), 4)

    def heads_put(src, dst, g, b):
        @pl.when(b != c)
        def _():
            g.put(src.at[b], dst.at[c], 0, (s, b))

        @pl.when(b == c)
        def _():
            dst[c] = src[c]

    ao_g = cp.group(1, ao.at[0:7])

    def fwd_step(n, _):
        ch = step_chip(n)

        @pl.when(ch < 2)
        def _():
            attend(ch, 512)

        @pl.when(ch >= 2)
        def _():
            attend(ch, 1024)
        heads_put(at, ao, ao_g, 2 * ch + k)

        @pl.when(n == 2)
        def _():
            ag_pass(rows_of(dyb), dy_g, 1)
            ag_pass(rows_of(dyb), dy_g, 2)
        heads_put(at, ao, ao_g, 2 * ch + 1 - k)
        return 0
    lax.fori_loop(0, 4, fwd_step, 0)

    ag_pass(rows_of(dyb), dy_g, 3)

    wo_s.got(wof.at[:, other_rows])
    ao_g.got(ao.at[0:7])
    wide = jnp.concatenate([ao[b] for b in range(8)], axis=1)
    mid = hid[...].astype(F32) + dot(wide, wof[...].reshape(1024, 1024), 1, 1)
    midb[...] = mid
    s2 = lax.rsqrt(jnp.mean(mid * mid, axis=-1, keepdims=True) + EPSILON)
    h_own = (mid * s2 * gain_m).astype(BF16)
    hb[c] = h_own
    logits = dot(rout[...], h_own, 1, 1)
    e8 = jnp.exp(logits - jnp.max(logits, axis=0, keepdims=True))
    gates = e8 / jnp.sum(e8, axis=0, keepdims=True)
    er = iota((8, 128), 0)
    member = jnp.zeros((8, 128), F32)
    for j in range(4):
        member = member + jnp.where(rt[j:j + 1, :] == er, 1.0, 0.0)
    gtb[c] = gates * member
    gt_g = cp.group(7, gtb.at[0:7])
    for dc in (1, 7, 2, 6, 3, 5, 4):
        gt_g.put(gtb.at[c], gtb.at[c], dc - 1, cpeer(dc))
    h_g = ag_start(rows_of(hb), hb.at[0:7])
    w_x[1].got(wb.at[0:12])

    def draw_step(n, _):
        ch = ag_have(rows_of(dyb), dy_g, n)
        drawb[ch] = dot(dyb[pl.ds(2 * ch, 2)].reshape(256, 1024), wd_full(), 1, 0)
        return 0
    lax.fori_loop(0, 4, draw_step, 0)

    one_c = jnp.where(lax.rem(iota((16, 128), 0), 8) == c, 1.0, 0.0).astype(BF16)
    dh_g, res_g = rs_new(0), rs_new(1)

    def expert_step(n, _):
        ch = ag_have(rows_of(hb), h_g, n)
        gu = dot(hb[pl.ds(2 * ch, 2)].reshape(256, 1024), wi_full(), 1, 0)
        g, u = gu[:, :512], gu[:, 512:]
        sig = 1.0 / (1.0 + jnp.exp(-g))
        sw = g * sig
        act = sw * u

        for b in (2 * ch, 2 * ch + 1):
            @pl.when(b != c)
            def _(b=b):
                gt_g.got(gtb.at[0], lax.rem(c - b + 8, 8) - 1)
        gate = jnp.concatenate([dot(split(gtb[2 * ch]), one_c, 0, 0), dot(split(gtb[2 * ch + 1]), one_c, 0, 0)], axis=0)
        gate = jnp.concatenate([gate] * 4, axis=1)
        draw = drawb[ch]
        agb[ch] = (act * gate).astype(BF16)
        rows = row_sums(jnp.ones((8, 512), BF16), act * draw)
        dgs[2 * ch] = rows[:, 0:128]
        dgs[2 * ch + 1] = rows[:, 128:256]
        d_act = draw * gate
        dgub[ch, :, 0:512] = (d_act * u * sig * (1.0 + g * (1.0 - sig))).astype(BF16)
        dgub[ch, :, 512:1024] = (d_act * sw).astype(BF16)
        dh = dot(dgub[ch], wi_full(), 1, 1)
        part[0, ch] = dh.astype(BF16).reshape(2, 128, 1024)
        rs_first(0, dh_g, ch)
        rs = dot(agb[ch], wd_full(), 1, 1)
        part[1, ch] = rs.astype(BF16).reshape(2, 128, 1024)
        rs_first(1, res_g, ch)

        @pl.when(n == 0)
        def _():
            ag_pass(rows_of(hb), h_g, 1)
            ag_pass(rows_of(hb), h_g, 2)

        @pl.when(n == 2)
        def _():
            ag_pass(rows_of(hb), h_g, 3)
        rs_second(0, dh_g, ch)
        return 0
    lax.fori_loop(0, 4, expert_step, 0)
    dgr[c] = dgs[c]
    dg_g = ctx_put(dgs, dgr)

    def gw_step(i, _):
        cols = pl.ds(pl.multiple_of(i * 256, 256), 256)
        g = dot(dyb[:, :, cols].reshape(1024, 256), agb[...].reshape(1024, 512), 0, 0)
        g_s[pl.ds(4 * i, 4), :, 1024:1536] = g.astype(BF16).reshape(4, 64, 512)
        g = dot(hb[:, :, cols].reshape(1024, 256), dgub[...].reshape(1024, 1024), 0, 0)
        g_s[pl.ds(4 * i, 4), :, 0:1024] = g.astype(BF16).reshape(4, 64, 1024)
        return 0
    lax.fori_loop(0, 4, gw_step, 0)
    g1, g2 = cp.group(1, g_s.at[0:12]), cp.group(1, g_s.at[0:3])
    for d in (1, 3, 2):
        for e in range(4):
            g1.put(g_s.at[cross(d, e)], g_r1.at[d - 1, e], 0, (near(d), c))

    for i in range(4):
        rs_second(1, res_g, lax.rem(z + 1 + i, 4))

    dg_g.got(dgr.at[0:7])
    dg = jnp.concatenate([dgr[e, 0:1, :] for e in range(8)], axis=0) * member
    d_logits = (gates * (dg - jnp.sum(gates * dg, axis=0, keepdims=True))).astype(BF16)
    d_h = rs_finish(0, dh_g) + dot(d_logits, rout[...], 0, 0)
    mid = midb[...]
    s2 = lax.rsqrt(jnp.mean(mid * mid, axis=-1, keepdims=True) + EPSILON)
    n2 = mid * s2
    up = d_h * gain_m
    d_mid = og[...].astype(F32) + s2 * (up - n2 * jnp.mean(up * n2, axis=-1, keepdims=True))
    gi_o[...] = d_mid
    d_branch = d_mid.astype(BF16)
    d_attn = dot(d_branch, wof[...].reshape(1024, 1024), 1, 0).astype(BF16)
    for b in range(8):
        da_s[b] = d_attn[:, 128 * b:128 * b + 128]
    da_g = cp.group(1, dab.at[0:7])
    dab[c] = da_s[c]
    for dc in (4, 3, 5, 2, 6, 1, 7):
        dev = cpeer(dc)
        da_g.put(da_s.at[dev[1]], dab.at[c], 0, dev)
    dbb[c] = d_branch
    db_g = ag_start(rows_of(dbb), dbb.at[0:7])
    g_router = dot(d_logits, hb[c], 1, 0)
    g_mlp = jnp.sum(d_h * n2, axis=0, keepdims=True)
    for p in range(8):
        edge = slice(128 * p, 128 * p + 128)
        sm3[p, 0:8, :] = g_router[:, edge]
        sm3[p, 9:10, :] = g_mlp[:, edge]

    dkv[...] = jnp.zeros_like(dkv)
    low256 = iota((256, 128), 1) < 64

    def attend_back(ch, length):
        da = dab[pl.ds(2 * ch, 2)].reshape(256, 128)
        q = qr[pl.ds(2 * ch, 2)].reshape(256, 128).astype(F32)
        daf = da.astype(F32)
        dq = None
        left, right = [], []
        for h, (kk, vv) in enumerate(((ka, va), (kb, vb))):
            p = pb[h, ch, :, 0:length]
            pf = p.astype(F32)
            dp = dot(da, keys(vv, length), 1, 1)
            ds = (pf * (dp - jnp.sum(pf * dp, axis=-1, keepdims=True))).astype(BF16)
            o = dot(ds, keys(kk, length), 1, 0)
            dq = o if dq is None else dq + o
            qh = jnp.where(low256, q if h == 0 else pltpu.roll(q, 64, 1), 0.0)
            dh_ = jnp.where(low256, 0.0, daf if h == 1 else pltpu.roll(daf, 64, 1))
            left += [ds, p]
            right += [qh.astype(BF16), dh_.astype(BF16)]
        dqb[ch] = dq * 0.125
        for l, r in zip(left, right):
            dkv[0:length, :] += dot(l, r, 0, 0)

    def bwd_step(n, _):
        ch = n

        @pl.when(n == 2)
        def _():
            ag_pass(rows_of(dbb), db_g, 1)
            ag_pass(rows_of(dbb), db_g, 2)

        @pl.when(ch < 2)
        def _():
            attend_back(ch, 512)

        @pl.when(ch >= 2)
        def _():
            attend_back(ch, 1024)
        return 0
    da_g.got(dab.at[0:7])
    lax.fori_loop(0, 4, bwd_step, 0)

    acc[...] = jnp.zeros_like(acc)

    def unrope_step(ch, _):
        for kk in range(2):
            b = 2 * ch + kk
            rows = slice(128 * kk, 128 * kk + 128)
            cs, sn = tables(b)
            wq_ = dqb[ch, rows, :]
            wk_ = dkv[pl.ds(pl.multiple_of(b * 128, 128), 128), :]
            dq = wq_ * cs - partner(wq_) * sn
            dk = wk_ * jnp.where(low64, cs, 1.0) - partner(wk_) * jnp.where(low64, sn, 0.0)
            dn = jnp.concatenate([dq, dk], axis=1)
            normed = qkvb[ch, rows, :]
            acc[1:2, 0:256] += jnp.sum(dn * normed, axis=0, keepdims=True)
            dnb[ch, rows, :] = dn * gains
        put_rows(st2, ch, row_sums(sel8, dnb[ch] * qkvb[ch]))
        return 0
    lax.fori_loop(0, 4, unrope_step, 0)
    finish2 = all_reduce(st2, stb.at[1])

    g1.got(g_s.at[0:12])

    def fold(e, _):
        own = g_s[cross(0, e)].astype(F32)
        for i in range(3):
            own = own + g_r1[i, e].astype(F32)
        g_p[e] = own.astype(BF16)
        return 0
    lax.fori_loop(0, 4, fold, 0)
    for d in (1, 3, 2):
        g2.put(g_p.at[d], g_r2.at[d - 1], 0, (far(d), c))

    ag_pass(rows_of(dbb), db_g, 3)
    for n in range(4):
        ag_have(rows_of(dbb), db_g, n)
    def go_step(i, _):
        cols = pl.ds(pl.multiple_of(i * 256, 256), 256)
        g = dot(dbb[:, :, cols].reshape(1024, 256), at[...].reshape(1024, 128), 0, 0)
        go_s[pl.ds(4 * i, 4)] = g.astype(BF16).reshape(4, 64, 128)
        return 0
    lax.fori_loop(0, 4, go_step, 0)

    def seq_put(src, dst, spread=True):
        g = cp.group(1, dst.at[0:15])

        def body(ds, _):
            dev = speer(ds)
            g.put(src.at[dev[0]] if spread else src.at[s], dst.at[s], 0, dev)
            return 0
        lax.fori_loop(1, 16, body, 0)
        return g
    go_r[s] = go_s[s]
    go_g = seq_put(go_s, go_r)
    mean_parts = split(finish2() * count)

    def dqkv_step(b, _):
        rows = pl.ds(lax.rem(b, 2) * 128, 128)
        ch = lax.div(b, 2)
        mean = dot(mean_parts, pick(b), 0, 0)
        d = scb[ch, rows, :] * (dnb[ch, rows, :] - qkvb[ch, rows, :] * mean)
        dqkv[ch, rows, :] = d.astype(BF16)
        return 0
    lax.fori_loop(0, 8, dqkv_step, 0)
    g = dot(dqkv[...].reshape(1024, 256), xl[...].reshape(1024, 1024), 0, 0)
    gq_s[...] = g.astype(BF16).reshape(16, 16, 1024)
    gq_r[s] = gq_s[s]
    gq_g = seq_put(gq_s, gq_r)
    g_attn = jnp.sum(g * wqb[...].reshape(256, 1024).astype(F32), axis=0, keepdims=True) / gain_a
    for p in range(8):
        sm3[p, 8:9, :] = g_attn[:, 128 * p:128 * p + 128]
        sm3[p, 10:16, :] = jnp.zeros((6, 128), F32)
    sm1[c] = sm3[c]
    m1_g = ctx_put(sm3, sm1)

    dx_g = rs_new(2)

    def dx_step(n, _):
        ch = step_chip(n)
        dx = dot(dqkv[ch], wqb[...].reshape(256, 1024), 1, 0)
        part[2, ch] = dx.astype(BF16).reshape(2, 128, 1024)
        rs_first(2, dx_g, ch)

        @pl.when(n > 0)
        def _():
            rs_second(2, dx_g, step_chip(n - 1))
        return 0
    lax.fori_loop(0, 4, dx_step, 0)
    rs_second(2, dx_g, z)
    gq_g.got(gq_r.at[0:15])

    def add_q(i, t):
        return t + gq_r[i].astype(F32)
    gq_t[...] = lax.fori_loop(1, 16, add_q, gq_r[0].astype(F32))
    back_g = cp.group(1, None)

    @pl.when(mine)
    def _():
        gq_o[...] = gq_t[...]

    @pl.when(jnp.logical_not(mine))
    def _():
        back_g.put(gq_t, gq_o, 0, home)
    g2.got(g_s.at[0:3])
    gsum[...] = (g_p[0].astype(F32) + g_r2[0].astype(F32) + g_r2[1].astype(F32)
                 + g_r2[2].astype(F32)).reshape(8, 8, 1536)
    gw_o[c] = gsum[c]
    gw_g = ctx_put(gsum, gw_o)

    m1_g.got(sm1.at[0:7])
    tot = jnp.sum(sm1[...], axis=0)
    r16 = iota((16, 128), 0)
    tot = tot + jnp.where(r16 == 10, acc[1:2, 0:128], 0.0) + jnp.where(r16 == 11, acc[1:2, 128:256], 0.0)
    sm2[s] = tot
    m2_g = seq_put(sm2, sm2, False)
    go_g.got(go_r.at[0:15])

    def add_o(i, t):
        return t + go_r[i].astype(F32)
    gsum_o[...] = lax.fori_loop(1, 16, add_o, go_r[0].astype(F32)).reshape(8, 8, 128)
    go_o[c] = gsum_o[c]
    go2_g = ctx_put(gsum_o, go_o)
    res_o[...] = (midb[...] + rs_finish(1, res_g)).astype(BF16)
    m2_g.got(sm2.at[0:15])
    sm_o[c] = jnp.sum(sm2[...], axis=0)
    m3_g = ctx_put(sm_o, sm_o, False)

    x = hid[...].astype(F32)
    s1 = lax.rsqrt(jnp.mean(x * x, axis=-1, keepdims=True) + EPSILON)
    n1 = x * s1
    up = rs_finish(2, dx_g) * gain_a
    gi_o[...] += s1 * (up - n1 * jnp.mean(up * n1, axis=-1, keepdims=True))

    @pl.when(jnp.logical_not(mine))
    def _():
        back_g.got(gq_o)
        back_g.sent(gq_t)
    for a in range(4):
        @pl.when(not_me(aim(a)))
        def _():
            home_g.sent(wq)
    gw_g.got(gw_o.at[0:7])
    go2_g.got(go_o.at[0:7])
    m3_g.got(sm_o.at[0:7])
    for group, total in cp.drains:
        group.sent(total)


def place(res, gi, gq, go, gw, sm, res_o, gi_o, gq_o, go_o, gin_o, gdn_o, gr_o, ga_o, gqg_o, gkg_o, gm_o):
    res_o[...] = res[...]
    gi_o[...] = gi[...]
    gq_o[...] = gq[...]
    for b in range(8):
        cols = slice(128 * b, 128 * b + 128)
        go_o[:, cols] = go[b]
        gin_o[:, b, :] = gw[b, :, 0:1024]
        gdn_o[:, b, :] = gw[b, :, 1024:1536]
        gr_o[:, cols] = sm[b, 0:8, :]
        ga_o[b:b + 1, :] = sm[b, 8:9, :]
        gm_o[b:b + 1, :] = sm[b, 9:10, :]
        gqg_o[b:b + 1, :] = sm[b, 10:11, :]
    for b in range(4):
        gkg_o[b:b + 1, :] = jnp.where(iota((1, 128), 1) < 64, sm[2 * b, 11:12, :],
                                      pltpu.roll(sm[2 * b + 1, 11:12, :], 64, 1))


def local(hidden_in, positions, starts, routes, qkv_weight, out_weight, expert_in, expert_out,
          router, attn_gain, query_gain, key_gain, mlp_gain, out_grad):
    lanes = np.arange(128, dtype=np.float32) % 32
    freq = (np.float32(ROPE_BASE) ** (-lanes * np.float32(2.0) / np.float32(64))).astype(np.float32)[None]
    wd = jnp.concatenate([expert_in, expert_out], axis=2).transpose(1, 0, 2)
    V = pltpu.VMEM
    scratch = dict(
        xl=V((8, 128, 1024), BF16), dyb=V((8, 128, 1024), BF16), hb=V((8, 128, 1024), BF16),
        dbb=V((8, 128, 1024), BF16), tb=V((8, 64, 128), F32), wqb=V((16, 16, 1024), BF16),
        wo1=V((8, 8, 1024), BF16), wd1=V((8, 8, 1536), BF16), wof=V((16, 64, 1024), BF16), wb=V((16, 64, 1536), BF16),
        qkvb=V((4, 256, 256), F32), scb=V((4, 256, 256), F32), qr=V((8, 128, 128), BF16),
        ka=V((8, 128, 128), BF16), kb=V((8, 128, 128), BF16), va=V((8, 128, 128), BF16), vb=V((8, 128, 128), BF16),
        at=V((8, 128, 128), BF16), pb=V((2, 4, 256, 1024), BF16), drawb=V((4, 256, 512), F32),
        dgub=V((4, 256, 1024), BF16), agb=V((4, 256, 512), BF16),
        part=V((3, 4, 2, 128, 1024), BF16), sibb=V((3, 4, 128, 1024), BF16), rin=V((3, 3, 128, 1024), BF16),
        st=V((16, 128), F32), stb=V((2, 8, 16, 128), F32), st2=V((16, 128), F32), gtb=V((8, 8, 128), F32),
        dgs=V((8, 8, 128), F32), dgr=V((8, 8, 128), F32), midb=V((128, 1024), F32), ao=V((8, 128, 128), BF16), da_s=V((8, 128, 128), BF16), dab=V((8, 128, 128), BF16),
        dkv=V((1024, 128), F32), dqkv=V((4, 256, 256), BF16),
        g_s=V((16, 64, 1536), BF16), g_r1=V((3, 4, 64, 1536), BF16), g_p=V((4, 64, 1536), BF16),
        g_r2=V((3, 64, 1536), BF16), go_s=V((16, 64, 128), BF16), go_r=V((16, 64, 128), BF16),
        gq_s=V((16, 16, 1024), BF16), gq_r=V((16, 16, 1024), BF16), gq_t=V((16, 1024), F32),
        gsum=V((8, 8, 1536), F32), gsum_o=V((8, 8, 128), F32),
        sm3=V((8, 16, 128), F32), sm1=V((8, 16, 128), F32), sm2=V((16, 16, 128), F32), acc=V((8, 1024), F32),
        send=pltpu.SemaphoreType.DMA((SENDS,)), recv=pltpu.SemaphoreType.DMA((RECVS,)))
    vm = pl.BlockSpec(memory_space=pltpu.VMEM)
    outs = pl.pallas_call(
        kernel,
        out_shape=[jax.ShapeDtypeStruct(sh, dt) for sh, dt in (
            ((128, 1024), BF16), ((128, 1024), F32), ((16, 1024), F32), ((8, 8, 128), F32),
            ((8, 8, 1536), F32), ((8, 16, 128), F32))],
        in_specs=[vm] * 11 + [pl.BlockSpec(memory_space=pltpu.SMEM)] + [vm] * 2,
        out_specs=[vm] * 6,
        scratch_shapes=list(scratch.values()),
        compiler_params=pltpu.CompilerParams(collective_id=0, has_side_effects=True,
                                             vmem_limit_bytes=60 * 2**20),
        name="layer",
    )(hidden_in[0], out_grad[0], qkv_weight, out_weight, wd, attn_gain, mlp_gain, query_gain, key_gain, positions, freq, starts, routes[0].T, router.T)
    shapes = (((128, 1024), BF16), ((128, 1024), F32), ((16, 1024), F32), ((8, 1024), F32), ((8, 8, 1024), F32),
              ((8, 8, 512), F32), ((8, 1024), F32), ((8, 128), F32), ((8, 128), F32), ((4, 128), F32), ((8, 128), F32))
    res, gi, gq, go, gin, gdn, gr, ga, gqg, gkg, gm = pl.pallas_call(
        place, out_shape=[jax.ShapeDtypeStruct(sh, dt) for sh, dt in shapes],
        in_specs=[vm] * 6, out_specs=[vm] * 11, name="place",
        compiler_params=pltpu.CompilerParams(vmem_limit_bytes=60 * 2**20),
    )(*outs)
    return (res[None], gi[None], gq, go, gin, gdn, gr.T, ga.reshape(1024), gqg.reshape(1024), gkg.reshape(512),
            gm.reshape(1024))


def solution(mesh):
    t = ("seq", "ctx")
    in_specs = (P("seq", "ctx", None), P("seq", "ctx"), P("seq", None), P("seq", "ctx", None),
                P(t, None), P(t, None), P(t, None, None), P(t, None, None),
                P(), P(), P(), P(), P(), P("seq", "ctx", None))
    out_specs = (P("seq", "ctx", None), P("seq", "ctx", None), P(t, None), P(t, None),
                 P(t, None, None), P(t, None, None), P(), P(), P(), P(), P())
    return jax.shard_map(local, mesh=mesh, in_specs=in_specs, out_specs=out_specs, check_vma=False)
```
